32 devices in a mesh: dp: 8 (over y, x, core), tensor: 4 (over z).
Axes of the slice: x: 2, y: 2, z: 4, core: 2. Of those that a mesh axis runs over, the one named last changes fastest.
Arguments:
- latents: bfloat16 [16384, 1280], P('dp'), may hold values from -6 to 6
- norm1_gain: float32 [1280], replicated, may hold values from 0.5 to 1.5
- norm1_shift: float32 [1280], replicated, may hold values from -1.75 to 1.75
- query_weight: bfloat16 [1280, 1280], P(None, 'tensor'), may hold values from -0.15625 to 0.15625
- query_bias: float32 [1280], P('tensor'), may hold values from -1.75 to 1.75
- key_weight: bfloat16 [1280, 1280], P(None, 'tensor'), may hold values from -0.15625 to 0.15625
- value_weight: bfloat16 [1280, 1280], P(None, 'tensor'), may hold values from -0.15625 to 0.15625
- value_bias: float32 [1280], P('tensor'), may hold values from -1.75 to 1.75
- out_weight: bfloat16 [1280, 1280], P('tensor'), may hold values from -0.625 to 0.625
- out_bias: float32 [1280], replicated, may hold values from -1.75 to 1.75
- norm2_gain: float32 [1280], replicated, may hold values from 0.5 to 1.5
- norm2_shift: float32 [1280], replicated, may hold values from -1.75 to 1.75
- hidden_weight: bfloat16 [1280, 1280], P(None, 'tensor'), may hold values from -0.15625 to 0.15625
- hidden_bias: float32 [1280], P('tensor'), may hold values from -1.75 to 1.75
- proj_weight: bfloat16 [1280, 1280], P('tensor'), may hold values from -0.25 to 0.25
- proj_bias: float32 [1280], replicated, may hold values from -1.75 to 1.75
- segments: int32 [16, 1024], P('dp'), may hold values from 0 to 7, never falling along the last dimension, each value on 1 to 512 neighbouring positions
- valid_mask: int32 [16, 1024], P('dp'), may hold values 0 or 1
- cotangent: bfloat16 [16384, 1280], P('dp'), may hold values from -6 to 6
Outputs:
- output: bfloat16 [16384, 1280], P('dp')
- grad_input: float32 [16384, 1280], P('dp')
- grad_norm1_gain: float32 [1280], replicated
- grad_norm1_shift: float32 [1280], replicated
- grad_query_weight: float32 [1280, 1280], P(None, 'tensor')
- grad_query_bias: float32 [1280], P('tensor')
- grad_key_weight: float32 [1280, 1280], P(None, 'tensor')
- grad_value_weight: float32 [1280, 1280], P(None, 'tensor')
- grad_value_bias: float32 [1280], P('tensor')
- grad_out_weight: float32 [1280, 1280], P('tensor')
- grad_out_bias: float32 [1280], replicated
- grad_norm2_gain: float32 [1280], replicated
- grad_norm2_shift: float32 [1280], replicated
- grad_hidden_weight: float32 [1280, 1280], P(None, 'tensor')
- grad_hidden_bias: float32 [1280], P('tensor')
- grad_proj_weight: float32 [1280, 1280], P('tensor')
- grad_proj_bias: float32 [1280], replicated
- rms: float32 [16, 3], P('dp')
The draws below stay inside these ranges and needn't reach their ends.
Inputs may be any that keep to these rules, and one draw needn't show every extreme that they name: `segments`: in each row segment numbers never fall, each document has 1 to 512 positions, and one has exactly that many.
All inputs are finite; a program needn't handle non-finite values. No bound on the sum of `valid_mask` on one device may be relied on, other than what follows from the above.
Results may differ from the reference program's by a relative error of at most 0.013.
Values sent between devices are 32-bit elements; how exact they have to be, the bound alone decides.
A program may use at most 192 MiB of HBM per device.

```python
import math
import jax
import jax.numpy as jnp
import numpy as np
from jax import lax

D = 1280
HEADS = 8
HEAD_DIM = 160
FF = 1280
SEQ_LEN = 1024
SEQS = 16
TOKENS = 16384


def touch_ends(drawn, rng, low, high):
    shape = drawn.shape
    place = [jax.random.randint(jax.random.fold_in(rng, axis), (), 0, shape[axis]) for axis in range(len(shape))]
    drawn = drawn.at[tuple(place)].set(low)
    longest = shape.index(max(shape))
    place[longest] = (place[longest] + 1) % shape[longest]
    return drawn.at[tuple(place)].set(high)


def level_of(key, extent, cuts, smallest, largest):
    def one(axis_at, parts):
        heights = jax.random.uniform(jax.random.fold_in(jax.random.fold_in(key, 6), axis_at), (parts,), jnp.float32, smallest / len(cuts), largest / len(cuts))
        return jnp.repeat(jnp.exp(heights), extent[axis_at] // parts).reshape((-1,) + (1,) * (len(extent) - axis_at - 1))

    factor_of = one(*cuts[0])
    for cut in cuts[1:]:
        factor_of = factor_of * one(*cut)
    return factor_of


def profile(count, total, bound, lean):
    loads = [(1 << 20) // math.isqrt(standing ** lean) + 1 for standing in range(2, count + 1)]
    rest, given = total - bound - (count - 1), [1] * (count - 1)
    while rest > 0:
        candidates = [i for i in range(count - 1) if given[i] < bound]
        whole, budget = sum([loads[i] for i in candidates]), rest
        for i in candidates:
            extra = min(bound - given[i], max(1, budget * loads[i] // whole), rest)
            given[i] = given[i] + extra
            rest = rest - extra
    return np.array([bound] + given)


def ragged(stream_key, amount, total, limit, lean):
    if amount == 2:
        one = jax.random.randint(stream_key, (), max(1, total - limit), min(limit, total - 1) + 1)
        return jnp.stack([one, total - one])
    tallies = jnp.asarray(profile(amount, total, limit, lean), jnp.int32)
    pairs = (amount - 1) // 2
    giver, receiver = tallies[1:1 + 2 * pairs:2], tallies[2:2 + 2 * pairs:2]
    margin = jnp.minimum(giver - 1, limit - receiver)
    passed = jax.random.randint(jax.random.fold_in(stream_key, 1), (pairs,), 0, 1 << 20) % (margin + 1)
    tallies = tallies.at[1:1 + 2 * pairs:2].set(giver - passed).at[2:2 + 2 * pairs:2].set(receiver + passed)
    return tallies[jax.random.permutation(jax.random.fold_in(stream_key, 2), amount)]


def centred(key, shape, scale, bound, pieces=(), kind=jnp.bfloat16):
    array = scale * jax.random.normal(key, shape, jnp.float32)
    if pieces:
        array = array * level_of(key, shape, pieces, -0.22, 0.18)
    return jnp.clip(array, -bound, bound).astype(kind)


def setup_inputs(seed: int = 0) -> dict:
    key_list = jax.random.split(jax.random.key(seed), 20)
    return {
        "latents": centred(key_list[0], (TOKENS, D), 1.0, 6.0, ((0, 8),)),
        "norm1_gain": jnp.clip(1.0 + 0.1 * jax.random.normal(key_list[1], (D,), jnp.float32), 0.5, 1.5),
        "norm1_shift": centred(key_list[2], (D,), 0.3, 1.75, (), jnp.float32),
        "query_weight": centred(key_list[3], (D, D), D ** -0.5, 0.15625, ((1, 4),)),
        "query_bias": centred(key_list[4], (D,), 0.3, 1.75, ((0, 4),), jnp.float32),
        "key_weight": centred(key_list[5], (D, D), D ** -0.5, 0.15625, ((1, 4),)),
        "value_weight": centred(key_list[6], (D, D), D ** -0.5, 0.15625, ((1, 4),)),
        "value_bias": centred(key_list[7], (D,), 0.3, 1.75, ((0, 4),), jnp.float32),
        "out_weight": centred(key_list[8], (D, D), (D // 16) ** -0.5, 0.625, ((0, 4),)),
        "out_bias": centred(key_list[9], (D,), 0.3, 1.75, (), jnp.float32),
        "norm2_gain": jnp.clip(1.0 + 0.1 * jax.random.normal(key_list[10], (D,), jnp.float32), 0.5, 1.5),
        "norm2_shift": centred(key_list[11], (D,), 0.3, 1.75, (), jnp.float32),
        "hidden_weight": centred(key_list[12], (D, FF), D ** -0.5, 0.15625, ((1, 4),)),
        "hidden_bias": centred(key_list[13], (FF,), 0.3, 1.75, ((0, 4),), jnp.float32),
        "proj_weight": centred(key_list[14], (FF, D), (FF // 2) ** -0.5, 0.25, ((0, 4),)),
        "proj_bias": centred(key_list[15], (D,), 0.3, 1.75, (), jnp.float32),
        "segments": jax.vmap(lambda own: jnp.searchsorted(jnp.cumsum(ragged(own, 8, SEQ_LEN, SEQ_LEN // 2, 2)), jnp.arange(SEQ_LEN), side="right"))(jax.random.split(key_list[16], SEQS)).reshape((SEQS, SEQ_LEN)).astype(jnp.int32),
        "valid_mask": touch_ends((jax.random.randint(key_list[17], (SEQS, SEQ_LEN), 0, 8) < 7).astype(jnp.int32), jax.random.fold_in(key_list[17], 1), 0, 1),
        "cotangent": centred(key_list[18], (TOKENS, D), 1.0, 6.0, ((0, 8),)),
    }


@jax.custom_vjp
def low(v):
    return lax.optimization_barrier(v.astype(jnp.bfloat16)).astype(jnp.float32)

@jax.custom_vjp
def low_back(v):
    return v

def low_keep(v):
    return (low(v), None)

def low_pass(kept, grad):
    return (grad,)

def back_keep(v):
    return (v, None)

def back_low(kept, grad):
    return (low(grad),)
low.defvjp(low_keep, low_pass)
low_back.defvjp(back_keep, back_low)
EPS = 1e-05
NEG = -1e+30

def layer_norm(v, gain, shift):
    center = v - lax.optimization_barrier(jnp.mean(v, axis=-1, keepdims=True))
    spread = lax.optimization_barrier(jnp.mean(center * center, axis=-1, keepdims=True))
    return center * lax.rsqrt(spread + EPS) * gain + shift

def matmul(left, right):
    return jnp.dot(left, right, precision=lax.Precision.HIGHEST)

def attend_one(query, keyed, valued, seg):
    length = query.shape[0]
    scores = jnp.einsum('qhe,khe->hqk', query, keyed, precision=lax.Precision.HIGHEST) / math.sqrt(HEAD_DIM)
    scores = low_back(scores)
    pos = jnp.arange(length, dtype=jnp.int32)
    allowed = (pos[:, None] >= pos[None, :]) & (seg[:, None] == seg[None, :])
    scores = jnp.where(allowed[None], scores, NEG)
    top = lax.optimization_barrier(jnp.max(scores, axis=-1, keepdims=True))
    weights = jnp.where(allowed[None], jnp.exp(scores - top), 0.0)
    probs = low(weights / lax.optimization_barrier(jnp.sum(weights, axis=-1, keepdims=True)))
    return jnp.einsum('hqk,khe->qhe', probs, valued, precision=lax.Precision.HIGHEST)

def block(x, g1, c1, wq, bq, wk, wv, bv, wo, bo, g2, c2, w1, b1, w2, b2, segments, valid_mask):
    normed1 = low(layer_norm(x, g1, c1))
    query = low(low_back(matmul(normed1, wq) + bq))
    keyed = low(low_back(matmul(normed1, wk)))
    valued = low(low_back(matmul(normed1, wv) + bv))
    shape4 = (SEQS, SEQ_LEN, HEADS, HEAD_DIM)
    attend = jax.checkpoint(attend_one)
    mixed = lax.map(lambda t: attend(t[0], t[1], t[2], t[3]), (query.reshape(shape4), keyed.reshape(shape4), valued.reshape(shape4), segments))
    mixed = low(low_back(mixed.reshape(TOKENS, D)))
    attended = low_back(matmul(mixed, wo) + bo)
    resid = x + attended
    normed2 = low(layer_norm(resid, g2, c2))
    pre = low_back(matmul(normed2, w1) + b1)
    act = low(jax.nn.gelu(pre, approximate=False))
    branch = low_back(matmul(act, w2) + b2)
    output = resid + branch
    weight = valid_mask.astype(jnp.float32)
    count = jnp.maximum(lax.optimization_barrier(jnp.sum(weight, axis=1)), 1.0) * D

    def per_seq(v):
        return lax.optimization_barrier(jnp.sum(weight * lax.optimization_barrier(jnp.sum(v * v, axis=-1)).reshape(SEQS, SEQ_LEN), axis=1))
    sums = jnp.stack([per_seq(attended), per_seq(branch), per_seq(output)], axis=1)
    return (output, jnp.sqrt(sums / count[:, None]))

def reference(latents, norm1_gain, norm1_shift, query_weight, query_bias, key_weight, value_weight, value_bias, out_weight, out_bias, norm2_gain, norm2_shift, hidden_weight, hidden_bias, proj_weight, proj_bias, segments, valid_mask, cotangent):
    params = (latents.astype(jnp.float32), norm1_gain, norm1_shift, query_weight.astype(jnp.float32), query_bias, key_weight.astype(jnp.float32), value_weight.astype(jnp.float32), value_bias, out_weight.astype(jnp.float32), out_bias, norm2_gain, norm2_shift, hidden_weight.astype(jnp.float32), hidden_bias, proj_weight.astype(jnp.float32), proj_bias)

    def forward(*args):
        return block(*args, segments, valid_mask)
    output, back, rms = jax.vjp(forward, *params, has_aux=True)
    grads = back(cotangent.astype(jnp.float32))
    return (output.astype(jnp.bfloat16), grads[0], grads[1], grads[2], grads[3], grads[4], grads[5], grads[6], grads[7], grads[8], grads[9], grads[10], grads[11], grads[12], grads[13], grads[14], grads[15], rms)
```

```python
import functools
import math

import jax
import jax.numpy as jnp
from jax import lax
from jax.experimental import pallas as pl
from jax.experimental.pallas import tpu as pltpu
from jax.sharding import PartitionSpec as P

HEAD_DIM = 160
MAX_DOC = 512
EPS = 1e-05
NEG = -1e30
BLK = 256
WIN = 256
LANES = 128
SCALE = 1.0 / math.sqrt(HEAD_DIM)
LOG2E = 1.0 / math.log(2.0)
BF = jnp.bfloat16
F32 = jnp.float32
VMEM_MAX = 60 << 20


def nn(a, b):
    return lax.dot_general(a, b, (((1,), (0,)), ((), ())), preferred_element_type=F32)


def nt(a, b):
    return lax.dot_general(a, b, (((1,), (1,)), ((), ())), preferred_element_type=F32)


def tn(a, b):
    return lax.dot_general(a, b, (((0,), (0,)), ((), ())), preferred_element_type=F32)


def whole(shape):
    return pl.BlockSpec(shape, lambda *_: (0,) * len(shape), pipeline_mode=pl.Buffered(1))


def held(shape):
    return pl.BlockSpec(shape, lambda *_: (0,) * len(shape))


def rows(width):
    return pl.BlockSpec((BLK, width), lambda i: (i, 0))


def column_of(row):
    n = row.shape[1]
    eye = lax.broadcasted_iota(jnp.int32, (n, n), 0) == lax.broadcasted_iota(jnp.int32, (n, n), 1)
    return jnp.sum(jnp.where(eye, row, jnp.zeros_like(row)), axis=1, keepdims=True)


def fold8(t):
    return jnp.sum(t.reshape(t.shape[0] // 8, 8, t.shape[1]), axis=0)


def params(grid, vmem=VMEM_MAX):
    return pltpu.CompilerParams(dimension_semantics=("arbitrary",) * grid, vmem_limit_bytes=vmem)


def normalize(v):
    center = v - jnp.mean(v, axis=-1, keepdims=True)
    inv = lax.rsqrt(jnp.mean(center * center, axis=-1, keepdims=True) + EPS)
    return center * inv, inv


def project_kernel(x_ref, g_ref, c_ref, wq_ref, wk_ref, wv_ref, bq_ref, bv_ref, n_ref, q_ref, k_ref, v_ref):
    hat, _ = normalize(x_ref[...].astype(F32))
    normed = (hat * g_ref[...] + c_ref[...]).astype(BF)
    n_ref[...] = normed
    q_ref[...] = (nt(normed, wq_ref[...]) + bq_ref[...]).astype(BF)
    k_ref[...] = nt(normed, wk_ref[...]).astype(BF)
    v_ref[...] = (nt(normed, wv_ref[...]) + bv_ref[...]).astype(BF)


def project(x, g1, c1, wq, wk, wv, bq, bv):
    tokens, width = x.shape
    out = wq.shape[0]
    return pl.pallas_call(
        project_kernel,
        grid=(tokens // BLK,),
        in_specs=[rows(width), whole((1, width)), whole((1, width))]
        + [whole((out, width))] * 3
        + [whole((1, out))] * 2,
        out_specs=[rows(width)] + [rows(out)] * 3,
        out_shape=[jax.ShapeDtypeStruct((tokens, width), BF)] + [jax.ShapeDtypeStruct((tokens, out), BF)] * 3,
        compiler_params=params(1),
        cost_estimate=pl.CostEstimate(
            flops=6 * tokens * width * out, bytes_accessed=2 * (tokens * (2 * width + 3 * out) + 3 * width * out), transcendentals=0
        ),
        name="project",
    )(x, g1, c1, wq, wk, wv, bq, bv)


HEADS_IN_GROUP = 4
GROUP = HEADS_IN_GROUP * HEAD_DIM


def window_of(head):
    low = head * HEAD_DIM
    start = low // LANES * LANES
    return start, low - start


def lane_mask(offset):
    lane = lax.broadcasted_iota(jnp.int32, (1, WIN), 1)
    return (lane >= offset) & (lane < offset + HEAD_DIM)


def spread(parts):
    tiles = [None] * (GROUP // LANES)
    for head, part in enumerate(parts):
        first = window_of(head)[0] // LANES
        for half in range(WIN // LANES):
            piece = part[:, half * LANES : (half + 1) * LANES]
            at = first + half
            tiles[at] = piece if tiles[at] is None else tiles[at] + piece
    return jnp.concatenate(tiles, axis=1)


def attend_kernel(seg_s, q_ref, k_ref, v_ref, seg_ref, o_ref, lse_ref, bias):
    s, i = pl.program_id(0), pl.program_id(1)
    groups = q_ref.shape[1] // GROUP
    back = MAX_DOC // BLK
    lead = seg_s[s, i * BLK]
    count = jnp.int32(1)
    for d in range(1, back + 1):
        last = seg_s[s, jnp.maximum((i - d + 1) * BLK - 1, 0)]
        count = count + jnp.where((i >= d) & (last == lead), 1, 0)
    seg_col = column_of(seg_ref[0, :, pl.ds(pl.multiple_of(i * BLK, BLK), BLK)])

    def body(blocks):
        keys = blocks * BLK
        start = pl.multiple_of((i + 1 - blocks) * BLK, BLK)
        row = i * BLK + lax.broadcasted_iota(jnp.int32, (BLK, keys), 0)
        col = start + lax.broadcasted_iota(jnp.int32, (BLK, keys), 1)
        allowed = (row >= col) & (seg_col == seg_ref[0, :, pl.ds(start, keys)])
        bias[:, :keys] = jnp.where(allowed, 0.0, NEG)

        def group(gi, _):
            parts = []
            lse = lse_ref[...]
            head_lane = lax.broadcasted_iota(jnp.int32, (1, LANES), 1)
            for h in range(HEADS_IN_GROUP):
                at, off = window_of(h)
                lanes = pl.ds(pl.multiple_of(gi * GROUP + at, LANES), WIN)
                mask = lane_mask(off)
                q = q_ref[:, lanes]
                q = jnp.where(mask, q, jnp.zeros_like(q))
                t = nt(q, k_ref[pl.ds(start, keys), lanes]) * (SCALE * LOG2E) + bias[:, :keys]
                top = jnp.max(t, axis=1, keepdims=True)
                p = jnp.exp2(t - top)
                total = jnp.sum(p, axis=1, keepdims=True)
                o = nn(p.astype(BF), v_ref[pl.ds(start, keys), lanes])
                parts.append(jnp.where(mask, o * (1.0 / total), 0.0))
                lse = jnp.where(head_lane == gi * HEADS_IN_GROUP + h, top + jnp.log2(total), lse)
            lse_ref[...] = lse
            o_ref[:, pl.ds(pl.multiple_of(gi * GROUP, LANES), GROUP)] = spread(parts).astype(BF)
            return 0

        lax.fori_loop(0, groups, group, 0)

    lse_ref[...] = jnp.zeros_like(lse_ref)
    for blocks in range(1, back + 2):
        pl.when(count == blocks)(functools.partial(body, blocks))


def attend(q, k, v, seg):
    tokens, width = q.shape
    seqs, length = seg.shape
    n = length // BLK
    spec_q = pl.BlockSpec((BLK, width), lambda s, i, _: (s * n + i, 0))
    spec_k = pl.BlockSpec((length, width), lambda s, i, _: (s, 0))
    pairs = seqs * n * 2.5 * BLK * BLK * (width // HEAD_DIM)
    return pl.pallas_call(
        attend_kernel,
        grid_spec=pltpu.PrefetchScalarGridSpec(
            num_scalar_prefetch=1,
            grid=(seqs, n),
            in_specs=[spec_q, spec_k, spec_k, pl.BlockSpec((1, 1, length), lambda s, i, _: (s, 0, 0))],
            out_specs=[spec_q, pl.BlockSpec((BLK, LANES), lambda s, i, _: (s * n + i, 0))],
            scratch_shapes=[pltpu.VMEM((BLK, BLK + MAX_DOC), F32)],
        ),
        out_shape=[jax.ShapeDtypeStruct((tokens, width), BF), jax.ShapeDtypeStruct((tokens, LANES), F32)],
        compiler_params=params(2),
        cost_estimate=pl.CostEstimate(
            flops=int(pairs * 8 * WIN), bytes_accessed=8 * tokens * width, transcendentals=int(pairs)
        ),
        name="attend",
    )(seg, q, k, v, seg.reshape(seqs, 1, length))


def attend_back_kernel(
    seg_s, q_ref, do_ref, o_ref, lse_ref, k_ref, v_ref, seg_ref, dq_ref, dk_ref, dv_ref, bias, dq_acc, lse_t, delta_t
):
    s, j = pl.program_id(0), pl.program_id(1)
    n = pl.num_programs(1)
    length, width = q_ref.shape
    groups = width // GROUP
    ahead = MAX_DOC // BLK

    @pl.when(j == 0)
    def _():
        dq_acc[...] = jnp.zeros_like(dq_acc)
        head = lax.broadcasted_iota(jnp.int32, (16, width), 0)
        lane = lax.broadcasted_iota(jnp.int32, (16, width), 1)
        pick = jnp.where((lane >= head * HEAD_DIM) & (lane < (head + 1) * HEAD_DIM), 1.0, 0.0).astype(BF)
        for b in range(length // BLK):
            at = slice(b * BLK, (b + 1) * BLK)
            lse_t[:, at] = lse_ref[at, :].T[:16, :]
            prod = do_ref[at, :].astype(F32) * o_ref[at, :].astype(F32)
            high = prod.astype(BF)
            rest = (prod - high.astype(F32)).astype(BF)
            delta_t[:, at] = nt(pick, high) + nt(pick, rest)

    tail = seg_s[s, (j + 1) * BLK - 1]
    count = jnp.int32(1)
    for d in range(1, ahead + 1):
        first = seg_s[s, jnp.minimum((j + d) * BLK, length - 1)]
        count = count + jnp.where((j + d < n) & (first == tail), 1, 0)
    start = pl.multiple_of(j * BLK, BLK)
    seg_col = column_of(seg_ref[0, :, pl.ds(start, BLK)])

    def body(blocks):
        queries = blocks * BLK
        span = pl.ds(start, queries)
        row = lax.broadcasted_iota(jnp.int32, (BLK, queries), 0)
        col = lax.broadcasted_iota(jnp.int32, (BLK, queries), 1)
        allowed = (row <= col) & (seg_col == seg_ref[0, :, span])
        bias[:, :queries] = jnp.where(allowed, 0.0, NEG)

        def group(gi, _):
            dks, dvs = [], []
            for h in range(HEADS_IN_GROUP):
                at, off = window_of(h)
                lanes = pl.ds(pl.multiple_of(gi * GROUP + at, LANES), WIN)
                mask = lane_mask(off)
                head = pl.ds(gi * HEADS_IN_GROUP + h, 1)
                k = k_ref[:, lanes]
                k = jnp.where(mask, k, jnp.zeros_like(k))
                v = v_ref[:, lanes]
                v = jnp.where(mask, v, jnp.zeros_like(v))
                q = q_ref[span, lanes]
                do = do_ref[span, lanes]
                t = nt(k, q) * (SCALE * LOG2E) + bias[:, :queries]
                p = jnp.exp2(t - lse_t[head, span])
                dvs.append(jnp.where(mask, nn(p.astype(BF), do), 0.0))
                ds = (p * (nt(v, do) - delta_t[head, span])).astype(BF)
                dks.append(jnp.where(mask, nn(ds, q), 0.0))
                dq_acc[span, lanes] += tn(ds, k)
            out = pl.ds(pl.multiple_of(gi * GROUP, LANES), GROUP)
            dk_ref[:, out] = (spread(dks) * SCALE).astype(BF)
            dv_ref[:, out] = spread(dvs).astype(BF)
            return 0

        lax.fori_loop(0, groups, group, 0)

    for blocks in range(1, ahead + 2):
        pl.when(count == blocks)(functools.partial(body, blocks))

    @pl.when(j == n - 1)
    def _():
        dq_ref[...] = (dq_acc[...] * SCALE).astype(BF)


def attend_back(q, k, v, seg, mixed, d_mixed, lse):
    tokens, width = q.shape
    seqs, length = seg.shape
    n = length // BLK
    spec_k = pl.BlockSpec((BLK, width), lambda s, j, _: (s * n + j, 0))
    spec_q = pl.BlockSpec((length, width), lambda s, j, _: (s, 0))
    pairs = seqs * n * 2.5 * BLK * BLK * (width // HEAD_DIM)
    return pl.pallas_call(
        attend_back_kernel,
        grid_spec=pltpu.PrefetchScalarGridSpec(
            num_scalar_prefetch=1,
            grid=(seqs, n),
            in_specs=[
                spec_q,
                spec_q,
                spec_q,
                pl.BlockSpec((length, LANES), lambda s, j, _: (s, 0)),
                spec_k,
                spec_k,
                pl.BlockSpec((1, 1, length), lambda s, j, _: (s, 0, 0)),
            ],
            out_specs=[spec_q, spec_k, spec_k],
            scratch_shapes=[
                pltpu.VMEM((BLK, BLK + MAX_DOC), F32),
                pltpu.VMEM((length, width), F32),
                pltpu.VMEM((16, length), F32),
                pltpu.VMEM((16, length), F32),
            ],
        ),
        out_shape=[jax.ShapeDtypeStruct((tokens, width), BF)] * 3,
        compiler_params=params(2),
        cost_estimate=pl.CostEstimate(
            flops=int(pairs * 20 * WIN), bytes_accessed=16 * tokens * width, transcendentals=int(pairs)
        ),
        name="attend_back",
    )(seg, q, d_mixed, mixed, lse, k, v, seg.reshape(seqs, 1, length))


def middle_kernel(
    own, m_ref, x_ref, g_ref, w_ref, wo_ref, w1_ref, w2_ref, bo_ref, g2_ref, c2_ref, b1_ref, b2_ref,
    y_ref, dr_ref, dm_ref, gwo_ref, gw1_ref, gw2_ref, vec_ref, sq_ref,
):
    i = pl.program_id(0)

    @pl.when(i == 0)
    def _():
        for ref in (gwo_ref, gw1_ref, gw2_ref, vec_ref):
            ref[...] = jnp.zeros_like(ref)

    mixed = m_ref[...]
    cot = g_ref[...]
    attended = nn(mixed, wo_ref[...]) + bo_ref[...]
    resid = x_ref[...].astype(F32) + attended
    hat, inv = normalize(resid)
    normed = (hat * g2_ref[...] + c2_ref[...]).astype(BF)
    pre = nt(normed, w1_ref[...]) + b1_ref[...]
    cdf = 0.5 + 0.5 * lax.erf(pre * math.sqrt(0.5))
    act = (pre * cdf).astype(BF)
    slope = cdf + pre * jnp.exp(-0.5 * pre * pre) * (1.0 / math.sqrt(2.0 * math.pi))
    branch = nn(act, w2_ref[...]) + b2_ref[...]
    output = resid + branch
    y_ref[...] = output.astype(BF)
    weight = column_of(w_ref[0])
    lane = lax.broadcasted_iota(jnp.int32, (1, LANES), 1)
    sums = jnp.zeros((1, LANES), F32)
    for at, v in enumerate((attended, branch, output)):
        one = jnp.sum(weight * jnp.sum(v * v, axis=1, keepdims=True), axis=0, keepdims=True)
        sums = jnp.where(lane == at, one, sums)
    sq_ref[...] = jnp.broadcast_to(sums, sq_ref.shape[1:])[None]

    d_pre = (nt(cot, w2_ref[...]) * slope).astype(BF)
    gw2_ref[...] += tn(act[:, :own], cot)
    gw1_ref[...] += tn(d_pre[:, :own], normed)
    d_normed = nn(d_pre, w1_ref[...])
    d_hat = d_normed * g2_ref[...]
    grad = cot.astype(F32)
    d_resid = grad + inv * (
        d_hat - jnp.mean(d_hat, axis=1, keepdims=True) - hat * jnp.mean(d_hat * hat, axis=1, keepdims=True)
    )
    dr_ref[...] = d_resid
    low = d_resid.astype(BF)
    gwo_ref[...] += tn(mixed[:, :own], low)
    dm_ref[...] = nt(low, wo_ref[...]).astype(BF)
    for at, v in enumerate((grad, d_pre.astype(F32), d_normed * hat, d_normed, low.astype(F32))):
        vec_ref[at] += fold8(v)


def middle(own, mixed, x, cot, valid, wo, w1, w2, bo, g2, c2, b1, b2):
    tokens, width = x.shape
    inner, hidden = wo.shape[0], w1.shape[0]
    n = tokens // BLK
    return pl.pallas_call(
        functools.partial(middle_kernel, own),
        grid=(n,),
        in_specs=[rows(inner), rows(width), rows(width), pl.BlockSpec((1, 1, BLK), lambda i: (i, 0, 0))]
        + [whole((inner, width)), whole((hidden, width)), whole((hidden, width))]
        + [whole((1, width))] * 3
        + [whole((1, hidden)), whole((1, width))],
        out_specs=[rows(width), rows(width), rows(inner)]
        + [held((own, width))] * 3
        + [held((5, 8, width)), pl.BlockSpec((1, 8, LANES), lambda i: (i, 0, 0))],
        out_shape=[
            jax.ShapeDtypeStruct((tokens, width), BF),
            jax.ShapeDtypeStruct((tokens, width), F32),
            jax.ShapeDtypeStruct((tokens, inner), BF),
        ]
        + [jax.ShapeDtypeStruct((own, width), F32)] * 3
        + [jax.ShapeDtypeStruct((5, 8, width), F32), jax.ShapeDtypeStruct((n, 8, LANES), F32)],
        compiler_params=params(1),
        cost_estimate=pl.CostEstimate(
            flops=2 * tokens * width * (6 * width + 3 * own),
            bytes_accessed=14 * tokens * width + 6 * width * width,
            transcendentals=2 * tokens * hidden,
        ),
        name="middle",
    )(mixed, x, cot, valid.astype(F32).reshape(n, 1, BLK), wo, w1, w2, bo, g2, c2, b1, b2)


def finish_kernel(dq_ref, dk_ref, dv_ref, x_ref, dr_ref, g_ref, wq_ref, wk_ref, wv_ref, dx_ref, vec_ref):
    @pl.when(pl.program_id(0) == 0)
    def _():
        vec_ref[...] = jnp.zeros_like(vec_ref)

    d_normed = nn(dq_ref[...], wq_ref[...]) + nn(dk_ref[...], wk_ref[...]) + nn(dv_ref[...], wv_ref[...])
    hat, inv = normalize(x_ref[...].astype(F32))
    d_hat = d_normed * g_ref[...]
    dx_ref[...] = dr_ref[...] + inv * (
        d_hat - jnp.mean(d_hat, axis=1, keepdims=True) - hat * jnp.mean(d_hat * hat, axis=1, keepdims=True)
    )
    vec_ref[0] += fold8(d_normed * hat)
    vec_ref[1] += fold8(d_normed)


def finish(dq, dk, dv, x, d_resid, g1, wq, wk, wv):
    tokens, width = x.shape
    inner = wq.shape[0]
    return pl.pallas_call(
        finish_kernel,
        grid=(tokens // BLK,),
        in_specs=[rows(inner)] * 3 + [rows(width), rows(width), whole((1, width))] + [whole((inner, width))] * 3,
        out_specs=[rows(width), held((2, 8, width))],
        out_shape=[jax.ShapeDtypeStruct((tokens, width), F32), jax.ShapeDtypeStruct((2, 8, width), F32)],
        compiler_params=params(1),
        cost_estimate=pl.CostEstimate(
            flops=6 * tokens * width * inner, bytes_accessed=16 * tokens * width + 6 * width * inner, transcendentals=0
        ),
        name="finish",
    )(dq, dk, dv, x, d_resid, g1, wq, wk, wv)


def round_kernel(x_ref, o_ref):
    o_ref[...] = x_ref[...].astype(BF)


def round_rows(t):
    count, width = t.shape
    return pl.pallas_call(
        round_kernel,
        grid=(pl.cdiv(count, BLK),),
        in_specs=[rows(width)],
        out_specs=rows(width),
        out_shape=jax.ShapeDtypeStruct(t.shape, BF),
        compiler_params=params(1),
        name="round_rows",
    )(t)


def gather(parts, extra, dp, tp):
    own, width = parts[0].shape
    piece = own // dp
    mine = jnp.stack([t.reshape(dp, piece, width) for t in parts], axis=1)
    mine = lax.dynamic_index_in_dim(mine, lax.axis_index("dp"), 0, keepdims=False).astype(F32)
    mine = mine.reshape(len(parts) * piece, width)
    if extra is not None:
        mine = jnp.concatenate([mine, extra], axis=0)
    full = lax.all_gather(mine, ("tensor", "dp"))
    full = full.reshape(tp, dp, -1, width)
    vecs = full[:, 0, len(parts) * piece :]
    full = round_rows(full.reshape(-1, width)).reshape(full.shape)
    twice = jnp.concatenate([full, full], axis=0)
    full = lax.dynamic_slice_in_dim(twice, lax.axis_index("tensor"), tp, 0)
    count = len(parts) * piece
    body = full[:, :, :count].reshape(tp, dp, len(parts), piece, width)
    wholes = [body[:, :, m].reshape(tp * own, width) for m in range(len(parts))]
    vecs = jnp.concatenate([vecs, vecs], axis=0)
    return wholes, lax.dynamic_slice_in_dim(vecs, lax.axis_index("tensor"), tp, 0)


def shards(dp, tp, x, g1, c1, wq, bq, wk, wv, bv, wo, bo, g2, c2, w1, b1, w2, b2, seg, valid, cot):
    tokens, width = x.shape
    seqs, length = seg.shape
    own = wq.shape[1]

    def line(t):
        return t.reshape(1, -1)

    biases = jnp.concatenate([bq, bv, b1]).reshape(3, own)
    extra = jnp.zeros((8, width), F32).at[:3, :own].set(biases)
    (fq, fk, fv), more = gather([wq.T, wk.T, wv.T], extra, dp, tp)
    (fo, f1, f2), _ = gather([wo, w1.T, w2], None, dp, tp)
    abq, abv, ab1 = (line(more[:, r, :own]) for r in range(3))

    normed1, q, k, v = project(x, line(g1), line(c1), fq, fk, fv, abq, abv)
    mixed, lse = attend(q, k, v, seg)
    y, d_resid, d_mixed, gwo, gw1, gw2, vec, sq = middle(
        own, mixed, x, cot, valid, fo, f1, f2, line(bo), line(g2), line(c2), ab1, line(b2)
    )
    dq, dk, dv = attend_back(q, k, v, seg, mixed, d_mixed, lse)
    mine = [t[:, :own] for t in (dq, dk, dv)]
    gq, gk, gv = (tn(t, normed1) for t in mine)
    gbq, gbv = (jnp.sum(t.astype(F32), axis=0) for t in (mine[0], mine[2]))
    grad_input, last = finish(dq, dk, dv, x, d_resid, line(g1), fq, fk, fv)

    weight = valid.astype(F32)
    counted = jnp.maximum(jnp.sum(weight, axis=1), 1.0) * width
    stat = jnp.sum(sq[:, 0, :3].reshape(seqs, length // BLK, 3), axis=1)
    rms = jnp.sqrt(stat / counted[:, None])

    vec = jnp.sum(vec, axis=1)
    last = jnp.sum(last, axis=1)
    big = lax.psum((gwo, gw1, gw2), "dp")
    mats = lax.psum((gq, gk, gv), "dp")
    gb2, gb1, gg2, gc2, gbo, gg1, gc1, gbq, gbv = lax.psum(
        (vec[0], vec[1, :own], vec[2], vec[3], vec[4], last[0], last[1], gbq, gbv), "dp"
    )
    gwo, gw1, gw2 = big
    gq, gk, gv = mats
    return (
        y, grad_input, gg1, gc1, gq.T, gbq, gk.T, gv.T, gbv, gwo, gbo, gg2, gc2, gw1.T, gb1, gw2, gb2, rms,
    )


def solution(mesh):
    dp, tp = mesh.shape["dp"], mesh.shape["tensor"]
    tok, col, row, vec, rep = P("dp", None), P(None, "tensor"), P("tensor", None), P("tensor"), P()
    return jax.shard_map(
        functools.partial(shards, dp, tp),
        mesh=mesh,
        in_specs=(tok, rep, rep, col, vec, col, col, vec, row, rep, rep, rep, col, vec, row, rep, tok, tok, tok),
        out_specs=(tok, tok, rep, rep, col, vec, col, col, vec, row, rep, rep, rep, col, vec, row, rep, tok),
        check_vma=False,
    )
```

```python
import functools
import math

import jax
import jax.numpy as jnp
from jax import lax
from jax.experimental import pallas as pl
from jax.experimental.pallas import tpu as pltpu
from jax.sharding import PartitionSpec as P

HEAD_DIM = 160
MAX_DOC = 512
EPS = 1e-05
NEG = -1e30
BLK = 256
WIN = 256
LANES = 128
SCALE = 1.0 / math.sqrt(HEAD_DIM)
LOG2E = 1.0 / math.log(2.0)
BF = jnp.bfloat16
F32 = jnp.float32
VMEM_MAX = 60 << 20


def nn(a, b):
    return lax.dot_general(a, b, (((1,), (0,)), ((), ())), preferred_element_type=F32)


def nt(a, b):
    return lax.dot_general(a, b, (((1,), (1,)), ((), ())), preferred_element_type=F32)


def tn(a, b):
    return lax.dot_general(a, b, (((0,), (0,)), ((), ())), preferred_element_type=F32)


def whole(shape):
    return pl.BlockSpec(shape, lambda *_: (0,) * len(shape), pipeline_mode=pl.Buffered(1))


def held(shape):
    return pl.BlockSpec(shape, lambda *_: (0,) * len(shape))


def rows(width):
    return pl.BlockSpec((BLK, width), lambda i: (i, 0))


def column_of(row):
    n = row.shape[1]
    eye = lax.broadcasted_iota(jnp.int32, (n, n), 0) == lax.broadcasted_iota(jnp.int32, (n, n), 1)
    return jnp.sum(jnp.where(eye, row, jnp.zeros_like(row)), axis=1, keepdims=True)


def fold8(t):
    return jnp.sum(t.reshape(t.shape[0] // 8, 8, t.shape[1]), axis=0)


def params(grid, vmem=VMEM_MAX):
    return pltpu.CompilerParams(dimension_semantics=("arbitrary",) * grid, vmem_limit_bytes=vmem)


def normalize(v):
    center = v - jnp.mean(v, axis=-1, keepdims=True)
    inv = lax.rsqrt(jnp.mean(center * center, axis=-1, keepdims=True) + EPS)
    return center * inv, inv


def project_kernel(x_ref, g_ref, c_ref, wq_ref, wk_ref, wv_ref, bq_ref, bv_ref, n_ref, q_ref, k_ref, v_ref):
    hat, _ = normalize(x_ref[...].astype(F32))
    normed = (hat * g_ref[...] + c_ref[...]).astype(BF)
    n_ref[...] = normed
    q_ref[...] = (nt(normed, wq_ref[...]) + bq_ref[...]).astype(BF)
    k_ref[...] = nt(normed, wk_ref[...]).astype(BF)
    v_ref[...] = (nt(normed, wv_ref[...]) + bv_ref[...]).astype(BF)


def project(x, g1, c1, wq, wk, wv, bq, bv):
    tokens, width = x.shape
    out = wq.shape[0]
    return pl.pallas_call(
        project_kernel,
        grid=(tokens // BLK,),
        in_specs=[rows(width), whole((1, width)), whole((1, width))]
        + [whole((out, width))] * 3
        + [whole((1, out))] * 2,
        out_specs=[rows(width)] + [rows(out)] * 3,
        out_shape=[jax.ShapeDtypeStruct((tokens, width), BF)] + [jax.ShapeDtypeStruct((tokens, out), BF)] * 3,
        compiler_params=params(1),
        cost_estimate=pl.CostEstimate(
            flops=6 * tokens * width * out, bytes_accessed=2 * (tokens * (2 * width + 3 * out) + 3 * width * out), transcendentals=0
        ),
        name="project",
    )(x, g1, c1, wq, wk, wv, bq, bv)


HEADS_IN_GROUP = 4
GROUP = HEADS_IN_GROUP * HEAD_DIM


def window_of(head):
    low = head * HEAD_DIM
    start = low // LANES * LANES
    return start, low - start


def lane_mask(offset):
    lane = lax.broadcasted_iota(jnp.int32, (1, WIN), 1)
    return (lane >= offset) & (lane < offset + HEAD_DIM)


def spread(parts):
    tiles = [None] * (GROUP // LANES)
    for head, part in enumerate(parts):
        first = window_of(head)[0] // LANES
        for half in range(WIN // LANES):
            piece = part[:, half * LANES : (half + 1) * LANES]
            at = first + half
            tiles[at] = piece if tiles[at] is None else tiles[at] + piece
    return jnp.concatenate(tiles, axis=1)


def attend_kernel(seg_s, q_ref, k_ref, v_ref, seg_ref, o_ref, lse_ref, bias):
    s, i = pl.program_id(0), pl.program_id(1)
    groups = q_ref.shape[1] // GROUP
    back = MAX_DOC // BLK
    lead = seg_s[s, i * BLK]
    count = jnp.int32(1)
    for d in range(1, back + 1):
        last = seg_s[s, jnp.maximum((i - d + 1) * BLK - 1, 0)]
        count = count + jnp.where((i >= d) & (last == lead), 1, 0)
    seg_col = column_of(seg_ref[0, :, pl.ds(pl.multiple_of(i * BLK, BLK), BLK)])

    def body(blocks):
        keys = blocks * BLK
        start = pl.multiple_of((i + 1 - blocks) * BLK, BLK)
        row = i * BLK + lax.broadcasted_iota(jnp.int32, (BLK, keys), 0)
        col = start + lax.broadcasted_iota(jnp.int32, (BLK, keys), 1)
        allowed = (row >= col) & (seg_col == seg_ref[0, :, pl.ds(start, keys)])
        bias[:, :keys] = jnp.where(allowed, 0.0, NEG)

        def group(gi, _):
            parts = []
            lse = lse_ref[...]
            head_lane = lax.broadcasted_iota(jnp.int32, (1, LANES), 1)
            for h in range(HEADS_IN_GROUP):
                at, off = window_of(h)
                lanes = pl.ds(pl.multiple_of(gi * GROUP + at, LANES), WIN)
                mask = lane_mask(off)
                q = q_ref[:, lanes]
                q = jnp.where(mask, q, jnp.zeros_like(q))
                t = nt(q, k_ref[pl.ds(start, keys), lanes]) * (SCALE * LOG2E) + bias[:, :keys]
                top = jnp.max(t, axis=1, keepdims=True)
                p = jnp.exp2(t - top)
                total = jnp.sum(p, axis=1, keepdims=True)
                o = nn(p.astype(BF), v_ref[pl.ds(start, keys), lanes])
                parts.append(jnp.where(mask, o * (1.0 / total), 0.0))
                lse = jnp.where(head_lane == gi * HEADS_IN_GROUP + h, top + jnp.log2(total), lse)
            lse_ref[...] = lse
            o_ref[:, pl.ds(pl.multiple_of(gi * GROUP, LANES), GROUP)] = spread(parts).astype(BF)
            return 0

        lax.fori_loop(0, groups, group, 0)

    lse_ref[...] = jnp.zeros_like(lse_ref)
    for blocks in range(1, back + 2):
        pl.when(count == blocks)(functools.partial(body, blocks))


def attend(q, k, v, seg):
    tokens, width = q.shape
    seqs, length = seg.shape
    n = length // BLK
    spec_q = pl.BlockSpec((BLK, width), lambda s, i, _: (s * n + i, 0))
    spec_k = pl.BlockSpec((length, width), lambda s, i, _: (s, 0))
    pairs = seqs * n * 2.5 * BLK * BLK * (width // HEAD_DIM)
    return pl.pallas_call(
        attend_kernel,
        grid_spec=pltpu.PrefetchScalarGridSpec(
            num_scalar_prefetch=1,
            grid=(seqs, n),
            in_specs=[spec_q, spec_k, spec_k, pl.BlockSpec((1, 1, length), lambda s, i, _: (s, 0, 0))],
            out_specs=[spec_q, pl.BlockSpec((BLK, LANES), lambda s, i, _: (s * n + i, 0))],
            scratch_shapes=[pltpu.VMEM((BLK, BLK + MAX_DOC), F32)],
        ),
        out_shape=[jax.ShapeDtypeStruct((tokens, width), BF), jax.ShapeDtypeStruct((tokens, LANES), F32)],
        compiler_params=params(2),
        cost_estimate=pl.CostEstimate(
            flops=int(pairs * 8 * WIN), bytes_accessed=8 * tokens * width, transcendentals=int(pairs)
        ),
        name="attend",
    )(seg, q, k, v, seg.reshape(seqs, 1, length))


def attend_back_kernel(
    seg_s, q_ref, do_ref, o_ref, lse_ref, k_ref, v_ref, seg_ref, dq_ref, dk_ref, dv_ref, bias, dq_acc, lse_t, delta_t
):
    s, j = pl.program_id(0), pl.program_id(1)
    n = pl.num_programs(1)
    length, width = q_ref.shape
    groups = width // GROUP
    ahead = MAX_DOC // BLK

    @pl.when(j == 0)
    def _():
        dq_acc[...] = jnp.zeros_like(dq_acc)
        head = lax.broadcasted_iota(jnp.int32, (16, width), 0)
        lane = lax.broadcasted_iota(jnp.int32, (16, width), 1)
        pick = jnp.where((lane >= head * HEAD_DIM) & (lane < (head + 1) * HEAD_DIM), 1.0, 0.0).astype(BF)
        for b in range(length // BLK):
            at = slice(b * BLK, (b + 1) * BLK)
            lse_t[:, at] = lse_ref[at, :].T[:16, :]
            prod = do_ref[at, :].astype(F32) * o_ref[at, :].astype(F32)
            high = prod.astype(BF)
            rest = (prod - high.astype(F32)).astype(BF)
            delta_t[:, at] = nt(pick, high) + nt(pick, rest)

    tail = seg_s[s, (j + 1) * BLK - 1]
    count = jnp.int32(1)
    for d in range(1, ahead + 1):
        first = seg_s[s, jnp.minimum((j + d) * BLK, length - 1)]
        count = count + jnp.where((j + d < n) & (first == tail), 1, 0)
    start = pl.multiple_of(j * BLK, BLK)
    seg_col = column_of(seg_ref[0, :, pl.ds(start, BLK)])

    def body(blocks):
        queries = blocks * BLK
        span = pl.ds(start, queries)
        row = lax.broadcasted_iota(jnp.int32, (BLK, queries), 0)
        col = lax.broadcasted_iota(jnp.int32, (BLK, queries), 1)
        allowed = (row <= col) & (seg_col == seg_ref[0, :, span])
        bias[:, :queries] = jnp.where(allowed, 0.0, NEG)

        def group(gi, _):
            dks, dvs = [], []
            for h in range(HEADS_IN_GROUP):
                at, off = window_of(h)
                lanes = pl.ds(pl.multiple_of(gi * GROUP + at, LANES), WIN)
                mask = lane_mask(off)
                head = pl.ds(gi * HEADS_IN_GROUP + h, 1)
                k = k_ref[:, lanes]
                k = jnp.where(mask, k, jnp.zeros_like(k))
                v = v_ref[:, lanes]
                v = jnp.where(mask, v, jnp.zeros_like(v))
                q = q_ref[span, lanes]
                do = do_ref[span, lanes]
                t = nt(k, q) * (SCALE * LOG2E) + bias[:, :queries]
                p = jnp.exp2(t - lse_t[head, span])
                dvs.append(jnp.where(mask, nn(p.astype(BF), do), 0.0))
                ds = (p * (nt(v, do) - delta_t[head, span])).astype(BF)
                dks.append(jnp.where(mask, nn(ds, q), 0.0))
                dq_acc[span, lanes] += tn(ds, k)
            out = pl.ds(pl.multiple_of(gi * GROUP, LANES), GROUP)
            dk_ref[:, out] = (spread(dks) * SCALE).astype(BF)
            dv_ref[:, out] = spread(dvs).astype(BF)
            return 0

        lax.fori_loop(0, groups, group, 0)

    for blocks in range(1, ahead + 2):
        pl.when(count == blocks)(functools.partial(body, blocks))

    @pl.when(j == n - 1)
    def _():
        dq_ref[...] = (dq_acc[...] * SCALE).astype(BF)


def attend_back(q, k, v, seg, mixed, d_mixed, lse):
    tokens, width = q.shape
    seqs, length = seg.shape
    n = length // BLK
    spec_k = pl.BlockSpec((BLK, width), lambda s, j, _: (s * n + j, 0))
    spec_q = pl.BlockSpec((length, width), lambda s, j, _: (s, 0))
    pairs = seqs * n * 2.5 * BLK * BLK * (width // HEAD_DIM)
    return pl.pallas_call(
        attend_back_kernel,
        grid_spec=pltpu.PrefetchScalarGridSpec(
            num_scalar_prefetch=1,
            grid=(seqs, n),
            in_specs=[
                spec_q,
                spec_q,
                spec_q,
                pl.BlockSpec((length, LANES), lambda s, j, _: (s, 0)),
                spec_k,
                spec_k,
                pl.BlockSpec((1, 1, length), lambda s, j, _: (s, 0, 0)),
            ],
            out_specs=[spec_q, spec_k, spec_k],
            scratch_shapes=[
                pltpu.VMEM((BLK, BLK + MAX_DOC), F32),
                pltpu.VMEM((length, width), F32),
                pltpu.VMEM((16, length), F32),
                pltpu.VMEM((16, length), F32),
            ],
        ),
        out_shape=[jax.ShapeDtypeStruct((tokens, width), BF)] * 3,
        compiler_params=params(2),
        cost_estimate=pl.CostEstimate(
            flops=int(pairs * 20 * WIN), bytes_accessed=16 * tokens * width, transcendentals=int(pairs)
        ),
        name="attend_back",
    )(seg, q, d_mixed, mixed, lse, k, v, seg.reshape(seqs, 1, length))


def middle_kernel(
    own, m_ref, x_ref, g_ref, w_ref, wo_ref, w1_ref, w2_ref, bo_ref, g2_ref, c2_ref, b1_ref, b2_ref,
    y_ref, dr_ref, dm_ref, gwo_ref, gw1_ref, gw2_ref, vec_ref, sq_ref,
):
    i = pl.program_id(0)

    @pl.when(i == 0)
    def _():
        for ref in (gwo_ref, gw1_ref, gw2_ref, vec_ref):
            ref[...] = jnp.zeros_like(ref)

    mixed = m_ref[...]
    cot = g_ref[...]
    attended = nn(mixed, wo_ref[...]) + bo_ref[...]
    resid = x_ref[...].astype(F32) + attended
    hat, inv = normalize(resid)
    normed = (hat * g2_ref[...] + c2_ref[...]).astype(BF)
    pre = nt(normed, w1_ref[...]) + b1_ref[...]
    cdf = 0.5 + 0.5 * lax.erf(pre * math.sqrt(0.5))
    act = (pre * cdf).astype(BF)
    slope = cdf + pre * jnp.exp(-0.5 * pre * pre) * (1.0 / math.sqrt(2.0 * math.pi))
    branch = nn(act, w2_ref[...]) + b2_ref[...]
    output = resid + branch
    y_ref[...] = output.astype(BF)
    weight = column_of(w_ref[0])
    lane = lax.broadcasted_iota(jnp.int32, (1, LANES), 1)
    sums = jnp.zeros((1, LANES), F32)
    for at, v in enumerate((attended, branch, output)):
        one = jnp.sum(weight * jnp.sum(v * v, axis=1, keepdims=True), axis=0, keepdims=True)
        sums = jnp.where(lane == at, one, sums)
    sq_ref[...] = jnp.broadcast_to(sums, sq_ref.shape[1:])[None]

    d_pre = (nt(cot, w2_ref[...]) * slope).astype(BF)
    gw2_ref[...] += tn(act[:, :own], cot)
    gw1_ref[...] += tn(d_pre[:, :own], normed)
    d_normed = nn(d_pre, w1_ref[...])
    d_hat = d_normed * g2_ref[...]
    grad = cot.astype(F32)
    d_resid = grad + inv * (
        d_hat - jnp.mean(d_hat, axis=1, keepdims=True) - hat * jnp.mean(d_hat * hat, axis=1, keepdims=True)
    )
    dr_ref[...] = d_resid
    low = d_resid.astype(BF)
    gwo_ref[...] += tn(mixed[:, :own], low)
    dm_ref[...] = nt(low, wo_ref[...]).astype(BF)
    for at, v in enumerate((grad, d_pre.astype(F32), d_normed * hat, d_normed, low.astype(F32))):
        vec_ref[at] += fold8(v)


def middle(own, mixed, x, cot, valid, wo, w1, w2, bo, g2, c2, b1, b2):
    tokens, width = x.shape
    inner, hidden = wo.shape[0], w1.shape[0]
    n = tokens // BLK
    return pl.pallas_call(
        functools.partial(middle_kernel, own),
        grid=(n,),
        in_specs=[rows(inner), rows(width), rows(width), pl.BlockSpec((1, 1, BLK), lambda i: (i, 0, 0))]
        + [whole((inner, width)), whole((hidden, width)), whole((hidden, width))]
        + [whole((1, width))] * 3
        + [whole((1, hidden)), whole((1, width))],
        out_specs=[rows(width), rows(width), rows(inner)]
        + [held((own, width))] * 3
        + [held((5, 8, width)), pl.BlockSpec((1, 8, LANES), lambda i: (i, 0, 0))],
        out_shape=[
            jax.ShapeDtypeStruct((tokens, width), BF),
            jax.ShapeDtypeStruct((tokens, width), F32),
            jax.ShapeDtypeStruct((tokens, inner), BF),
        ]
        + [jax.ShapeDtypeStruct((own, width), F32)] * 3
        + [jax.ShapeDtypeStruct((5, 8, width), F32), jax.ShapeDtypeStruct((n, 8, LANES), F32)],
        compiler_params=params(1),
        cost_estimate=pl.CostEstimate(
            flops=2 * tokens * width * (6 * width + 3 * own),
            bytes_accessed=14 * tokens * width + 6 * width * width,
            transcendentals=2 * tokens * hidden,
        ),
        name="middle",
    )(mixed, x, cot, valid.astype(F32).reshape(n, 1, BLK), wo, w1, w2, bo, g2, c2, b1, b2)


def finish_kernel(dq_ref, dk_ref, dv_ref, x_ref, dr_ref, g_ref, wq_ref, wk_ref, wv_ref, dx_ref, vec_ref):
    @pl.when(pl.program_id(0) == 0)
    def _():
        vec_ref[...] = jnp.zeros_like(vec_ref)

    d_normed = nn(dq_ref[...], wq_ref[...]) + nn(dk_ref[...], wk_ref[...]) + nn(dv_ref[...], wv_ref[...])
    hat, inv = normalize(x_ref[...].astype(F32))
    d_hat = d_normed * g_ref[...]
    dx_ref[...] = dr_ref[...] + inv * (
        d_hat - jnp.mean(d_hat, axis=1, keepdims=True) - hat * jnp.mean(d_hat * hat, axis=1, keepdims=True)
    )
    vec_ref[0] += fold8(d_normed * hat)
    vec_ref[1] += fold8(d_normed)


def finish(dq, dk, dv, x, d_resid, g1, wq, wk, wv):
    tokens, width = x.shape
    inner = wq.shape[0]
    return pl.pallas_call(
        finish_kernel,
        grid=(tokens // BLK,),
        in_specs=[rows(inner)] * 3 + [rows(width), rows(width), whole((1, width))] + [whole((inner, width))] * 3,
        out_specs=[rows(width), held((2, 8, width))],
        out_shape=[jax.ShapeDtypeStruct((tokens, width), F32), jax.ShapeDtypeStruct((2, 8, width), F32)],
        compiler_params=params(1),
        cost_estimate=pl.CostEstimate(
            flops=6 * tokens * width * inner, bytes_accessed=16 * tokens * width + 6 * width * inner, transcendentals=0
        ),
        name="finish",
    )(dq, dk, dv, x, d_resid, g1, wq, wk, wv)


def sibling(index, bit):
    return index + bit - 2 * bit * (index // bit % 2)


def gather_kernel(
    bits, chunks, count, mine_ref, local_ref, bias_ref, full_ref, biases_ref, land, sem_s, sem_r, bias_s, bias_r
):
    d, z = lax.axis_index("dp"), lax.axis_index("tensor")
    first, second = bits
    core = d % 2
    spot = d // first % 2 + 2 * (d // second % 2)
    piece = mine_ref.shape[1]
    own = local_ref.shape[1]

    def at(dp=None, tensor=None):
        return {"dp": d if dp is None else dp, "tensor": z if tensor is None else tensor}

    z_peer = [None, sibling(z, 1), sibling(z, 2), sibling(sibling(z, 1), 2)]
    x_peer, y_peer, c_peer = sibling(d, first), sibling(d, second), sibling(d, 1)
    x_spot, y_spot = sibling(spot, 1), sibling(spot, 2)
    targets = [at(tensor=t) for t in z_peer[1:]] + [at(dp=t) for t in (x_peer, y_peer, c_peer)]
    barrier = pltpu.get_barrier_semaphore()
    for target in targets:
        pl.semaphore_signal(barrier, inc=1, device_id=target, device_id_type=pl.DeviceIdType.MESH)
    pl.semaphore_wait(barrier, len(targets))

    def copy(k, kind, src, dst, target):
        return pltpu.make_async_remote_copy(
            src_ref=src,
            dst_ref=dst,
            send_sem=sem_s.at[k, kind],
            recv_sem=sem_r.at[k, kind],
            device_id=target,
            device_id_type=pl.DeviceIdType.MESH,
        )

    def slot(k, c, where, low=None, high=None):
        m, j, r0, r1 = chunks[k]
        return land.at[m, j - 1, c, where, pl.ds(r0 if low is None else low, (r1 if high is None else high) - (r0 if low is None else low))]

    def middle_row(k):
        m, j, r0, r1 = chunks[k]
        half = (r1 - r0) // 2
        return r0 + (half + 7 if k % 2 else half) // 8 * 8

    def over_z(k):
        m, j, r0, r1 = chunks[k]
        return copy(k, 0, mine_ref.at[m, pl.ds(r0, r1 - r0)], slot(k, core, spot), at(tensor=z_peer[j]))

    def over_x(k):
        return copy(k, 1, slot(k, core, spot), slot(k, core, spot), at(dp=x_peer))

    def over_y(k):
        return copy(k, 2, slot(k, core, spot), slot(k, core, spot), at(dp=y_peer))

    def on_x(k):
        part = slot(k, core, y_spot, None, middle_row(k))
        return copy(k, 3, part, part, at(dp=x_peer))

    def on_y(k):
        part = slot(k, core, x_spot, middle_row(k), None)
        return copy(k, 4, part, part, at(dp=y_peer))

    def swap(k):
        m, j, r0, r1 = chunks[k]
        part = land.at[m, j - 1, core, :, pl.ds(r0, r1 - r0)]
        return copy(k, 5, part, part, at(dp=c_peer))

    bias_copies = [
        pltpu.make_async_remote_copy(
            src_ref=bias_ref,
            dst_ref=biases_ref.at[j],
            send_sem=bias_s.at[j],
            recv_sem=bias_r.at[j],
            device_id=at(tensor=z_peer[j]),
            device_id_type=pl.DeviceIdType.MESH,
        )
        for j in (1, 2, 3)
    ]
    total = len(chunks)
    ahead = 3
    for k in range(min(ahead, total)):
        over_z(k).start()
    for one in bias_copies:
        one.start()
    biases_ref[0] = bias_ref[...]
    for m in range(count):
        full_ref[m, :own] = local_ref[m]
    done = {}
    for tick in range(total + 3):
        k = tick
        if k < total:
            over_z(k).wait_recv()
            over_x(k).start()
            over_y(k).start()
            if k + ahead < total:
                over_z(k + ahead).start()
        k = tick - 1
        if 0 <= k < total:
            over_y(k).wait_recv()
            on_x(k).start()
            over_x(k).wait_recv()
            on_y(k).start()
        k = tick - 2
        if 0 <= k < total:
            on_x(k).wait_recv()
            on_y(k).wait_recv()
            swap(k).start()
        k = tick - 3
        if 0 <= k < total:
            swap(k).wait_recv()
            m, j, r0, r1 = chunks[k]
            done[m, j] = done.get((m, j), 0) + r1 - r0
            if done[m, j] == piece:
                full_ref[m, j * own : (j + 1) * own] = land[m, j - 1].reshape(own, -1).astype(BF)
    for k in range(total):
        for make in (over_z, over_x, over_y, on_x, on_y, swap):
            make(k).wait_send()
    for one in bias_copies:
        one.wait()


def gather(shards_, bias, dp, tp, ident):
    count = len(shards_)
    own, width = shards_[0].shape
    bits = (2, 4) if dp == 8 else (2, 8)
    piece = own // 8
    local = jnp.stack(shards_)
    d = lax.axis_index("dp")
    at = 4 * (d % 2) + d // bits[0] % 2 + 2 * (d // bits[1] % 2)
    mine = lax.dynamic_index_in_dim(local.reshape(count, 8, piece, width), at, 1, keepdims=False).astype(F32)
    cut = (piece * 5 // 8) // 8 * 8
    chunks = [(m, j, *span) for m in range(count) for j in range(1, tp) for span in ((0, cut), (cut, piece))]
    total = len(chunks)
    vm = pl.BlockSpec(memory_space=pltpu.VMEM)
    return pl.pallas_call(
        functools.partial(gather_kernel, bits, chunks, count),
        in_specs=[vm] * 3,
        out_specs=[vm] * 2,
        out_shape=[
            jax.ShapeDtypeStruct((count, tp * own, width), BF),
            jax.ShapeDtypeStruct((tp,) + bias.shape, F32),
        ],
        scratch_shapes=[
            pltpu.VMEM((count, tp - 1, 2, 4, piece, width), F32),
            pltpu.SemaphoreType.DMA((total, 6)),
            pltpu.SemaphoreType.DMA((total, 6)),
            pltpu.SemaphoreType.DMA((tp,)),
            pltpu.SemaphoreType.DMA((tp,)),
        ],
        compiler_params=pltpu.CompilerParams(
            collective_id=ident, has_side_effects=True, vmem_limit_bytes=VMEM_MAX
        ),
        cost_estimate=pl.CostEstimate(flops=0, bytes_accessed=6 * count * tp * own * width, transcendentals=0),
        name="gather_weights",
    )(mine, local, bias)


def shards(dp, tp, x, g1, c1, wq, bq, wk, wv, bv, wo, bo, g2, c2, w1, b1, w2, b2, seg, valid, cot):
    tokens, width = x.shape
    seqs, length = seg.shape
    own = wq.shape[1]

    def line(t):
        return t.reshape(1, -1)

    bias = jnp.zeros((8, -(-own // LANES) * LANES), F32).at[:3, :own].set(jnp.stack([bq, bv, b1]))
    full, biases = gather([wq.T, wk.T, wv.T, wo, w1.T, w2], bias, dp, tp, 0)
    fq, fk, fv, fo, f1, f2 = (full[m] for m in range(6))
    abq, abv, ab1 = (line(biases[:, r, :own]) for r in range(3))

    normed1, q, k, v = project(x, line(g1), line(c1), fq, fk, fv, abq, abv)
    mixed, lse = attend(q, k, v, seg)
    y, d_resid, d_mixed, gwo, gw1, gw2, vec, sq = middle(
        own, mixed, x, cot, valid, fo, f1, f2, line(bo), line(g2), line(c2), ab1, line(b2)
    )
    dq, dk, dv = attend_back(q, k, v, seg, mixed, d_mixed, lse)
    mine = [t[:, :own] for t in (dq, dk, dv)]
    gq, gk, gv = (tn(t, normed1) for t in mine)
    gbq, gbv = (jnp.sum(t.astype(F32), axis=0) for t in (mine[0], mine[2]))
    grad_input, last = finish(dq, dk, dv, x, d_resid, line(g1), fq, fk, fv)

    weight = valid.astype(F32)
    counted = jnp.maximum(jnp.sum(weight, axis=1), 1.0) * width
    stat = jnp.sum(sq[:, 0, :3].reshape(seqs, length // BLK, 3), axis=1)
    rms = jnp.sqrt(stat / counted[:, None])

    vec = jnp.sum(vec, axis=1)
    last = jnp.sum(last, axis=1)
    big = lax.psum((gwo, gw1, gw2), "dp")
    mats = lax.psum((gq, gk, gv), "dp")
    gb2, gb1, gg2, gc2, gbo, gg1, gc1, gbq, gbv = lax.psum(
        (vec[0], vec[1, :own], vec[2], vec[3], vec[4], last[0], last[1], gbq, gbv), "dp"
    )
    gwo, gw1, gw2 = big
    gq, gk, gv = mats
    return (
        y, grad_input, gg1, gc1, gq.T, gbq, gk.T, gv.T, gbv, gwo, gbo, gg2, gc2, gw1.T, gb1, gw2, gb2, rms,
    )


def solution(mesh):
    dp, tp = mesh.shape["dp"], mesh.shape["tensor"]
    tok, col, row, vec, rep = P("dp", None), P(None, "tensor"), P("tensor", None), P("tensor"), P()
    return jax.shard_map(
        functools.partial(shards, dp, tp),
        mesh=mesh,
        in_specs=(tok, rep, rep, col, vec, col, col, vec, row, rep, rep, rep, col, vec, row, rep, tok, tok, tok),
        out_specs=(tok, tok, rep, rep, col, vec, col, col, vec, row, rep, rep, rep, col, vec, row, rep, tok),
        check_vma=False,
    )
```

```python
import functools
import math

import jax
import jax.numpy as jnp
from jax import lax
from jax.experimental import pallas as pl
from jax.experimental.pallas import tpu as pltpu
from jax.sharding import PartitionSpec as P

HEAD_DIM = 160
MAX_DOC = 512
EPS = 1e-05
NEG = -1e30
BLK = 256
WIN = 256
LANES = 128
SCALE = 1.0 / math.sqrt(HEAD_DIM)
LOG2E = 1.0 / math.log(2.0)
BF = jnp.bfloat16
F32 = jnp.float32
VMEM_MAX = 60 << 20


def nn(a, b):
    return lax.dot_general(a, b, (((1,), (0,)), ((), ())), preferred_element_type=F32)


def nt(a, b):
    return lax.dot_general(a, b, (((1,), (1,)), ((), ())), preferred_element_type=F32)


def tn(a, b):
    return lax.dot_general(a, b, (((0,), (0,)), ((), ())), preferred_element_type=F32)


def whole(shape):
    return pl.BlockSpec(shape, lambda *_: (0,) * len(shape), pipeline_mode=pl.Buffered(1))


def held(shape):
    return pl.BlockSpec(shape, lambda *_: (0,) * len(shape))


def rows(width):
    return pl.BlockSpec((BLK, width), lambda i: (i, 0))


def column_of(row):
    n = row.shape[1]
    eye = lax.broadcasted_iota(jnp.int32, (n, n), 0) == lax.broadcasted_iota(jnp.int32, (n, n), 1)
    return jnp.sum(jnp.where(eye, row, jnp.zeros_like(row)), axis=1, keepdims=True)


def fold8(t):
    return jnp.sum(t.reshape(t.shape[0] // 8, 8, t.shape[1]), axis=0)


def params(grid, vmem=VMEM_MAX):
    return pltpu.CompilerParams(dimension_semantics=("arbitrary",) * grid, vmem_limit_bytes=vmem)


def hosting(grid, ident):
    return pltpu.CompilerParams(
        dimension_semantics=("arbitrary",) * grid,
        vmem_limit_bytes=VMEM_MAX,
        collective_id=ident,
        has_side_effects=True,
    )


def sibling(index, bit):
    return index + bit - 2 * bit * (index // bit % 2)


class Place:
    def __init__(self, bits):
        self.d, self.z = lax.axis_index("dp"), lax.axis_index("tensor")
        self.core = self.d % 2
        self.a, self.b = (self.d // bit % 2 for bit in bits)
        self.spot = self.a + 2 * self.b
        self.on_core = {"dp": sibling(self.d, 1), "tensor": self.z}
        self.on_a, self.on_b = ({"dp": sibling(self.d, bit), "tensor": self.z} for bit in bits)
        peers = (None, sibling(self.z, 1), sibling(self.z, 2), sibling(sibling(self.z, 1), 2))
        self.on_z = [None] + [{"dp": self.d, "tensor": peer} for peer in peers[1:]]

    def plane(self):
        return [{"dp": (self.d + step) % 8, "tensor": self.z} for step in range(1, 8)]


def greet(targets):
    barrier = pltpu.get_barrier_semaphore()
    for target in targets:
        pl.semaphore_signal(barrier, inc=1, device_id=target, device_id_type=pl.DeviceIdType.MESH)
    pl.semaphore_wait(barrier, len(targets))


def send(src, dst, sems, at, target):
    return pltpu.make_async_remote_copy(
        src_ref=src,
        dst_ref=dst,
        send_sem=sems[0].at[at],
        recv_sem=sems[1].at[at],
        device_id=target,
        device_id_type=pl.DeviceIdType.MESH,
    )


def bits_of(dp):
    return (2, 4) if dp == 8 else (2, 8)


def chunks_of(count, tp, piece):
    cut = (piece * 5 // 8) // 8 * 8
    return [(m, j, *span) for m in range(count) for j in range(1, tp) for span in ((0, cut), (cut, piece))]


AHEAD = 3


class Gather:
    def __init__(self, place, chunks, mine, local, full, land, sems):
        self.place, self.chunks, self.mine, self.local, self.full, self.land, self.sems = (
            place, chunks, mine, local, full, land, sems
        )
        self.ticks = len(chunks) + 3
        self.got = {}

    def slot(self, k, where, low=None, high=None):
        m, j, r0, r1 = self.chunks[k]
        low, high = (r0 if low is None else low), (r1 if high is None else high)
        return self.land.at[m, j - 1, self.place.core, where, pl.ds(low, high - low)]

    def middle(self, k):
        _, _, r0, r1 = self.chunks[k]
        half = (r1 - r0) // 2
        return r0 + (half + 7 if k % 2 else half) // 8 * 8

    def over_z(self, k):
        m, j, r0, r1 = self.chunks[k]
        here = self.slot(k, self.place.spot)
        return send(self.mine.at[m, pl.ds(r0, r1 - r0)], here, self.sems, (k, 0), self.place.on_z[j])

    def over_a(self, k):
        here = self.slot(k, self.place.spot)
        return send(here, here, self.sems, (k, 1), self.place.on_a)

    def over_b(self, k):
        here = self.slot(k, self.place.spot)
        return send(here, here, self.sems, (k, 2), self.place.on_b)

    def on_a(self, k):
        part = self.slot(k, sibling(self.place.spot, 2), None, self.middle(k))
        return send(part, part, self.sems, (k, 3), self.place.on_a)

    def on_b(self, k):
        part = self.slot(k, sibling(self.place.spot, 1), self.middle(k), None)
        return send(part, part, self.sems, (k, 4), self.place.on_b)

    def swap(self, k):
        m, j, r0, r1 = self.chunks[k]
        part = self.land.at[m, j - 1, self.place.core, :, pl.ds(r0, r1 - r0)]
        return send(part, part, self.sems, (k, 5), self.place.on_core)

    def begin(self):
        place = self.place
        greet(place.on_z[1:] + [place.on_a, place.on_b, place.on_core])
        for k in range(min(AHEAD, len(self.chunks))):
            self.over_z(k).start()
        for full, local in zip(self.full, self.local):
            full[: local.shape[0]] = local[...]

    def tick(self, t):
        total = len(self.chunks)
        if 0 <= t < total:
            self.over_z(t).wait_recv()
            self.over_a(t).start()
            self.over_b(t).start()
            if t + AHEAD < total:
                self.over_z(t + AHEAD).start()
        k = t - 1
        if 0 <= k < total:
            self.over_b(k).wait_recv()
            self.on_a(k).start()
            self.over_a(k).wait_recv()
            self.on_b(k).start()
        k = t - 2
        if 0 <= k < total:
            self.on_a(k).wait_recv()
            self.on_b(k).wait_recv()
            self.swap(k).start()
        k = t - 3
        if 0 <= k < total:
            self.swap(k).wait_recv()
            m, j, r0, r1 = self.chunks[k]
            piece = self.land.shape[4]
            self.got[m, j] = self.got.get((m, j), 0) + r1 - r0
            if self.got[m, j] == piece:
                own = 8 * piece
                self.full[m][j * own : (j + 1) * own] = self.land[m, j - 1].reshape(own, -1).astype(BF)

    def end(self):
        for k in range(len(self.chunks)):
            for make in (self.over_z, self.over_a, self.over_b, self.on_a, self.on_b, self.swap):
                make(k).wait_send()


def gather_scratch(count, tp, piece, width):
    total = len(chunks_of(count, tp, piece))
    return [
        pltpu.VMEM((count, tp - 1, 2, 4, piece, width), F32),
        pltpu.SemaphoreType.DMA((total, 6)),
        pltpu.SemaphoreType.DMA((total, 6)),
    ]


class Reduce:
    def __init__(self, place, part, scratch, publish):
        self.place, self.part, self.publish = place, part, publish
        self.out, self.half, self.from_core, self.first, self.second, *self.sems = scratch
        self.count, self.own, self.width = part.shape
        self.ticks = self.count + 6

    def greet(self):
        return [self.place.on_a, self.place.on_b, self.place.on_core]

    def ways(self):
        place = self.place
        return (
            (0, place.a, place.on_a, place.b, place.on_b),
            (1, place.b, place.on_b, place.a, place.on_a),
        )

    def rows_of(self, size, index, count):
        return pl.ds(pl.multiple_of(size * index, 8), count)

    def out_rows(self, way, bit):
        quarter = self.own // 8
        return self.rows_of(quarter, 4 * self.place.core + 2 * way + bit, quarter)

    def copies(self, m, stage):
        place, own = self.place, self.own
        quarter, lanes = own // 8, self.width // 2
        if stage == 0:
            src = self.part.at[m, self.rows_of(own // 2, 1 - place.core, own // 2)]
            return [send(src, self.from_core.at[m], self.sems, (m, 0, 0), place.on_core)]
        if stage == 5:
            rows_ = self.out.at[m, self.rows_of(own // 2, place.core, own // 2)]
            return [send(rows_, rows_, self.sems, (m, 5, 0), place.on_core)]
        made = []
        for way, bit, peer, bit2, peer2 in self.ways():
            columns = pl.ds(pl.multiple_of(lanes * bit2, LANES), lanes)
            others = pl.ds(pl.multiple_of(lanes * (1 - bit2), LANES), lanes)
            if stage == 1:
                src, dst, to = self.half.at[m, self.rows_of(quarter, 2 * way + 1 - bit, quarter)], self.first.at[m, way], peer
            elif stage == 2:
                src = self.half.at[m, self.rows_of(quarter, 2 * way + bit, quarter), others]
                dst, to = self.second.at[m, way], peer2
            elif stage == 3:
                src = dst = self.out.at[m, self.out_rows(way, bit), columns]
                to = peer2
            else:
                src = dst = self.out.at[m, self.out_rows(way, bit)]
                to = peer
            made.append(send(src, dst, self.sems, (m, stage, way), to))
        return made

    def step(self, m, stage):
        if stage >= 1:
            for one in self.copies(m, stage - 1):
                one.wait_recv()
        place, own = self.place, self.own
        quarter, lanes = own // 8, self.width // 2
        if stage == 1:
            self.half[m] = self.part[m, self.rows_of(own // 2, place.core, own // 2)] + self.from_core[m]
        for way, bit, _, bit2, _ in self.ways():
            mine = self.rows_of(quarter, 2 * way + bit, quarter)
            columns = pl.ds(pl.multiple_of(lanes * bit2, LANES), lanes)
            if stage == 2:
                self.half[m, mine] = self.half[m, mine] + self.first[m, way]
            if stage == 3:
                self.out[m, self.out_rows(way, bit), columns] = self.half[m, mine, columns] + self.second[m, way]
        if stage < 6:
            for one in self.copies(m, stage):
                one.start()
        else:
            self.publish(m, self.out[m])

    def tick(self, t):
        for m in range(self.count):
            if 0 <= t - m <= 6:
                self.step(m, t - m)

    def end(self):
        for m in range(self.count):
            for stage in range(6):
                for one in self.copies(m, stage):
                    one.wait_send()


def reduce_scratch(count, own, width):
    return [
        pltpu.VMEM((count, own, width), F32),
        pltpu.VMEM((count, own // 2, width), F32),
        pltpu.VMEM((count, own // 2, width), F32),
        pltpu.VMEM((count, 2, own // 8, width), F32),
        pltpu.VMEM((count, 2, own // 8, width // 2), F32),
        pltpu.SemaphoreType.DMA((count, 6, 2)),
        pltpu.SemaphoreType.DMA((count, 6, 2)),
    ]


def host(work, step, steps, spread_over=None):
    spread_over = spread_over or steps
    for t in range(work.ticks):
        pl.when(step == t * spread_over // work.ticks)(functools.partial(work.tick, t))
    pl.when(step == steps - 1)(work.end)


def gather_kernel(bits, chunks, count, mine, *refs):
    local, bias_ref = refs[:count], refs[count]
    full, biases_ref, land = refs[count + 1 : 2 * count + 1], refs[2 * count + 1], refs[2 * count + 2]
    sems, bias_sems = refs[2 * count + 3 : 2 * count + 5], refs[2 * count + 5 :]
    place = Place(bits)
    work = Gather(place, chunks, mine, local, full, land, sems)
    work.begin()
    vectors = [send(bias_ref, biases_ref.at[j], bias_sems, j, place.on_z[j]) for j in range(1, len(place.on_z))]
    for one in vectors:
        one.start()
    biases_ref[0] = bias_ref[...]
    for t in range(work.ticks):
        work.tick(t)
    work.end()
    for one in vectors:
        one.wait()


def slices_of(shards_, bits):
    own, width = shards_[0].shape
    piece = own // 8
    d = lax.axis_index("dp")
    at = 4 * (d % 2) + d // bits[0] % 2 + 2 * (d // bits[1] % 2)
    cut = [lax.dynamic_index_in_dim(t.reshape(8, piece, width), at, 0, keepdims=False) for t in shards_]
    return [t.astype(F32) for t in cut]


def gather(shards_, bias, dp, tp):
    count = len(shards_)
    own, width = shards_[0].shape
    bits = bits_of(dp)
    piece = own // 8
    mine = jnp.stack(slices_of(shards_, bits))
    vm = pl.BlockSpec(memory_space=pltpu.VMEM)
    return pl.pallas_call(
        functools.partial(gather_kernel, bits, chunks_of(count, tp, piece), count),
        in_specs=[vm] * (count + 2),
        out_specs=[vm] * (count + 1),
        out_shape=[jax.ShapeDtypeStruct((tp * own, width), BF)] * count + [jax.ShapeDtypeStruct((tp,) + bias.shape, F32)],
        scratch_shapes=gather_scratch(count, tp, piece, width)
        + [pltpu.SemaphoreType.DMA((tp,)), pltpu.SemaphoreType.DMA((tp,))],
        compiler_params=pltpu.CompilerParams(collective_id=0, has_side_effects=True, vmem_limit_bytes=VMEM_MAX),
        cost_estimate=pl.CostEstimate(flops=0, bytes_accessed=6 * count * tp * own * width, transcendentals=0),
        name="gather_weights",
    )(mine, *shards_, bias)


def normalize(v):
    center = v - jnp.mean(v, axis=-1, keepdims=True)
    inv = lax.rsqrt(jnp.mean(center * center, axis=-1, keepdims=True) + EPS)
    return center * inv, inv


def project_kernel(
    bits, steps, chunks, x_ref, g_ref, c_ref, wq_ref, wk_ref, wv_ref, bq_ref, bv_ref, mine, *refs
):
    count = mine.shape[0]
    local, refs = refs[:count], refs[count:]
    n_ref, q_ref, k_ref, v_ref, *full = refs[: 4 + count]
    land, *sems = refs[4 + count :]
    step = pl.program_id(0)
    work = Gather(Place(bits), chunks, mine, local, full, land, sems)
    pl.when(step == 0)(work.begin)
    hat, _ = normalize(x_ref[...].astype(F32))
    normed = (hat * g_ref[...] + c_ref[...]).astype(BF)
    n_ref[...] = normed
    q_ref[...] = (nt(normed, wq_ref[...]) + bq_ref[...]).astype(BF)
    k_ref[...] = nt(normed, wk_ref[...]).astype(BF)
    v_ref[...] = (nt(normed, wv_ref[...]) + bv_ref[...]).astype(BF)
    host(work, step, steps)


def project(x, g1, c1, wq, wk, wv, bq, bv, shards_, dp, tp):
    tokens, width = x.shape
    out = wq.shape[0]
    count, own = len(shards_), shards_[0].shape[0]
    bits, piece, steps = bits_of(dp), own // 8, tokens // BLK
    mine = jnp.stack(slices_of(shards_, bits))
    return pl.pallas_call(
        functools.partial(project_kernel, bits, steps, chunks_of(count, tp, piece)),
        grid=(steps,),
        in_specs=[rows(width), whole((1, width)), whole((1, width))]
        + [whole((out, width))] * 3
        + [whole((1, out))] * 2
        + [whole(mine.shape)]
        + [whole((own, width))] * count,
        out_specs=[rows(width)] + [rows(out)] * 3 + [held((tp * own, width))] * count,
        out_shape=[jax.ShapeDtypeStruct((tokens, width), BF)]
        + [jax.ShapeDtypeStruct((tokens, out), BF)] * 3
        + [jax.ShapeDtypeStruct((tp * own, width), BF)] * count,
        scratch_shapes=gather_scratch(count, tp, piece, width),
        compiler_params=hosting(1, 1),
        cost_estimate=pl.CostEstimate(
            flops=6 * tokens * width * out, bytes_accessed=2 * (tokens * (2 * width + 3 * out) + 3 * width * out), transcendentals=0
        ),
        name="project",
    )(x, g1, c1, wq, wk, wv, bq, bv, mine, *shards_)


HEADS_IN_GROUP = 4
GROUP = HEADS_IN_GROUP * HEAD_DIM


def window_of(head):
    low = head * HEAD_DIM
    start = low // LANES * LANES
    return start, low - start


def lane_mask(offset):
    lane = lax.broadcasted_iota(jnp.int32, (1, WIN), 1)
    return (lane >= offset) & (lane < offset + HEAD_DIM)


def spread(parts):
    tiles = [None] * (GROUP // LANES)
    for head, part in enumerate(parts):
        first = window_of(head)[0] // LANES
        for half in range(WIN // LANES):
            piece = part[:, half * LANES : (half + 1) * LANES]
            at = first + half
            tiles[at] = piece if tiles[at] is None else tiles[at] + piece
    return jnp.concatenate(tiles, axis=1)


def attend_kernel(bits, steps, chunks, q_ref, k_ref, v_ref, seg_ref, mine, *refs):
    kinds = mine.shape[0]
    local, refs = refs[:kinds], refs[kinds:]
    o_ref, lse_ref, *full = refs[: 2 + kinds]
    bias, land, *sems = refs[2 + kinds :]
    s, i = pl.program_id(0), pl.program_id(1)
    groups = q_ref.shape[1] // GROUP
    back = MAX_DOC // BLK
    count = jnp.minimum(i, back) + 1
    step = s * pl.num_programs(1) + i
    work = Gather(Place(bits), chunks, mine, local, full, land, sems)
    pl.when(step == 0)(work.begin)
    seg_col = column_of(seg_ref[0, :, pl.ds(pl.multiple_of(i * BLK, BLK), BLK)])

    def body(blocks):
        keys = blocks * BLK
        start = pl.multiple_of((i + 1 - blocks) * BLK, BLK)
        row = i * BLK + lax.broadcasted_iota(jnp.int32, (BLK, keys), 0)
        col = start + lax.broadcasted_iota(jnp.int32, (BLK, keys), 1)
        allowed = (row >= col) & (seg_col == seg_ref[0, :, pl.ds(start, keys)])
        bias[:, :keys] = jnp.where(allowed, 0.0, NEG)

        def group(gi, _):
            parts = []
            lse = lse_ref[...]
            head_lane = lax.broadcasted_iota(jnp.int32, (1, LANES), 1)
            for h in range(HEADS_IN_GROUP):
                at, off = window_of(h)
                lanes = pl.ds(pl.multiple_of(gi * GROUP + at, LANES), WIN)
                mask = lane_mask(off)
                q = q_ref[:, lanes]
                q = jnp.where(mask, q, jnp.zeros_like(q))
                t = nt(q, k_ref[pl.ds(start, keys), lanes]) * (SCALE * LOG2E) + bias[:, :keys]
                top = jnp.max(t, axis=1, keepdims=True)
                p = jnp.exp2(t - top)
                total = jnp.sum(p, axis=1, keepdims=True)
                o = nn(p.astype(BF), v_ref[pl.ds(start, keys), lanes])
                parts.append(jnp.where(mask, o * (1.0 / total), 0.0))
                lse = jnp.where(head_lane == gi * HEADS_IN_GROUP + h, top + jnp.log2(total), lse)
            lse_ref[...] = lse
            o_ref[:, pl.ds(pl.multiple_of(gi * GROUP, LANES), GROUP)] = spread(parts).astype(BF)
            return 0

        lax.fori_loop(0, groups, group, 0)

    lse_ref[...] = jnp.zeros_like(lse_ref)
    for blocks in range(1, back + 2):
        pl.when(count == blocks)(functools.partial(body, blocks))
    host(work, step, steps)


def attend(q, k, v, seg, shards_, dp, tp):
    tokens, width = q.shape
    seqs, length = seg.shape
    n = length // BLK
    count, own = len(shards_), shards_[0].shape[0]
    bits, piece = bits_of(dp), own // 8
    mine = jnp.stack(slices_of(shards_, bits))
    spec_q = pl.BlockSpec((BLK, width), lambda s, i: (s * n + i, 0))
    spec_k = pl.BlockSpec((length, width), lambda s, i: (s, 0))
    pairs = seqs * n * 2.5 * BLK * BLK * (width // HEAD_DIM)
    return pl.pallas_call(
        functools.partial(attend_kernel, bits, seqs * n, chunks_of(count, tp, piece)),
        grid=(seqs, n),
        in_specs=[spec_q, spec_k, spec_k, pl.BlockSpec((1, 1, length), lambda s, i: (s, 0, 0)), whole(mine.shape)]
        + [whole((own, shards_[0].shape[1]))] * count,
        out_specs=[spec_q, pl.BlockSpec((BLK, LANES), lambda s, i: (s * n + i, 0))]
        + [held((tp * own, shards_[0].shape[1]))] * count,
        scratch_shapes=[pltpu.VMEM((BLK, BLK + MAX_DOC), F32)]
        + gather_scratch(count, tp, piece, shards_[0].shape[1]),
        out_shape=[jax.ShapeDtypeStruct((tokens, width), BF), jax.ShapeDtypeStruct((tokens, LANES), F32)]
        + [jax.ShapeDtypeStruct((tp * own, shards_[0].shape[1]), BF)] * count,
        compiler_params=hosting(2, 2),
        cost_estimate=pl.CostEstimate(
            flops=int(pairs * 8 * WIN), bytes_accessed=8 * tokens * width, transcendentals=int(pairs)
        ),
        name="attend",
    )(q, k, v, seg.reshape(seqs, 1, length), mine, *shards_)


def attend_back_kernel(
    steps, bits, q_ref, do_ref, o_ref, lse_ref, k_ref, v_ref, seg_ref, part_ref, dq_ref, dk_ref, dv_ref, go_ref, g1_ref, g2_ref,
    bias, dq_acc, lse_t, delta_t, *reduce_refs,
):
    s, j = pl.program_id(0), pl.program_id(1)
    n = pl.num_programs(1)
    length, width = q_ref.shape
    groups = width // GROUP
    ahead = MAX_DOC // BLK

    def publish(m, total):
        (go_ref, g1_ref, g2_ref)[m][...] = total.T if m == 1 else total

    if bits is not None:
        work = Reduce(Place(bits), part_ref, reduce_refs, publish)

    @pl.when(j == 0)
    def _():
        dq_acc[...] = jnp.zeros_like(dq_acc)
        head = lax.broadcasted_iota(jnp.int32, (16, width), 0)
        lane = lax.broadcasted_iota(jnp.int32, (16, width), 1)
        pick = jnp.where((lane >= head * HEAD_DIM) & (lane < (head + 1) * HEAD_DIM), 1.0, 0.0).astype(BF)
        for b in range(length // BLK):
            at = slice(b * BLK, (b + 1) * BLK)
            lse_t[:, at] = lse_ref[at, :].T[:16, :]
            prod = do_ref[at, :].astype(F32) * o_ref[at, :].astype(F32)
            high = prod.astype(BF)
            rest = (prod - high.astype(F32)).astype(BF)
            delta_t[:, at] = nt(pick, high) + nt(pick, rest)

    count = jnp.minimum(n - j, ahead + 1)
    start = pl.multiple_of(j * BLK, BLK)
    seg_col = column_of(seg_ref[0, :, pl.ds(start, BLK)])

    def body(blocks):
        queries = blocks * BLK
        span = pl.ds(start, queries)
        row = lax.broadcasted_iota(jnp.int32, (BLK, queries), 0)
        col = lax.broadcasted_iota(jnp.int32, (BLK, queries), 1)
        allowed = (row <= col) & (seg_col == seg_ref[0, :, span])
        bias[:, :queries] = jnp.where(allowed, 0.0, NEG)

        def group(gi, _):
            dks, dvs = [], []
            for h in range(HEADS_IN_GROUP):
                at, off = window_of(h)
                lanes = pl.ds(pl.multiple_of(gi * GROUP + at, LANES), WIN)
                mask = lane_mask(off)
                head = pl.ds(gi * HEADS_IN_GROUP + h, 1)
                k = k_ref[:, lanes]
                k = jnp.where(mask, k, jnp.zeros_like(k))
                v = v_ref[:, lanes]
                v = jnp.where(mask, v, jnp.zeros_like(v))
                q = q_ref[span, lanes]
                do = do_ref[span, lanes]
                t = nt(k, q) * (SCALE * LOG2E) + bias[:, :queries]
                p = jnp.exp2(t - lse_t[head, span])
                dvs.append(jnp.where(mask, nn(p.astype(BF), do), 0.0))
                ds = (p * (nt(v, do) - delta_t[head, span])).astype(BF)
                dks.append(jnp.where(mask, nn(ds, q), 0.0))
                dq_acc[span, lanes] += tn(ds, k)
            out = pl.ds(pl.multiple_of(gi * GROUP, LANES), GROUP)
            dk_ref[:, out] = (spread(dks) * SCALE).astype(BF)
            dv_ref[:, out] = spread(dvs).astype(BF)
            return 0

        lax.fori_loop(0, groups, group, 0)

    step = s * n + j
    if bits is not None:

        @pl.when(step == 0)
        def _():
            greet(work.greet())
            work.tick(0)

    for blocks in range(1, ahead + 2):
        pl.when(count == blocks)(functools.partial(body, blocks))

    if bits is not None:
        for t in range(1, work.ticks):
            pl.when(step == min(t - 1, steps - 1))(functools.partial(work.tick, t))
        pl.when(step == steps - 1)(work.end)
    else:
        for m in range(3):
            publish(m, part_ref[m])

    @pl.when(j == n - 1)
    def _():
        dq_ref[...] = (dq_acc[...] * SCALE).astype(BF)


def attend_back(q, k, v, seg, mixed, d_mixed, lse, parts, bits):
    tokens, width = q.shape
    seqs, length = seg.shape
    own, model = parts.shape[1:]
    n = length // BLK
    spec_k = pl.BlockSpec((BLK, width), lambda s, j: (s * n + j, 0))
    spec_q = pl.BlockSpec((length, width), lambda s, j: (s, 0))
    pairs = seqs * n * 2.5 * BLK * BLK * (width // HEAD_DIM)
    hosted = bits is not None
    turned = [(own, model), (model, own), (own, model)]
    return pl.pallas_call(
        functools.partial(attend_back_kernel, seqs * n, bits),
        grid=(seqs, n),
        in_specs=[
            spec_q,
            spec_q,
            spec_q,
            pl.BlockSpec((length, LANES), lambda s, j: (s, 0)),
            spec_k,
            spec_k,
            pl.BlockSpec((1, 1, length), lambda s, j: (s, 0, 0)),
            whole(parts.shape),
        ],
        out_specs=[spec_q, spec_k, spec_k] + [held(t) for t in turned],
        scratch_shapes=[
            pltpu.VMEM((BLK, BLK + MAX_DOC), F32),
            pltpu.VMEM((length, width), F32),
            pltpu.VMEM((16, length), F32),
            pltpu.VMEM((16, length), F32),
        ]
        + (reduce_scratch(*parts.shape) if hosted else []),
        out_shape=[jax.ShapeDtypeStruct((tokens, width), BF)] * 3 + [jax.ShapeDtypeStruct(t, F32) for t in turned],
        compiler_params=hosting(2, 3) if hosted else params(2),
        cost_estimate=pl.CostEstimate(
            flops=int(pairs * 20 * WIN), bytes_accessed=16 * tokens * width, transcendentals=int(pairs)
        ),
        name="attend_back",
    )(q, d_mixed, mixed, lse, k, v, seg.reshape(seqs, 1, length), parts)


OWN_ROW = 6


def middle_kernel(
    own, m_ref, x_ref, g_ref, w_ref, wo_ref, w1_ref, w2_ref, bo_ref, g2_ref, c2_ref, b1_ref, b2_ref,
    y_ref, dr_ref, dm_ref, part_ref, small_ref, sq_ref, vec,
):
    i = pl.program_id(0)

    @pl.when(i == 0)
    def _():
        part_ref[...] = jnp.zeros_like(part_ref)
        vec[...] = jnp.zeros_like(vec)

    mixed = m_ref[...]
    cot = g_ref[...]
    attended = nn(mixed, wo_ref[...]) + bo_ref[...]
    resid = x_ref[...].astype(F32) + attended
    hat, inv = normalize(resid)
    normed = (hat * g2_ref[...] + c2_ref[...]).astype(BF)
    pre = nt(normed, w1_ref[...]) + b1_ref[...]
    cdf = 0.5 + 0.5 * lax.erf(pre * math.sqrt(0.5))
    act = (pre * cdf).astype(BF)
    slope = cdf + pre * jnp.exp(-0.5 * pre * pre) * (1.0 / math.sqrt(2.0 * math.pi))
    branch = nn(act, w2_ref[...]) + b2_ref[...]
    output = resid + branch
    y_ref[...] = output.astype(BF)
    weight = column_of(w_ref[0])
    lane = lax.broadcasted_iota(jnp.int32, (1, LANES), 1)
    sums = jnp.zeros((1, LANES), F32)
    for at, v in enumerate((attended, branch, output)):
        one = jnp.sum(weight * jnp.sum(v * v, axis=1, keepdims=True), axis=0, keepdims=True)
        sums = jnp.where(lane == at, one, sums)
    sq_ref[...] = jnp.broadcast_to(sums, sq_ref.shape[1:])[None]

    d_pre = (nt(cot, w2_ref[...]) * slope).astype(BF)
    part_ref[2] += tn(act[:, :own], cot)
    part_ref[1] += tn(d_pre[:, :own], normed)
    d_normed = nn(d_pre, w1_ref[...])
    d_hat = d_normed * g2_ref[...]
    grad = cot.astype(F32)
    d_resid = grad + inv * (
        d_hat - jnp.mean(d_hat, axis=1, keepdims=True) - hat * jnp.mean(d_hat * hat, axis=1, keepdims=True)
    )
    dr_ref[...] = d_resid
    low = d_resid.astype(BF)
    part_ref[0] += tn(mixed[:, :own], low)
    dm_ref[...] = nt(low, wo_ref[...]).astype(BF)
    for at, v in enumerate((grad, d_normed * hat, d_normed, low.astype(F32), d_pre.astype(F32))):
        vec[at] += fold8(v)

    @pl.when(i == pl.num_programs(0) - 1)
    def _():
        small_ref[...] = jnp.zeros_like(small_ref)
        for at, row in enumerate((0, 1, 2, 3, OWN_ROW)):
            small_ref[row : row + 1] = jnp.sum(vec[at], axis=0, keepdims=True)


def middle(own, mixed, x, cot, valid, wo, w1, w2, bo, g2, c2, b1, b2):
    tokens, width = x.shape
    inner, hidden = wo.shape[0], w1.shape[0]
    n = tokens // BLK
    return pl.pallas_call(
        functools.partial(middle_kernel, own),
        grid=(n,),
        in_specs=[rows(inner), rows(width), rows(width), pl.BlockSpec((1, 1, BLK), lambda i: (i, 0, 0))]
        + [whole((inner, width)), whole((hidden, width)), whole((hidden, width))]
        + [whole((1, width))] * 3
        + [whole((1, hidden)), whole((1, width))],
        out_specs=[
            rows(width),
            rows(width),
            rows(inner),
            held((3, own, width)),
            held((8, width)),
            pl.BlockSpec((1, 8, LANES), lambda i: (i, 0, 0)),
        ],
        out_shape=[
            jax.ShapeDtypeStruct((tokens, width), BF),
            jax.ShapeDtypeStruct((tokens, width), F32),
            jax.ShapeDtypeStruct((tokens, inner), BF),
            jax.ShapeDtypeStruct((3, own, width), F32),
            jax.ShapeDtypeStruct((8, width), F32),
            jax.ShapeDtypeStruct((n, 8, LANES), F32),
        ],
        scratch_shapes=[pltpu.VMEM((5, 8, width), F32)],
        compiler_params=params(1),
        cost_estimate=pl.CostEstimate(
            flops=2 * tokens * width * (6 * width + 3 * own),
            bytes_accessed=14 * tokens * width + 6 * width * width,
            transcendentals=2 * tokens * hidden,
        ),
        name="middle",
    )(mixed, x, cot, valid.astype(F32).reshape(n, 1, BLK), wo, w1, w2, bo, g2, c2, b1, b2)


def finish_kernel(
    bits, own, steps, dq_ref, dk_ref, dv_ref, x_ref, dr_ref, g_ref, wq_ref, wk_ref, wv_ref, mq_ref, mk_ref, mv_ref, n_ref, in_ref,
    dx_ref, gq_ref, gk_ref, gv_ref, small_ref, vec, part, *refs,
):
    step = pl.program_id(0)
    grads = (mq_ref, mk_ref, mv_ref)
    count = len(grads)
    half = part.shape[2] // 2

    def publish(m, total):
        (gq_ref, gk_ref, gv_ref)[m][...] = total.T

    if bits is not None:
        place = Place(bits)
        work = Reduce(place, part, refs[:-3], publish)
        box, *sems = refs[-3:]

    @pl.when(step == 0)
    def _():
        vec[...] = jnp.zeros_like(vec)
        small_ref[...] = in_ref[...]
        if bits is not None:
            greet(place.plane())

    def weight_grad(m):
        mine = grads[m][:, :own]
        part[m] = tn(mine, n_ref[...])
        if m != 1:
            at = 0 if m == 0 else half
            small_ref[OWN_ROW + 1 : OWN_ROW + 2, at : at + own] = jnp.sum(mine.astype(F32), axis=0, keepdims=True)

    for m in range(count):
        pl.when(step == m)(functools.partial(weight_grad, m))

    @pl.when(step >= count)
    def _():
        d_normed = nn(dq_ref[...], wq_ref[...]) + nn(dk_ref[...], wk_ref[...]) + nn(dv_ref[...], wv_ref[...])
        hat, inv = normalize(x_ref[...].astype(F32))
        d_hat = d_normed * g_ref[...]
        dx_ref[...] = dr_ref[...] + inv * (
            d_hat - jnp.mean(d_hat, axis=1, keepdims=True) - hat * jnp.mean(d_hat * hat, axis=1, keepdims=True)
        )
        vec[0] += fold8(d_normed * hat)
        vec[1] += fold8(d_normed)

    if bits is not None:
        for t in range(work.ticks):
            pl.when(step == min(t, steps - 1))(functools.partial(work.tick, t))

    @pl.when(step == steps - 1)
    def _():
        for at in range(2):
            small_ref[4 + at : 5 + at] = jnp.sum(vec[at], axis=0, keepdims=True)
        if bits is None:
            for m in range(count):
                publish(m, part[m])
        else:
            copies = [send(small_ref, box.at[place.d], sems, i, peer) for i, peer in enumerate(place.plane())]
            for one in copies:
                one.start()
            box[place.d] = small_ref[...]
            for one in copies:
                one.wait_recv()
            for one in copies:
                one.wait_send()
            total = box[0]
            for i in range(1, 8):
                total = total + box[i]
            small_ref[...] = total
            work.end()


def finish(dq, dk, dv, x, d_resid, g1, wq, wk, wv, normed1, small, own, bits):
    tokens, width = x.shape
    inner = wq.shape[0]
    hosted = bits is not None
    count = 3
    pad = -(-own // LANES) * LANES
    mine = pl.BlockSpec((tokens, pad), lambda i: (0, 0), pipeline_mode=pl.Buffered(1))

    def late(size):
        return pl.BlockSpec((BLK, size), lambda i: (jnp.maximum(i - count, 0), 0))

    return pl.pallas_call(
        functools.partial(finish_kernel, bits, own, count + tokens // BLK),
        grid=(count + tokens // BLK,),
        in_specs=[late(inner)] * 3
        + [late(width), late(width), whole((1, width))]
        + [whole((inner, width))] * 3
        + [mine] * 3
        + [whole((tokens, width)), whole((8, width))],
        out_specs=[late(width)] + [held((width, own))] * 3 + [held((8, width))],
        out_shape=[jax.ShapeDtypeStruct((tokens, width), F32)]
        + [jax.ShapeDtypeStruct((width, own), F32)] * 3
        + [jax.ShapeDtypeStruct((8, width), F32)],
        scratch_shapes=[pltpu.VMEM((2, 8, width), F32), pltpu.VMEM((count, own, width), F32)]
        + (
            reduce_scratch(count, own, width)
            + [pltpu.VMEM((8, 8, width), F32), pltpu.SemaphoreType.DMA((7,)), pltpu.SemaphoreType.DMA((7,))]
            if hosted
            else []
        ),
        compiler_params=hosting(1, 4) if hosted else params(1),
        cost_estimate=pl.CostEstimate(
            flops=6 * tokens * width * inner, bytes_accessed=16 * tokens * width + 6 * width * inner, transcendentals=0
        ),
        name="finish",
    )(dq, dk, dv, x, d_resid, g1, wq, wk, wv, dq, dk, dv, normed1, small)


def shards(dp, tp, x, g1, c1, wq, bq, wk, wv, bv, wo, bo, g2, c2, w1, b1, w2, b2, seg, valid, cot):
    tokens, width = x.shape
    seqs, length = seg.shape
    own = wq.shape[1]
    bits = bits_of(dp) if dp == 8 else None

    def line(t):
        return t.reshape(1, -1)

    bias = jnp.zeros((8, -(-own // LANES) * LANES), F32).at[:3, :own].set(jnp.stack([bq, bv, b1]))
    fq, fk, fv, biases = gather([wq.T, wk.T, wv.T], bias, dp, tp)
    abq, abv, ab1 = (line(biases[:, r, :own]) for r in range(3))

    normed1, q, k, v, fo = project(x, line(g1), line(c1), fq, fk, fv, abq, abv, [wo], dp, tp)
    mixed, lse, f1, f2 = attend(q, k, v, seg, [w1.T, w2], dp, tp)
    y, d_resid, d_mixed, parts, small, sq = middle(
        own, mixed, x, cot, valid, fo, f1, f2, line(bo), line(g2), line(c2), ab1, line(b2)
    )
    dq, dk, dv, gwo, gw1, gw2 = attend_back(q, k, v, seg, mixed, d_mixed, lse, parts, bits)
    grad_input, gq, gk, gv, small = finish(dq, dk, dv, x, d_resid, line(g1), fq, fk, fv, normed1, small, own, bits)
    if bits is None:
        gwo, gw1, gw2, gq, gk, gv, small = lax.psum((gwo, gw1, gw2, gq, gk, gv, small), "dp")

    weight = valid.astype(F32)
    counted = jnp.maximum(jnp.sum(weight, axis=1), 1.0) * width
    stat = jnp.sum(sq[:, 0, :3].reshape(seqs, length // BLK, 3), axis=1)
    rms = jnp.sqrt(stat / counted[:, None])

    gb2, gg2, gc2, gbo, gg1, gc1 = (small[r] for r in range(6))
    gb1 = small[OWN_ROW, :own]
    gbq = small[OWN_ROW + 1, :own]
    gbv = small[OWN_ROW + 1, width // 2 : width // 2 + own]
    return (y, grad_input, gg1, gc1, gq, gbq, gk, gv, gbv, gwo, gbo, gg2, gc2, gw1, gb1, gw2, gb2, rms)


def solution(mesh):
    dp, tp = mesh.shape["dp"], mesh.shape["tensor"]
    tok, col, row, vec, rep = P("dp", None), P(None, "tensor"), P("tensor", None), P("tensor"), P()
    return jax.shard_map(
        functools.partial(shards, dp, tp),
        mesh=mesh,
        in_specs=(tok, rep, rep, col, vec, col, col, vec, row, rep, rep, rep, col, vec, row, rep, tok, tok, tok),
        out_specs=(tok, tok, rep, rep, col, vec, col, col, vec, row, rep, rep, rep, col, vec, row, rep, tok),
        check_vma=False,
    )
```

```python
import functools
import math

import jax
import jax.numpy as jnp
from jax import lax
from jax.experimental import pallas as pl
from jax.experimental.pallas import tpu as pltpu
from jax.sharding import PartitionSpec as P

HEAD_DIM = 160
MAX_DOC = 512
EPS = 1e-05
NEG = -1e30
BLK = 256
WIN = 256
LANES = 128
SCALE = 1.0 / math.sqrt(HEAD_DIM)
LOG2E = 1.0 / math.log(2.0)
BF = jnp.bfloat16
F32 = jnp.float32
VMEM_MAX = 60 << 20


def nn(a, b):
    return lax.dot_general(a, b, (((1,), (0,)), ((), ())), preferred_element_type=F32)


def nt(a, b):
    return lax.dot_general(a, b, (((1,), (1,)), ((), ())), preferred_element_type=F32)


def tn(a, b):
    return lax.dot_general(a, b, (((0,), (0,)), ((), ())), preferred_element_type=F32)


def whole(shape):
    return pl.BlockSpec(shape, lambda *_: (0,) * len(shape), pipeline_mode=pl.Buffered(1))


def held(shape):
    return pl.BlockSpec(shape, lambda *_: (0,) * len(shape))


def rows(width):
    return pl.BlockSpec((BLK, width), lambda i: (i, 0))


def column_of(row):
    n = row.shape[1]
    eye = lax.broadcasted_iota(jnp.int32, (n, n), 0) == lax.broadcasted_iota(jnp.int32, (n, n), 1)
    return jnp.sum(jnp.where(eye, row, jnp.zeros_like(row)), axis=1, keepdims=True)


def fold8(t):
    return jnp.sum(t.reshape(t.shape[0] // 8, 8, t.shape[1]), axis=0)


def params(grid, vmem=VMEM_MAX):
    return pltpu.CompilerParams(dimension_semantics=("arbitrary",) * grid, vmem_limit_bytes=vmem)


def hosting(grid, ident):
    return pltpu.CompilerParams(
        dimension_semantics=("arbitrary",) * grid,
        vmem_limit_bytes=VMEM_MAX,
        collective_id=ident,
        has_side_effects=True,
    )


def sibling(index, bit):
    return index + bit - 2 * bit * (index // bit % 2)


class Place:
    def __init__(self, bits):
        self.d, self.z = lax.axis_index("dp"), lax.axis_index("tensor")
        self.core = self.d % 2
        self.a, self.b = (self.d // bit % 2 for bit in bits)
        self.spot = self.a + 2 * self.b
        self.on_core = {"dp": sibling(self.d, 1), "tensor": self.z}
        self.on_a, self.on_b = ({"dp": sibling(self.d, bit), "tensor": self.z} for bit in bits)
        peers = (None, sibling(self.z, 1), sibling(self.z, 2), sibling(sibling(self.z, 1), 2))
        self.on_z = [None] + [{"dp": self.d, "tensor": peer} for peer in peers[1:]]

    def plane(self):
        return [{"dp": (self.d + step) % 8, "tensor": self.z} for step in range(1, 8)]


def greet(targets):
    barrier = pltpu.get_barrier_semaphore()
    for target in targets:
        pl.semaphore_signal(barrier, inc=1, device_id=target, device_id_type=pl.DeviceIdType.MESH)
    pl.semaphore_wait(barrier, len(targets))


def send(src, dst, sems, at, target):
    return pltpu.make_async_remote_copy(
        src_ref=src,
        dst_ref=dst,
        send_sem=sems[0].at[at],
        recv_sem=sems[1].at[at],
        device_id=target,
        device_id_type=pl.DeviceIdType.MESH,
    )


def bits_of(dp):
    return (2, 4) if dp == 8 else (2, 8)


def chunks_of(count, tp, piece):
    cut = (piece * 5 // 8) // 8 * 8
    return [(m, j, *span) for m in range(count) for j in range(1, tp) for span in ((0, cut), (cut, piece))]


AHEAD = 4
LAG = 2


class Gather:
    def __init__(self, place, chunks, mine, land, sems, publish):
        self.place, self.chunks, self.mine, self.land, self.sems, self.publish = place, chunks, mine, land, sems, publish
        self.ticks = len(chunks) + 3 * LAG
        self.got = {}

    def slot(self, k, where, low=None, high=None):
        m, j, r0, r1 = self.chunks[k]
        low, high = (r0 if low is None else low), (r1 if high is None else high)
        return self.land.at[m, j - 1, self.place.core, where, pl.ds(low, high - low)]

    def middle(self, k):
        _, _, r0, r1 = self.chunks[k]
        half = (r1 - r0) // 2
        return r0 + (half + 7 if k % 2 else half) // 8 * 8

    def over_z(self, k):
        m, j, r0, r1 = self.chunks[k]
        spots = [self.place.spot] + ([3 - self.place.spot] if j == 1 else [])
        return [
            send(self.mine.at[m, i, pl.ds(r0, r1 - r0)], self.slot(k, spot), self.sems, (k, i), self.place.on_z[j])
            for i, spot in enumerate(spots)
        ]

    def over_a(self, k):
        here = self.slot(k, self.place.spot)
        return send(here, here, self.sems, (k, 2), self.place.on_a)

    def over_b(self, k):
        here = self.slot(k, self.place.spot)
        return send(here, here, self.sems, (k, 3), self.place.on_b)

    def on_a(self, k):
        part = self.slot(k, sibling(self.place.spot, 2), None, self.middle(k))
        return send(part, part, self.sems, (k, 4), self.place.on_a)

    def on_b(self, k):
        part = self.slot(k, sibling(self.place.spot, 1), self.middle(k), None)
        return send(part, part, self.sems, (k, 5), self.place.on_b)

    def relays(self, k):
        return [] if self.chunks[k][1] == 1 else [self.on_a(k), self.on_b(k)]

    def swap(self, k):
        m, j, r0, r1 = self.chunks[k]
        part = self.land.at[m, j - 1, self.place.core, :, pl.ds(r0, r1 - r0)]
        return send(part, part, self.sems, (k, 6), self.place.on_core)

    def start_z(self, k):
        for one in self.over_z(k):
            one.start()

    def tick(self, t):
        total = len(self.chunks)
        if 0 <= t < total:
            for one in self.over_z(t):
                one.wait_recv()
            self.over_a(t).start()
            self.over_b(t).start()
            if t + AHEAD < total:
                self.start_z(t + AHEAD)
        k = t - LAG
        if 0 <= k < total:
            self.over_b(k).wait_recv()
            for one in self.relays(k)[:1]:
                one.start()
            self.over_a(k).wait_recv()
            for one in self.relays(k)[1:]:
                one.start()
        k = t - 2 * LAG
        if 0 <= k < total:
            for one in self.relays(k):
                one.wait_recv()
            self.swap(k).start()
        k = t - 3 * LAG
        if 0 <= k < total:
            self.swap(k).wait_recv()
            m, j, r0, r1 = self.chunks[k]
            piece = self.land.shape[4]
            self.got[m, j] = self.got.get((m, j), 0) + r1 - r0
            if self.got[m, j] == piece:
                self.publish(m, j, self.land[m, j - 1].reshape(8 * piece, -1).astype(BF))

    def end(self):
        for k in range(len(self.chunks)):
            for one in self.over_z(k) + self.relays(k) + [self.over_a(k), self.over_b(k), self.swap(k)]:
                one.wait_send()


def gather_scratch(count, tp, piece, width):
    total = len(chunks_of(count, tp, piece))
    return [
        pltpu.VMEM((count, tp - 1, 2, 4, piece, width), F32),
        pltpu.SemaphoreType.DMA((total, 7)),
        pltpu.SemaphoreType.DMA((total, 7)),
        pltpu.VMEM((count, 2, piece, width), F32),
    ]


class Reduce:
    def __init__(self, place, part, scratch, plan, publish):
        self.place, self.part, self.publish = place, part, publish
        self.count, self.own, self.width = part.shape
        self.out, self.half, self.first, self.second, *self.sems = scratch
        self.points = 1 + max(row[-1] for row in plan)
        self.plan = {p: [] for p in range(self.points)}
        for k, row in enumerate(plan):
            for stage, p in enumerate(row):
                self.plan[p].append((k, stage))
        for p, found in self.plan.items():
            found.sort(key=lambda one: (one[1] if p == self.points - 1 else -one[1], one[0]))
        ends = [k for p in range(self.points) for k, stage in self.plan[p] if stage == 6]
        self.closing = [max(2 * m, 2 * m + 1, key=ends.index) for m in range(self.count)]

    def greet(self):
        return [self.place.on_a, self.place.on_b, self.place.on_core]

    def rows_of(self, size, index, count):
        return pl.ds(pl.multiple_of(size * index, 8), count)

    def way(self, k):
        p = self.place
        return (p.a, p.on_a, p.b, p.on_b) if k % 2 == 0 else (p.b, p.on_b, p.a, p.on_a)

    def columns(self, bit):
        lanes = self.width // 2
        return pl.ds(pl.multiple_of(lanes * bit, LANES), lanes)

    def out_rows(self, k, bit):
        piece = self.own // 8
        return self.rows_of(piece, 4 * self.place.core + 2 * (k % 2) + bit, piece)

    def quarter(self, k, core):
        size = self.own // 4
        return self.rows_of(size, 2 * core + k % 2, size)

    def copy(self, k, stage):
        place, m, piece = self.place, k // 2, self.own // 8
        bit, peer, bit2, peer2 = self.way(k)
        if stage == 0:
            src, dst, to = self.part.at[m, self.quarter(k, 1 - place.core)], self.half.at[k], place.on_core
        elif stage == 1:
            src, dst, to = self.half.at[k, self.rows_of(piece, 1 - bit, piece)], self.first.at[k], peer
        elif stage == 2:
            src, dst, to = self.half.at[k, self.rows_of(piece, bit, piece), self.columns(1 - bit2)], self.second.at[k], peer2
        elif stage == 3:
            src = dst = self.out.at[m, self.out_rows(k, bit), self.columns(bit2)]
            to = peer2
        elif stage == 4:
            src = dst = self.out.at[m, self.out_rows(k, bit)]
            to = peer
        else:
            src = dst = self.out.at[m, self.quarter(k, place.core)]
            to = place.on_core
        return send(src, dst, self.sems, (k, stage), to)

    def step(self, k, stage):
        m, piece = k // 2, self.own // 8
        bit, _, bit2, _ = self.way(k)
        mine = self.rows_of(piece, bit, piece)
        if stage >= 1:
            self.copy(k, stage - 1).wait_recv()
        if stage == 1:
            self.half[k] = self.part[m, self.quarter(k, self.place.core)] + self.half[k]
        if stage == 2:
            self.half[k, mine] = self.half[k, mine] + self.first[k]
        if stage == 3:
            columns = self.columns(bit2)
            self.out[m, self.out_rows(k, bit), columns] = self.half[k, mine, columns] + self.second[k]
        if stage < 6:
            self.copy(k, stage).start()
            return
        if k == self.closing[m]:
            self.publish(m, self.out[m])

    def point(self, p):
        for k, stage in self.plan[p]:
            self.step(k, stage)

    def end(self):
        for k in range(2 * self.count):
            for stage in range(6):
                self.copy(k, stage).wait_send()


def reduce_scratch(count, own, width):
    chunks = 2 * count
    return [
        pltpu.VMEM((count, own, width), F32),
        pltpu.VMEM((chunks, own // 4, width), F32),
        pltpu.VMEM((chunks, own // 8, width), F32),
        pltpu.VMEM((chunks, own // 8, width // 2), F32),
        pltpu.SemaphoreType.DMA((chunks, 6)),
        pltpu.SemaphoreType.DMA((chunks, 6)),
    ]


def normalize(v):
    center = v - jnp.mean(v, axis=-1, keepdims=True)
    inv = lax.rsqrt(jnp.mean(center * center, axis=-1, keepdims=True) + EPS)
    return center * inv, inv


HEADS_IN_GROUP = 4
GROUP = HEADS_IN_GROUP * HEAD_DIM


def window_of(head):
    low = head * HEAD_DIM
    start = low // LANES * LANES
    return start, low - start


def lane_mask(offset):
    lane = lax.broadcasted_iota(jnp.int32, (1, WIN), 1)
    return (lane >= offset) & (lane < offset + HEAD_DIM)


def spread(parts):
    tiles = [None] * (GROUP // LANES)
    for head, part in enumerate(parts):
        first = window_of(head)[0] // LANES
        for half in range(WIN // LANES):
            piece = part[:, half * LANES : (half + 1) * LANES]
            at = first + half
            tiles[at] = piece if tiles[at] is None else tiles[at] + piece
    return jnp.concatenate(tiles, axis=1)


def attend_block(i, q_ref, k_ref, v_ref, seg_ref, o_ref, lse_ref, bias):
    groups = q_ref.shape[1] // GROUP
    back = MAX_DOC // BLK
    here = pl.ds(pl.multiple_of(i * BLK, BLK), BLK)
    seg_col = column_of(seg_ref[0, :, here])

    def body(blocks):
        keys = blocks * BLK
        start = pl.multiple_of((i + 1 - blocks) * BLK, BLK)
        row = i * BLK + lax.broadcasted_iota(jnp.int32, (BLK, keys), 0)
        col = start + lax.broadcasted_iota(jnp.int32, (BLK, keys), 1)
        allowed = (row >= col) & (seg_col == seg_ref[0, :, pl.ds(start, keys)])
        bias[:, :keys] = jnp.where(allowed, 0.0, NEG)

        def group(gi, _):
            parts = []
            lse = lse_ref[...]
            head_lane = lax.broadcasted_iota(jnp.int32, (1, LANES), 1)
            for h in range(HEADS_IN_GROUP):
                at, off = window_of(h)
                lanes = pl.ds(pl.multiple_of(gi * GROUP + at, LANES), WIN)
                mask = lane_mask(off)
                q = q_ref[here, lanes]
                q = jnp.where(mask, q, jnp.zeros_like(q))
                t = nt(q, k_ref[pl.ds(start, keys), lanes]) * (SCALE * LOG2E) + bias[:, :keys]
                top = jnp.max(t, axis=1, keepdims=True)
                p = jnp.exp2(t - top)
                total = jnp.sum(p, axis=1, keepdims=True)
                o = nn(p.astype(BF), v_ref[pl.ds(start, keys), lanes])
                parts.append(jnp.where(mask, o * (1.0 / total), 0.0))
                lse = jnp.where(head_lane == gi * HEADS_IN_GROUP + h, top + jnp.log2(total), lse)
            lse_ref[...] = lse
            o_ref[:, pl.ds(pl.multiple_of(gi * GROUP, LANES), GROUP)] = spread(parts).astype(BF)
            return 0

        lax.fori_loop(0, groups, group, 0)

    lse_ref[...] = jnp.zeros_like(lse_ref)
    count = jnp.minimum(i, back) + 1
    for blocks in range(1, back + 2):
        pl.when(count == blocks)(functools.partial(body, blocks))


def front_kernel(
    bits, n, steps, chunks, count, x_ref, g_ref, c_ref, seg_ref, bias_ref, *refs
):
    local, refs = refs[:count], refs[count:]
    n_ref, q_ref, k_ref, v_ref, o_ref, lse_ref, vec_ref, *refs = refs
    full, refs = refs[:count], refs[count:]
    bias, weights, stage, qs, ks, vs, land, gather_s, gather_r, mine, raw, bias_in, bias_s, bias_r, local_sem, out_sem, raw_sem, copy_sem = refs
    own = local[0].shape[0]
    held_here = weights.shape[0]
    step = pl.program_id(0)
    place = Place(bits)
    shards_ = len(place.on_z)
    order = {}

    def rows_of(j):
        return pl.ds(j * own, own)

    def stage_copy(number):
        m, j = order[number]
        return pltpu.make_async_copy(stage.at[number % 2], full[m].at[rows_of(j)], out_sem.at[number])

    def publish(m, j, shard):
        if m < held_here:
            weights[m, rows_of(j)] = shard
            return
        number = len(order)
        order[number] = m, j
        if number >= 2:
            stage_copy(number - 2).wait()
        stage[number % 2] = shard
        stage_copy(number).start()

    work = Gather(place, chunks, mine, land, (gather_s, gather_r), publish)
    ready = max(k for k, chunk in enumerate(chunks) if chunk[0] < held_here) + 3 * LAG + 1

    def own_copies():
        held_ = [pltpu.make_async_copy(local[m], weights.at[m, rows_of(0)], local_sem.at[m]) for m in range(held_here)]
        rest = [
            pltpu.make_async_copy(local[m], full[m].at[rows_of(0)], local_sem.at[m]) for m in range(held_here, count)
        ]
        return held_, rest

    def held_out():
        return [pltpu.make_async_copy(weights.at[m], full[m], local_sem.at[m]) for m in range(held_here)]

    @pl.when(step == 0)
    def _():
        held_, rest = own_copies()
        piece = own // 8
        raws = [
            [
                pltpu.make_async_copy(
                    local[m].at[pl.ds(pl.multiple_of(piece * (4 * place.core + spot), 8), piece)],
                    raw.at[m % 2, i],
                    raw_sem.at[m % 2, i],
                )
                for i, spot in enumerate((place.spot, 3 - place.spot))
            ]
            for m in range(count)
        ]
        for one in sum(raws[:2], []) + held_ + rest:
            one.start()
        greet(place.on_z[1:] + [place.on_a, place.on_b, place.on_core])
        for m in range(count):
            for i, one in enumerate(raws[m]):
                one.wait()
                mine[m, i] = raw[m % 2, i].astype(F32)
            for one in raws[m + 2] if m + 2 < count else []:
                one.start()
            if m == 0:
                for k in range(AHEAD):
                    work.start_z(k)
        vectors = [
            send(bias_ref.at[j], bias_in.at[j], (bias_s, bias_r), j, place.on_z[j]) for j in range(1, shards_)
        ]
        for one in vectors:
            one.start()
        for t in range(ready):
            work.tick(t)
        for one in vectors:
            one.wait()
        vec_ref[...] = sum((bias_in[j] for j in range(1, shards_)), bias_ref[0])
        for one in held_:
            one.wait()
        for one in held_out():
            one.start()

    unit = step - 1
    seq, part = unit // (2 * n), unit % (2 * n)

    def outward(sequence, block):
        here = pl.ds(pl.multiple_of(block * BLK, BLK), BLK)
        there = pl.ds(pl.multiple_of((sequence * n + block) * BLK, BLK), BLK)
        return [
            pltpu.make_async_copy(src.at[here], dst.at[there], copy_sem.at[i, block])
            for i, (src, dst) in enumerate(((qs, q_ref), (ks, k_ref), (vs, v_ref)))
        ]

    @pl.when((step > 0) & (part < n))
    def _():
        here = pl.ds(pl.multiple_of(part * BLK, BLK), BLK)

        @pl.when(seq > 0)
        def _():
            for one in outward(seq - 1, part):
                one.wait()

        hat, _ = normalize(x_ref[...].astype(F32))
        normed = (hat * g_ref[...] + c_ref[...]).astype(BF)
        n_ref[...] = normed
        qs[here] = (nt(normed, weights[0]) + vec_ref[0:1]).astype(BF)
        ks[here] = nt(normed, weights[1]).astype(BF)
        vs[here] = (nt(normed, weights[2]) + vec_ref[1:2]).astype(BF)
        for one in outward(seq, part):
            one.start()

    @pl.when((step > 0) & (part >= n))
    def _():
        attend_block(part - n, qs, ks, vs, seg_ref, o_ref, lse_ref, bias)

    left = work.ticks - ready
    for t in range(left):
        pl.when(step == 1 + t * (steps - 1) // left)(functools.partial(work.tick, ready + t))

    @pl.when(step == steps - 1)
    def _():
        work.end()
        for number in range(max(0, len(order) - 2), len(order)):
            stage_copy(number).wait()
        for one in held_out() + own_copies()[1] + sum((outward((steps - 1) // (2 * n) - 1, b) for b in range(n)), []):
            one.wait()


def front(x, g1, c1, seg, biases, shards_, dp, tp):
    tokens, width = x.shape
    seqs, length = seg.shape
    n = length // BLK
    count, own = len(shards_), shards_[0].shape[0]
    bits, piece, steps, out = bits_of(dp), own // 8, 1 + 2 * seqs * n, tp * own
    chunks = chunks_of(count, tp, piece)

    def early(size):
        return pl.BlockSpec((BLK, size), lambda i: (jnp.maximum(i - 1, 0) // (2 * n) * n + jnp.minimum(jnp.maximum(i - 1, 0) % (2 * n), n - 1), 0))

    def late(size):
        return pl.BlockSpec((BLK, size), lambda i: (jnp.maximum(i - 1, 0) // (2 * n) * n + jnp.maximum(jnp.maximum(i - 1, 0) % (2 * n) - n, 0), 0))

    anywhere = pl.BlockSpec(memory_space=pl.ANY)
    pairs = seqs * n * 2.5 * BLK * BLK * (out // HEAD_DIM)
    return pl.pallas_call(
        functools.partial(front_kernel, bits, n, steps, chunks, count),
        grid=(steps,),
        in_specs=[
            early(width),
            whole((1, width)),
            whole((1, width)),
            pl.BlockSpec((1, 1, length), lambda i: (jnp.maximum(i - 1, 0) // (2 * n), 0, 0)),
            whole(biases.shape),
        ]
        + [anywhere] * count,
        out_specs=[early(width)] + [anywhere] * 3 + [late(out), late(LANES), held(biases.shape[1:])] + [anywhere] * count,
        out_shape=[jax.ShapeDtypeStruct((tokens, width), BF)]
        + [jax.ShapeDtypeStruct((tokens, out), BF)] * 4
        + [jax.ShapeDtypeStruct((tokens, LANES), F32), jax.ShapeDtypeStruct(biases.shape[1:], F32)]
        + [jax.ShapeDtypeStruct((out, width), BF)] * count,
        scratch_shapes=[
            pltpu.VMEM((BLK, BLK + MAX_DOC), F32),
            pltpu.VMEM((3, out, width), BF),
            pltpu.VMEM((2, own, width), BF),
        ]
        + [pltpu.VMEM((length, out), BF)] * 3
        + gather_scratch(count, tp, piece, width)
        + [
            pltpu.VMEM((2, 2, piece, width), BF),
            pltpu.VMEM(biases.shape, F32),
            pltpu.SemaphoreType.DMA((tp,)),
            pltpu.SemaphoreType.DMA((tp,)),
            pltpu.SemaphoreType.DMA((count,)),
            pltpu.SemaphoreType.DMA((count * tp,)),
            pltpu.SemaphoreType.DMA((2, 2)),
            pltpu.SemaphoreType.DMA((3, n)),
        ],
        compiler_params=hosting(1, 0),
        cost_estimate=pl.CostEstimate(
            flops=int(6 * tokens * width * out + pairs * 8 * WIN),
            bytes_accessed=12 * tokens * width + 4 * count * out * width,
            transcendentals=int(pairs),
        ),
        name="front",
    )(x, g1, c1, seg.reshape(seqs, 1, length), biases, *shards_)


def attend_back_kernel(
    steps, bits, q_ref, do_ref, o_ref, lse_ref, k_ref, v_ref, seg_ref, part_ref, dq_ref, dk_ref, dv_ref, go_ref, g1_ref, g2_ref,
    bias, dq_acc, lse_t, delta_t, *reduce_refs,
):
    s, j = pl.program_id(0), pl.program_id(1)
    n = pl.num_programs(1)
    length, width = q_ref.shape
    groups = width // GROUP
    ahead = MAX_DOC // BLK

    step = s * n + j

    def publish(m, total):
        (go_ref, g1_ref, g2_ref)[m][...] = total

    if bits is not None:
        work = Reduce(Place(bits), part_ref, reduce_refs, BACK_PLAN, publish)

        @pl.when(step == 0)
        def _():
            greet(work.greet())
            work.point(0)

    @pl.when(j == 0)
    def _():
        dq_acc[...] = jnp.zeros_like(dq_acc)
        head = lax.broadcasted_iota(jnp.int32, (16, width), 0)
        lane = lax.broadcasted_iota(jnp.int32, (16, width), 1)
        pick = jnp.where((lane >= head * HEAD_DIM) & (lane < (head + 1) * HEAD_DIM), 1.0, 0.0).astype(BF)
        for b in range(length // BLK):
            at = slice(b * BLK, (b + 1) * BLK)
            lse_t[:, at] = lse_ref[at, :].T[:16, :]
            prod = do_ref[at, :].astype(F32) * o_ref[at, :].astype(F32)
            high = prod.astype(BF)
            rest = (prod - high.astype(F32)).astype(BF)
            delta_t[:, at] = nt(pick, high) + nt(pick, rest)

    count = jnp.minimum(n - j, ahead + 1)
    start = pl.multiple_of(j * BLK, BLK)
    seg_col = column_of(seg_ref[0, :, pl.ds(start, BLK)])

    def mask_of(blocks):
        queries = blocks * BLK
        row = lax.broadcasted_iota(jnp.int32, (BLK, queries), 0)
        col = lax.broadcasted_iota(jnp.int32, (BLK, queries), 1)
        allowed = (row <= col) & (seg_col == seg_ref[0, :, pl.ds(start, queries)])
        bias[:, :queries] = jnp.where(allowed, 0.0, NEG)

    def heads(gi, blocks):
        queries = blocks * BLK
        span = pl.ds(start, queries)
        dks, dvs = [], []
        for h in range(HEADS_IN_GROUP):
            at, off = window_of(h)
            lanes = pl.ds(pl.multiple_of(gi * GROUP + at, LANES), WIN)
            mask = lane_mask(off)
            head = pl.ds(gi * HEADS_IN_GROUP + h, 1)
            k = k_ref[:, lanes]
            k = jnp.where(mask, k, jnp.zeros_like(k))
            v = v_ref[:, lanes]
            v = jnp.where(mask, v, jnp.zeros_like(v))
            q = q_ref[span, lanes]
            do = do_ref[span, lanes]
            t = nt(k, q) * (SCALE * LOG2E) + bias[:, :queries]
            p = jnp.exp2(t - lse_t[head, span])
            dvs.append(jnp.where(mask, nn(p.astype(BF), do), 0.0))
            ds = (p * (nt(v, do) - delta_t[head, span])).astype(BF)
            dks.append(jnp.where(mask, nn(ds, q), 0.0))
            dq_acc[span, lanes] += tn(ds, k)
        out = pl.ds(pl.multiple_of(gi * GROUP, LANES), GROUP)
        dk_ref[:, out] = (spread(dks) * SCALE).astype(BF)
        dv_ref[:, out] = spread(dvs).astype(BF)

    kinds = range(1, ahead + 2)
    for blocks in kinds:
        pl.when(count == blocks)(functools.partial(mask_of, blocks))

    def group(gi, carry):
        for blocks in kinds:
            pl.when(count == blocks)(functools.partial(heads, gi, blocks))
        if bits is not None:
            for p in range(1, work.points):
                pl.when(step * groups + gi + 1 == p)(functools.partial(work.point, p))
        return carry

    lax.fori_loop(0, groups, group, 0)

    if bits is not None:
        pl.when(step == steps - 1)(work.end)
    else:
        for m in range(3):
            publish(m, part_ref[m])

    @pl.when(j == n - 1)
    def _():
        dq_ref[...] = (dq_acc[...] * SCALE).astype(BF)


def attend_back(q, k, v, seg, mixed, d_mixed, lse, parts, bits):
    tokens, width = q.shape
    seqs, length = seg.shape
    own, model = parts.shape[1:]
    n = length // BLK
    spec_k = pl.BlockSpec((BLK, width), lambda s, j: (s * n + j, 0))
    spec_q = pl.BlockSpec((length, width), lambda s, j: (s, 0))
    pairs = seqs * n * 2.5 * BLK * BLK * (width // HEAD_DIM)
    hosted = bits is not None
    return pl.pallas_call(
        functools.partial(attend_back_kernel, seqs * n, bits),
        grid=(seqs, n),
        in_specs=[
            spec_q,
            spec_q,
            spec_q,
            pl.BlockSpec((length, LANES), lambda s, j: (s, 0)),
            spec_k,
            spec_k,
            pl.BlockSpec((1, 1, length), lambda s, j: (s, 0, 0)),
            whole(parts.shape),
        ],
        out_specs=[spec_q, spec_k, spec_k] + [held((own, model))] * 3,
        scratch_shapes=[
            pltpu.VMEM((BLK, BLK + MAX_DOC), F32),
            pltpu.VMEM((length, width), F32),
            pltpu.VMEM((16, length), F32),
            pltpu.VMEM((16, length), F32),
        ]
        + (reduce_scratch(*parts.shape) if hosted else []),
        out_shape=[jax.ShapeDtypeStruct((tokens, width), BF)] * 3 + [jax.ShapeDtypeStruct((own, model), F32)] * 3,
        compiler_params=hosting(2, 3) if hosted else params(2),
        cost_estimate=pl.CostEstimate(
            flops=int(pairs * 20 * WIN), bytes_accessed=16 * tokens * width, transcendentals=int(pairs)
        ),
        name="attend_back",
    )(q, d_mixed, mixed, lse, k, v, seg.reshape(seqs, 1, length), parts)


BACK_PLAN = (
    (1, 2, 4, 8, 10, 13, 16),
    (0, 1, 3, 4, 6, 12, 16),
    (3, 4, 9, 10, 11, 13, 16),
    (0, 2, 8, 9, 12, 14, 16),
    (0, 1, 3, 5, 12, 15, 16),
    (2, 3, 7, 9, 11, 13, 16),
)
FINISH_PLAN = (
    (0, 1, 6, 10, 13, 19, 26),
    (0, 1, 5, 9, 13, 18, 21),
    (5, 6, 12, 16, 19, 24, 26),
    (1, 3, 10, 17, 21, 25, 26),
    (2, 3, 9, 17, 20, 25, 26),
    (4, 5, 12, 16, 19, 23, 25),
)

OWN_ROW = 6


def middle_kernel(
    own, m_ref, x_ref, g_ref, w_ref, wo_ref, w1_ref, w2_ref, bo_ref, g2_ref, c2_ref, b1_ref, b2_ref,
    y_ref, dr_ref, dm_ref, part_ref, small_ref, sq_ref, vec,
):
    i = pl.program_id(0)

    @pl.when(i == 0)
    def _():
        part_ref[...] = jnp.zeros_like(part_ref)
        vec[...] = jnp.zeros_like(vec)

    mixed = m_ref[...]
    cot = g_ref[...]
    attended = nn(mixed, wo_ref[...]) + bo_ref[...]
    resid = x_ref[...].astype(F32) + attended
    hat, inv = normalize(resid)
    normed = (hat * g2_ref[...] + c2_ref[...]).astype(BF)
    pre = nt(normed, w1_ref[...]) + b1_ref[2:3]
    cdf = 0.5 + 0.5 * lax.erf(pre * math.sqrt(0.5))
    act = (pre * cdf).astype(BF)
    slope = cdf + pre * jnp.exp(-0.5 * pre * pre) * (1.0 / math.sqrt(2.0 * math.pi))
    branch = nn(act, w2_ref[...]) + b2_ref[...]
    output = resid + branch
    y_ref[...] = output.astype(BF)
    weight = column_of(w_ref[0])
    lane = lax.broadcasted_iota(jnp.int32, (1, LANES), 1)
    sums = jnp.zeros((1, LANES), F32)
    for at, v in enumerate((attended, branch, output)):
        one = jnp.sum(weight * jnp.sum(v * v, axis=1, keepdims=True), axis=0, keepdims=True)
        sums = jnp.where(lane == at, one, sums)
    sq_ref[...] = jnp.broadcast_to(sums, sq_ref.shape[1:])[None]

    d_pre = (nt(cot, w2_ref[...]) * slope).astype(BF)
    part_ref[2] += tn(act[:, :own], cot)
    part_ref[1] += tn(d_pre[:, :own], normed)
    d_normed = nn(d_pre, w1_ref[...])
    d_hat = d_normed * g2_ref[...]
    grad = cot.astype(F32)
    d_resid = grad + inv * (
        d_hat - jnp.mean(d_hat, axis=1, keepdims=True) - hat * jnp.mean(d_hat * hat, axis=1, keepdims=True)
    )
    dr_ref[...] = d_resid
    low = d_resid.astype(BF)
    part_ref[0] += tn(mixed[:, :own], low)
    dm_ref[...] = nt(low, wo_ref[...]).astype(BF)
    for at, v in enumerate((grad, d_normed * hat, d_normed, low.astype(F32), d_pre.astype(F32))):
        vec[at] += fold8(v)

    @pl.when(i == pl.num_programs(0) - 1)
    def _():
        small_ref[...] = jnp.zeros_like(small_ref)
        for at, row in enumerate((0, 1, 2, 3, OWN_ROW)):
            small_ref[row : row + 1] = jnp.sum(vec[at], axis=0, keepdims=True)


def middle(own, mixed, x, cot, valid, wo, w1, w2, bo, g2, c2, b1, b2):
    tokens, width = x.shape
    inner, hidden = wo.shape[0], w1.shape[0]
    n = tokens // BLK
    return pl.pallas_call(
        functools.partial(middle_kernel, own),
        grid=(n,),
        in_specs=[rows(inner), rows(width), rows(width), pl.BlockSpec((1, 1, BLK), lambda i: (i, 0, 0))]
        + [whole((inner, width)), whole((hidden, width)), whole((hidden, width))]
        + [whole((1, width))] * 3
        + [whole(b1.shape), whole((1, width))],
        out_specs=[
            rows(width),
            rows(width),
            rows(inner),
            held((3, own, width)),
            held((8, width)),
            pl.BlockSpec((1, 8, LANES), lambda i: (i, 0, 0)),
        ],
        out_shape=[
            jax.ShapeDtypeStruct((tokens, width), BF),
            jax.ShapeDtypeStruct((tokens, width), F32),
            jax.ShapeDtypeStruct((tokens, inner), BF),
            jax.ShapeDtypeStruct((3, own, width), F32),
            jax.ShapeDtypeStruct((8, width), F32),
            jax.ShapeDtypeStruct((n, 8, LANES), F32),
        ],
        scratch_shapes=[pltpu.VMEM((5, 8, width), F32)],
        compiler_params=params(1),
        cost_estimate=pl.CostEstimate(
            flops=2 * tokens * width * (6 * width + 3 * own),
            bytes_accessed=14 * tokens * width + 6 * width * width,
            transcendentals=2 * tokens * hidden,
        ),
        name="middle",
    )(mixed, x, cot, valid.astype(F32).reshape(n, 1, BLK), wo, w1, w2, bo, g2, c2, b1, b2)


def finish_kernel(
    bits, own, steps, dq_ref, dk_ref, dv_ref, x_ref, dr_ref, g_ref, wq_ref, wk_ref, wv_ref, mq_ref, mk_ref, mv_ref, n_ref, in_ref,
    dx_ref, gq_ref, gk_ref, gv_ref, small_ref, vec, part, acc, *refs,
):
    step = pl.program_id(0)
    grads = (mq_ref, mk_ref, mv_ref)
    count = len(grads)
    half = part.shape[2] // 2

    def publish(m, total):
        (gq_ref, gk_ref, gv_ref)[m][...] = total

    if bits is not None:
        place = Place(bits)
        work = Reduce(place, part, refs[:-3], FINISH_PLAN, publish)
        box, *sems = refs[-3:]

    @pl.when(step == 0)
    def _():
        vec[...] = jnp.zeros_like(vec)
        small_ref[...] = in_ref[...]
        if bits is not None:
            greet(place.plane())

    def weight_grad(m):
        mine = grads[m][:, :own]
        part[m] = tn(mine, n_ref[...])
        if m != 1:
            at = 0 if m == 0 else half
            small_ref[OWN_ROW + 1 : OWN_ROW + 2, at : at + own] = jnp.sum(mine.astype(F32), axis=0, keepdims=True)

    def points(first, at, every):
        if bits is not None:
            for p in range(first, work.points, every):
                if work.plan[p]:
                    pl.when(step == at + (p - first) // every)(functools.partial(work.point, p))

    for m in range(count):
        pl.when(step == m)(functools.partial(weight_grad, m))
        if bits is not None:
            pl.when(step == m)(functools.partial(work.point, m))

    @pl.when(step >= count)
    def _():
        acc[...] = nn(dq_ref[...], wq_ref[...])
        points(count, count, 3)
        acc[...] += nn(dk_ref[...], wk_ref[...])
        points(count + 1, count, 3)
        d_normed = acc[...] + nn(dv_ref[...], wv_ref[...])
        hat, inv = normalize(x_ref[...].astype(F32))
        d_hat = d_normed * g_ref[...]
        dx_ref[...] = dr_ref[...] + inv * (
            d_hat - jnp.mean(d_hat, axis=1, keepdims=True) - hat * jnp.mean(d_hat * hat, axis=1, keepdims=True)
        )
        vec[0] += fold8(d_normed * hat)
        vec[1] += fold8(d_normed)
        points(count + 2, count, 3)

    @pl.when(step == steps - 1)
    def _():
        for at in range(2):
            small_ref[4 + at : 5 + at] = jnp.sum(vec[at], axis=0, keepdims=True)
        if bits is None:
            for m in range(count):
                publish(m, part[m])
        else:
            copies = [send(small_ref, box.at[place.d], sems, i, peer) for i, peer in enumerate(place.plane())]
            for one in copies:
                one.start()
            box[place.d] = small_ref[...]
            for one in copies:
                one.wait_recv()
            for one in copies:
                one.wait_send()
            total = box[0]
            for i in range(1, 8):
                total = total + box[i]
            small_ref[...] = total
            work.end()


def finish(dq, dk, dv, x, d_resid, g1, wq, wk, wv, normed1, small, own, bits):
    tokens, width = x.shape
    inner = wq.shape[0]
    hosted = bits is not None
    count = 3
    pad = -(-own // LANES) * LANES
    mine = pl.BlockSpec((tokens, pad), lambda i: (0, 0), pipeline_mode=pl.Buffered(1))

    def late(size):
        return pl.BlockSpec((BLK, size), lambda i: (jnp.maximum(i - count, 0), 0))

    return pl.pallas_call(
        functools.partial(finish_kernel, bits, own, count + tokens // BLK),
        grid=(count + tokens // BLK,),
        in_specs=[late(inner)] * 3
        + [late(width), late(width), whole((1, width))]
        + [whole((inner, width))] * 3
        + [mine] * 3
        + [whole((tokens, width)), whole((8, width))],
        out_specs=[late(width)] + [held((own, width))] * 3 + [held((8, width))],
        out_shape=[jax.ShapeDtypeStruct((tokens, width), F32)]
        + [jax.ShapeDtypeStruct((own, width), F32)] * 3
        + [jax.ShapeDtypeStruct((8, width), F32)],
        scratch_shapes=[
            pltpu.VMEM((2, 8, width), F32),
            pltpu.VMEM((count, own, width), F32),
            pltpu.VMEM((BLK, width), F32),
        ]
        + (
            reduce_scratch(count, own, width)
            + [pltpu.VMEM((8, 8, width), F32), pltpu.SemaphoreType.DMA((7,)), pltpu.SemaphoreType.DMA((7,))]
            if hosted
            else []
        ),
        compiler_params=hosting(1, 4) if hosted else params(1),
        cost_estimate=pl.CostEstimate(
            flops=6 * tokens * width * inner, bytes_accessed=16 * tokens * width + 6 * width * inner, transcendentals=0
        ),
        name="finish",
    )(dq, dk, dv, x, d_resid, g1, wq, wk, wv, dq, dk, dv, normed1, small)


def shards(dp, tp, x, g1, c1, wq, bq, wk, wv, bv, wo, bo, g2, c2, w1, b1, w2, b2, seg, valid, cot):
    tokens, width = x.shape
    seqs, length = seg.shape
    own = wq.shape[1]
    bits = bits_of(dp) if dp == 8 else None

    def line(t):
        return t.reshape(1, -1)

    own_biases = jnp.stack([bq, bv, b1])
    own_biases = jnp.concatenate([jnp.tile(own_biases, (1, tp)), jnp.zeros((5, tp * own), F32)], axis=0)
    place = lax.broadcasted_iota(jnp.int32, (tp, 8, tp * own), 2) // own
    biases = jnp.where(place == lax.broadcasted_iota(jnp.int32, place.shape, 0), own_biases[None], 0.0)
    normed1, q, k, v, mixed, lse, vectors, fq, fk, fv, fo, f1, f2 = front(
        x, line(g1), line(c1), seg, biases, [wq.T, wk.T, wv.T, wo, w1.T, w2], dp, tp
    )

    y, d_resid, d_mixed, parts, small, sq = middle(
        own, mixed, x, cot, valid, fo, f1, f2, line(bo), line(g2), line(c2), vectors, line(b2)
    )
    dq, dk, dv, gwo, gw1, gw2 = attend_back(q, k, v, seg, mixed, d_mixed, lse, parts, bits)
    grad_input, gq, gk, gv, small = finish(dq, dk, dv, x, d_resid, line(g1), fq, fk, fv, normed1, small, own, bits)
    if bits is None:
        gwo, gw1, gw2, gq, gk, gv, small = lax.psum((gwo, gw1, gw2, gq, gk, gv, small), "dp")

    weight = valid.astype(F32)
    counted = jnp.maximum(jnp.sum(weight, axis=1), 1.0) * width
    stat = jnp.sum(sq[:, 0, :3].reshape(seqs, length // BLK, 3), axis=1)
    rms = jnp.sqrt(stat / counted[:, None])

    gb2, gg2, gc2, gbo, gg1, gc1 = (small[r] for r in range(6))
    gb1 = small[OWN_ROW, :own]
    gbq = small[OWN_ROW + 1, :own]
    gbv = small[OWN_ROW + 1, width // 2 : width // 2 + own]
    return (y, grad_input, gg1, gc1, gq.T, gbq, gk.T, gv.T, gbv, gwo, gbo, gg2, gc2, gw1.T, gb1, gw2, gb2, rms)


def solution(mesh):
    dp, tp = mesh.shape["dp"], mesh.shape["tensor"]
    tok, col, row, vec, rep = P("dp", None), P(None, "tensor"), P("tensor", None), P("tensor"), P()
    return jax.shard_map(
        functools.partial(shards, dp, tp),
        mesh=mesh,
        in_specs=(tok, rep, rep, col, vec, col, col, vec, row, rep, rep, rep, col, vec, row, rep, tok, tok, tok),
        out_specs=(tok, tok, rep, rep, col, vec, col, col, vec, row, rep, rep, rep, col, vec, row, rep, tok),
        check_vma=False,
    )
```

```python
import functools
import math

import jax
import jax.numpy as jnp
from jax import lax
from jax.experimental import pallas as pl
from jax.experimental.pallas import tpu as pltpu
from jax.sharding import PartitionSpec as P

HEAD_DIM = 160
MAX_DOC = 512
EPS = 1e-05
NEG = -1e30
BLK = 256
WIN = 256
LANES = 128
SCALE = 1.0 / math.sqrt(HEAD_DIM)
LOG2E = 1.0 / math.log(2.0)
BF = jnp.bfloat16
F32 = jnp.float32
VMEM_MAX = 60 << 20


def nn(a, b):
    return lax.dot_general(a, b, (((1,), (0,)), ((), ())), preferred_element_type=F32)


def nt(a, b):
    return lax.dot_general(a, b, (((1,), (1,)), ((), ())), preferred_element_type=F32)


def tn(a, b):
    return lax.dot_general(a, b, (((0,), (0,)), ((), ())), preferred_element_type=F32)


def whole(shape):
    return pl.BlockSpec(shape, lambda *_: (0,) * len(shape), pipeline_mode=pl.Buffered(1))


def held(shape):
    return pl.BlockSpec(shape, lambda *_: (0,) * len(shape))


def rows(width):
    return pl.BlockSpec((BLK, width), lambda i: (i, 0))


def column_of(row):
    n = row.shape[1]
    eye = lax.broadcasted_iota(jnp.int32, (n, n), 0) == lax.broadcasted_iota(jnp.int32, (n, n), 1)
    return jnp.sum(jnp.where(eye, row, jnp.zeros_like(row)), axis=1, keepdims=True)


def line(ref):
    return ref[...].reshape(1, ref.shape[0])


def fold8(t):
    return jnp.sum(t.reshape(t.shape[0] // 8, 8, t.shape[1]), axis=0)


def params(grid, vmem=VMEM_MAX):
    return pltpu.CompilerParams(dimension_semantics=("arbitrary",) * grid, vmem_limit_bytes=vmem)


def hosting(grid, ident):
    return pltpu.CompilerParams(
        dimension_semantics=("arbitrary",) * grid,
        vmem_limit_bytes=VMEM_MAX,
        collective_id=ident,
        has_side_effects=True,
    )


def sibling(index, bit):
    return index + bit - 2 * bit * (index // bit % 2)


class Place:
    def __init__(self, bits):
        self.d, self.z = lax.axis_index("dp"), lax.axis_index("tensor")
        self.core = self.d % 2
        self.a, self.b = (self.d // bit % 2 for bit in bits)
        self.spot = self.a + 2 * self.b
        self.on_core = {"dp": sibling(self.d, 1), "tensor": self.z}
        self.on_a, self.on_b = ({"dp": sibling(self.d, bit), "tensor": self.z} for bit in bits)
        peers = (None, sibling(self.z, 1), sibling(self.z, 2), sibling(sibling(self.z, 1), 2))
        self.on_z = [None] + [{"dp": self.d, "tensor": peer} for peer in peers[1:]]

    def plane(self):
        return [{"dp": (self.d + step) % 8, "tensor": self.z} for step in range(1, 8)]


def greet(targets):
    barrier = pltpu.get_barrier_semaphore()
    for target in targets:
        pl.semaphore_signal(barrier, inc=1, device_id=target, device_id_type=pl.DeviceIdType.MESH)
    pl.semaphore_wait(barrier, len(targets))


def send(src, dst, sems, at, target):
    return pltpu.make_async_remote_copy(
        src_ref=src,
        dst_ref=dst,
        send_sem=sems[0].at[at],
        recv_sem=sems[1].at[at],
        device_id=target,
        device_id_type=pl.DeviceIdType.MESH,
    )


def bits_of(dp):
    return (2, 4) if dp == 8 else (2, 8)


def chunks_of(count, tp, piece):
    cut = (piece * 5 // 8) // 8 * 8
    orders = [[1 + (j + m % 2) % (tp - 1) for j in range(tp - 1)] for m in range(count)]
    return [(m, j, *span) for m in range(count) for span in ((0, cut), (cut, piece)) for j in orders[m]]


AHEAD = 6
LAG = 2
ATTEND_COST = 0.9


class Gather:
    def __init__(self, place, chunks, mine, land, sems, publish):
        self.place, self.chunks, self.mine, self.land, self.sems, self.publish = place, chunks, mine, land, sems, publish
        self.ticks = len(chunks) + 3 * LAG
        self.got = {}

    def slot(self, k, where, low=None, high=None):
        m, j, r0, r1 = self.chunks[k]
        low, high = (r0 if low is None else low), (r1 if high is None else high)
        return self.land.at[m, j - 1, self.place.core, where, pl.ds(low, high - low)]

    def middle(self, k):
        _, _, r0, r1 = self.chunks[k]
        half = (r1 - r0) // 2
        return r0 + (half + 7 if k % 2 else half) // 8 * 8

    def over_z(self, k):
        m, j, r0, r1 = self.chunks[k]
        spots = [self.place.spot] + ([3 - self.place.spot] if j == 1 else [])
        return [
            send(self.mine.at[m, i, pl.ds(r0, r1 - r0)], self.slot(k, spot), self.sems, (k, i), self.place.on_z[j])
            for i, spot in enumerate(spots)
        ]

    def over_a(self, k):
        here = self.slot(k, self.place.spot)
        return send(here, here, self.sems, (k, 2), self.place.on_a)

    def over_b(self, k):
        here = self.slot(k, self.place.spot)
        return send(here, here, self.sems, (k, 3), self.place.on_b)

    def on_a(self, k):
        part = self.slot(k, sibling(self.place.spot, 2), None, self.middle(k))
        return send(part, part, self.sems, (k, 4), self.place.on_a)

    def on_b(self, k):
        part = self.slot(k, sibling(self.place.spot, 1), self.middle(k), None)
        return send(part, part, self.sems, (k, 5), self.place.on_b)

    def relays(self, k):
        return [] if self.chunks[k][1] == 1 else [self.on_a(k), self.on_b(k)]

    def swap(self, k):
        m, j, r0, r1 = self.chunks[k]
        part = self.land.at[m, j - 1, self.place.core, :, pl.ds(r0, r1 - r0)]
        return send(part, part, self.sems, (k, 6), self.place.on_core)

    def start_z(self, k):
        for one in self.over_z(k):
            one.start()

    def tick(self, t):
        total = len(self.chunks)
        if 0 <= t < total:
            for one in self.over_z(t):
                one.wait_recv()
            self.over_a(t).start()
            self.over_b(t).start()
            if t + AHEAD < total:
                self.start_z(t + AHEAD)
        k = t - LAG
        if 0 <= k < total:
            self.over_b(k).wait_recv()
            for one in self.relays(k)[:1]:
                one.start()
            self.over_a(k).wait_recv()
            for one in self.relays(k)[1:]:
                one.start()
        k = t - 2 * LAG
        if 0 <= k < total:
            for one in self.relays(k):
                one.wait_recv()
            self.swap(k).start()
        k = t - 3 * LAG
        if 0 <= k < total:
            self.swap(k).wait_recv()
            m, j, r0, r1 = self.chunks[k]
            piece = self.land.shape[4]
            self.got[m, j] = self.got.get((m, j), 0) + r1 - r0
            if self.got[m, j] == piece:
                self.publish(m, j, self.land[m, j - 1].reshape(8 * piece, -1).astype(BF))

    def end(self):
        for k in range(len(self.chunks)):
            for one in self.over_z(k) + self.relays(k) + [self.over_a(k), self.over_b(k), self.swap(k)]:
                one.wait_send()


def gather_scratch(count, tp, piece, width):
    total = len(chunks_of(count, tp, piece))
    return [
        pltpu.VMEM((count, tp - 1, 2, 4, piece, width), F32),
        pltpu.SemaphoreType.DMA((total, 7)),
        pltpu.SemaphoreType.DMA((total, 7)),
        pltpu.VMEM((count, 2, piece, width), F32),
    ]


class Reduce:
    def __init__(self, place, part, scratch, plan, publish):
        self.place, self.part, self.publish = place, part, publish
        self.count, self.own, self.width = part.shape
        self.out, self.half, self.first, self.second, *self.sems = scratch
        self.points = 1 + max(row[-1] for row in plan)
        self.plan = {p: [] for p in range(self.points)}
        for k, row in enumerate(plan):
            for stage, p in enumerate(row):
                self.plan[p].append((k, stage))
        for p, found in self.plan.items():
            found.sort(key=lambda one: (one[1] if p == self.points - 1 else -one[1], one[0]))
        ends = [k for p in range(self.points) for k, stage in self.plan[p] if stage == 6]
        self.closing = [max(2 * m, 2 * m + 1, key=ends.index) for m in range(self.count)]

    def greet(self):
        return [self.place.on_a, self.place.on_b, self.place.on_core]

    def rows_of(self, size, index, count):
        return pl.ds(pl.multiple_of(size * index, 8), count)

    def way(self, k):
        p = self.place
        return (p.a, p.on_a, p.b, p.on_b) if k % 2 == 0 else (p.b, p.on_b, p.a, p.on_a)

    def columns(self, bit):
        lanes = self.width // 2
        return pl.ds(pl.multiple_of(lanes * bit, LANES), lanes)

    def out_rows(self, k, bit):
        piece = self.own // 8
        return self.rows_of(piece, 4 * self.place.core + 2 * (k % 2) + bit, piece)

    def quarter(self, k, core):
        size = self.own // 4
        return self.rows_of(size, 2 * core + k % 2, size)

    def copy(self, k, stage):
        place, m, piece = self.place, k // 2, self.own // 8
        bit, peer, bit2, peer2 = self.way(k)
        if stage == 0:
            src, dst, to = self.part.at[m, self.quarter(k, 1 - place.core)], self.half.at[k], place.on_core
        elif stage == 1:
            src, dst, to = self.half.at[k, self.rows_of(piece, 1 - bit, piece)], self.first.at[k], peer
        elif stage == 2:
            src, dst, to = self.half.at[k, self.rows_of(piece, bit, piece), self.columns(1 - bit2)], self.second.at[k], peer2
        elif stage == 3:
            src = dst = self.out.at[m, self.out_rows(k, bit), self.columns(bit2)]
            to = peer2
        elif stage == 4:
            src = dst = self.out.at[m, self.out_rows(k, bit)]
            to = peer
        else:
            src = dst = self.out.at[m, self.quarter(k, place.core)]
            to = place.on_core
        return send(src, dst, self.sems, (k, stage), to)

    def step(self, k, stage):
        m, piece = k // 2, self.own // 8
        bit, _, bit2, _ = self.way(k)
        mine = self.rows_of(piece, bit, piece)
        if stage >= 1:
            self.copy(k, stage - 1).wait_recv()
        if stage == 1:
            self.half[k] = self.part[m, self.quarter(k, self.place.core)] + self.half[k]
        if stage == 2:
            self.half[k, mine] = self.half[k, mine] + self.first[k]
        if stage == 3:
            columns = self.columns(bit2)
            self.out[m, self.out_rows(k, bit), columns] = self.half[k, mine, columns] + self.second[k]
        if stage < 6:
            self.copy(k, stage).start()
            return
        if k == self.closing[m]:
            self.publish(m, self.out[m])

    def point(self, p):
        for k, stage in self.plan[p]:
            self.step(k, stage)

    def end(self):
        for k in range(2 * self.count):
            for stage in range(6):
                self.copy(k, stage).wait_send()


def reduce_scratch(count, own, width):
    chunks = 2 * count
    return [
        pltpu.VMEM((count, own, width), F32),
        pltpu.VMEM((chunks, own // 4, width), F32),
        pltpu.VMEM((chunks, own // 8, width), F32),
        pltpu.VMEM((chunks, own // 8, width // 2), F32),
        pltpu.SemaphoreType.DMA((chunks, 6)),
        pltpu.SemaphoreType.DMA((chunks, 6)),
    ]


def normalize(v):
    center = v - jnp.mean(v, axis=-1, keepdims=True)
    inv = lax.rsqrt(jnp.mean(center * center, axis=-1, keepdims=True) + EPS)
    return center * inv, inv


HEADS_IN_GROUP = 4
GROUP = HEADS_IN_GROUP * HEAD_DIM


def window_of(head):
    low = head * HEAD_DIM
    start = low // LANES * LANES
    return start, low - start


def lane_mask(offset):
    lane = lax.broadcasted_iota(jnp.int32, (1, WIN), 1)
    return (lane >= offset) & (lane < offset + HEAD_DIM)


def spread(parts):
    tiles = [None] * (GROUP // LANES)
    for head, part in enumerate(parts):
        first = window_of(head)[0] // LANES
        for half in range(WIN // LANES):
            piece = part[:, half * LANES : (half + 1) * LANES]
            at = first + half
            tiles[at] = piece if tiles[at] is None else tiles[at] + piece
    return jnp.concatenate(tiles, axis=1)


def attend_block(seq, i, q_ref, k_ref, v_ref, seg_ref, o_ref, lse_ref, bias):
    groups = q_ref.shape[1] // GROUP
    back = MAX_DOC // BLK
    here = pl.ds(pl.multiple_of(i * BLK, BLK), BLK)
    row = pl.ds(seq, 1)
    seg_col = column_of(seg_ref[row, here])

    def body(blocks):
        keys = blocks * BLK
        start = pl.multiple_of((i + 1 - blocks) * BLK, BLK)
        query = i * BLK + lax.broadcasted_iota(jnp.int32, (BLK, keys), 0)
        key = start + lax.broadcasted_iota(jnp.int32, (BLK, keys), 1)
        allowed = (query >= key) & (seg_col == seg_ref[row, pl.ds(start, keys)])
        bias[:, :keys] = jnp.where(allowed, 0.0, NEG)

        def group(gi, _):
            parts = []
            lse = lse_ref[...]
            head_lane = lax.broadcasted_iota(jnp.int32, (1, LANES), 1)
            for h in range(HEADS_IN_GROUP):
                at, off = window_of(h)
                lanes = pl.ds(pl.multiple_of(gi * GROUP + at, LANES), WIN)
                mask = lane_mask(off)
                q = q_ref[here, lanes]
                q = jnp.where(mask, q, jnp.zeros_like(q))
                t = nt(q, k_ref[pl.ds(start, keys), lanes]) * (SCALE * LOG2E) + bias[:, :keys]
                top = jnp.max(t, axis=1, keepdims=True)
                p = jnp.exp2(t - top)
                total = jnp.sum(p, axis=1, keepdims=True)
                o = nn(p.astype(BF), v_ref[pl.ds(start, keys), lanes])
                parts.append(jnp.where(mask, o * (1.0 / total), 0.0))
                lse = jnp.where(head_lane == gi * HEADS_IN_GROUP + h, top + jnp.log2(total), lse)
            lse_ref[...] = lse
            o_ref[:, pl.ds(pl.multiple_of(gi * GROUP, LANES), GROUP)] = spread(parts).astype(BF)
            return 0

        lax.fori_loop(0, groups, group, 0)

    lse_ref[...] = jnp.zeros_like(lse_ref)
    count = jnp.minimum(i, back) + 1
    for blocks in range(1, back + 2):
        pl.when(count == blocks)(functools.partial(body, blocks))


def front_kernel(
    bits, n, seqs, steps, chunks, count, x_ref, g_ref, c_ref, seg_ref, bias_ref, *refs
):
    local, refs = refs[:count], refs[count:]
    n_ref, q_ref, k_ref, v_ref, o_ref, lse_ref, vec_ref, *refs = refs
    full, refs = refs[:count], refs[count:]
    bias, weights, stage, qs, ks, vs, ns, passing, land, gather_s, gather_r, mine, raw, bias_in, bias_s, bias_r, local_sem, out_sem, raw_sem, copy_sem, back_sem = refs
    own = local[0].shape[0]
    held_here = weights.shape[0]
    step = pl.program_id(0)
    place = Place(bits)
    shards_ = len(place.on_z)
    ahead = 2 * n + (seqs - 1) * n
    order = {}

    def rows_of(j):
        return pl.ds(j * own, own)

    def stage_copy(number):
        m, j = order[number]
        return pltpu.make_async_copy(stage.at[number % 2], full[m].at[rows_of(j)], out_sem.at[number])

    def publish(m, j, shard):
        if m < held_here:
            weights[m, rows_of(j)] = shard
            return
        number = len(order)
        order[number] = m, j
        if number >= 2:
            stage_copy(number - 2).wait()
        stage[number % 2] = shard
        stage_copy(number).start()

    work = Gather(place, chunks, mine, land, (gather_s, gather_r), publish)
    ready = [max(k for k, chunk in enumerate(chunks) if chunk[0] == m) + 3 * LAG + 1 for m in range(held_here)]

    def own_copies():
        held_ = [pltpu.make_async_copy(local[m], weights.at[m, rows_of(0)], local_sem.at[m]) for m in range(held_here)]
        rest = [
            pltpu.make_async_copy(local[m], full[m].at[rows_of(0)], local_sem.at[m]) for m in range(held_here, count)
        ]
        return held_, rest

    def held_out():
        return [pltpu.make_async_copy(weights.at[m], full[m], local_sem.at[m]) for m in range(held_here)]

    @pl.when(step == 0)
    def _():
        held_, rest = own_copies()
        piece = own // 8
        raws = [
            [
                pltpu.make_async_copy(
                    local[m].at[pl.ds(pl.multiple_of(piece * (4 * place.core + spot), 8), piece)],
                    raw.at[m % 2, i],
                    raw_sem.at[m % 2, i],
                )
                for i, spot in enumerate((place.spot, 3 - place.spot))
            ]
            for m in range(count)
        ]
        for one in sum(raws[:2], []) + held_ + rest:
            one.start()
        greet(place.on_z[1:] + [place.on_a, place.on_b, place.on_core])
        for m in range(count):
            for i, one in enumerate(raws[m]):
                one.wait()
                mine[m, i] = raw[m % 2, i].astype(F32)
            for one in raws[m + 2] if m + 2 < count else []:
                one.start()
            if m == 0:
                for k in range(AHEAD):
                    work.start_z(k)
        vectors = [
            send(bias_ref.at[j], bias_in.at[j], (bias_s, bias_r), j, place.on_z[j]) for j in range(1, shards_)
        ]
        for one in vectors:
            one.start()
        for t in range(ready[0]):
            work.tick(t)
        for one in vectors:
            one.wait()
        vec_ref[...] = sum((bias_in[j] for j in range(1, shards_)), bias_ref[0])
        for one in held_:
            one.wait()

    @pl.when(step == 1 + ahead)
    def _():
        for one in held_out():
            one.start()

    unit = jnp.maximum(step - 1 - ahead, 0)
    seq, part = unit // (2 * n), unit % (2 * n)
    early = jnp.maximum(step - 1 - 2 * n, 0)
    block = jnp.where(step <= 2 * n, (step - 1 + n) % n, jnp.where(step <= ahead, early % n, part % n))
    here = pl.ds(pl.multiple_of(block * BLK, BLK), BLK)

    def norm():
        hat, _ = normalize(x_ref[...].astype(F32))
        return (hat * line(g_ref) + line(c_ref)).astype(BF)

    def make(m, normed):
        value = nt(normed, weights[m])
        if m != 1:
            value = value + vec_ref[m // 2 : m // 2 + 1]
        return value.astype(BF)

    def leave(i, src, dst, sequence):
        there = pl.ds(pl.multiple_of((sequence * n + block) * BLK, BLK), BLK)
        return pltpu.make_async_copy(src, dst.at[there], copy_sem.at[i, block])

    def enter(sequence):
        there = pl.ds(pl.multiple_of(sequence * n * BLK, BLK), n * BLK)
        return [
            pltpu.make_async_copy(src.at[there], dst, back_sem.at[i]) for i, (src, dst) in enumerate(((q_ref, qs), (k_ref, ks)))
        ]

    @pl.when((step > 0) & (step <= n))
    def _():
        ns[here] = norm()
        qs[here] = make(0, ns[here])
        leave(0, qs.at[here], q_ref, 0).start()
        leave(2, ns.at[here], n_ref, 0).start()

    @pl.when((step > n) & (step <= 2 * n))
    def _():
        ks[here] = make(1, ns[here])
        leave(1, ks.at[here], k_ref, 0).start()

    @pl.when((step > 2 * n) & (step <= ahead))
    def _():
        normed = norm()
        copies = []
        for i, dst in enumerate((q_ref, k_ref)):
            passing[i] = make(i, normed)
            copies.append(leave(3 + i, passing.at[i], dst, 1 + early // n))
            copies[-1].start()
        for one in copies:
            one.wait()

    first_part = (step > ahead) & (part < n)

    @pl.when(first_part & (seq == 0))
    def _():
        vs[here] = make(2, ns[here])
        leave(3, vs.at[here], v_ref, 0).start()

    @pl.when(first_part & (seq > 0))
    def _():
        @pl.when(part == 0)
        def _():
            for one in enter(seq):
                one.start()

        leave(2, ns.at[here], n_ref, seq - 1).wait()
        leave(3, vs.at[here], v_ref, seq - 1).wait()

        ns[here] = norm()
        vs[here] = make(2, ns[here])
        leave(2, ns.at[here], n_ref, seq).start()
        leave(3, vs.at[here], v_ref, seq).start()

        @pl.when(part == n - 1)
        def _():
            for one in enter(seq):
                one.wait()

    @pl.when((step > ahead) & (part == n) & (seq == 0))
    def _():
        for b in range(n):
            there = pl.ds(b * BLK, BLK)
            pltpu.make_async_copy(qs.at[there], q_ref.at[there], copy_sem.at[0, b]).wait()
            pltpu.make_async_copy(ks.at[there], k_ref.at[there], copy_sem.at[1, b]).wait()

    @pl.when((step > ahead) & (part >= n))
    def _():
        attend_block(seq, part - n, qs, ks, vs, seg_ref, o_ref, lse_ref, bias)

    reach = MAX_DOC // BLK + 1
    attention = [min(i + 1, reach) * ATTEND_COST for i in range(n)]
    lengths = [1.0] * (ahead + 1) + [1.0] * n + attention + ([1.6] * n + attention) * (seqs - 1)
    starts = (1, 1 + n, 1 + ahead, steps)
    for t in range(ready[0], work.ticks):
        m = sum(t >= one for one in ready)
        first, upto = ready[m - 1], (ready + [work.ticks])[m]
        span = lengths[starts[m - 1] : starts[m]]
        goal, at, passed = (t - first + 1) / (upto - first) * sum(span), starts[m - 1], span[0]
        while passed < goal - 1e-6 and at < starts[m] - 1:
            at += 1
            passed += lengths[at]
        pl.when(step == at)(functools.partial(work.tick, t))

    @pl.when(step == steps - 1)
    def _():
        work.end()
        for number in range(max(0, len(order) - 2), len(order)):
            stage_copy(number).wait()
        for one in held_out() + own_copies()[1]:
            one.wait()
        for b in range(n):
            for i, (src, dst) in ((2, (ns, n_ref)), (3, (vs, v_ref))):
                there = pl.ds(((seqs - 1) * n + b) * BLK, BLK)
                pltpu.make_async_copy(src.at[pl.ds(b * BLK, BLK)], dst.at[there], copy_sem.at[i, b]).wait()


def front(x, g1, c1, seg, biases, shards_, dp, tp):
    tokens, width = x.shape
    seqs, length = seg.shape
    n = length // BLK
    count, own = len(shards_), shards_[0].shape[0]
    bits, piece, steps, out = bits_of(dp), own // 8, 1 + 2 * n + (seqs - 1) * n + 2 * seqs * n, tp * own
    chunks = chunks_of(count, tp, piece)

    ahead = 2 * n + (seqs - 1) * n

    def unit(i):
        return jnp.maximum(i - 1 - ahead, 0)

    def early(i):
        opening = jnp.minimum(jnp.maximum(i - 1, 0), n - 1)
        later = n + jnp.maximum(i - 1 - 2 * n, 0)
        again = unit(i) // (2 * n) * n + jnp.minimum(unit(i) % (2 * n), n - 1)
        return (jnp.where(i <= 2 * n, opening, jnp.where(i <= ahead, later, jnp.where(unit(i) < 2 * n, ahead - n - 1, again))), 0)

    def late(size):
        return pl.BlockSpec((BLK, size), lambda i: (unit(i) // (2 * n) * n + jnp.maximum(unit(i) % (2 * n) - n, 0), 0))

    anywhere = pl.BlockSpec(memory_space=pl.ANY)
    pairs = seqs * n * 2.5 * BLK * BLK * (out // HEAD_DIM)
    return pl.pallas_call(
        functools.partial(front_kernel, bits, n, seqs, steps, chunks, count),
        grid=(steps,),
        in_specs=[
            pl.BlockSpec((BLK, width), early),
            whole(g1.shape),
            whole(c1.shape),
            whole(seg.shape),
            whole(biases.shape),
        ]
        + [anywhere] * count,
        out_specs=[anywhere] * 4 + [late(out), late(LANES), held(biases.shape[1:])] + [anywhere] * count,
        out_shape=[jax.ShapeDtypeStruct((tokens, width), BF)]
        + [jax.ShapeDtypeStruct((tokens, out), BF)] * 4
        + [jax.ShapeDtypeStruct((tokens, LANES), F32), jax.ShapeDtypeStruct(biases.shape[1:], F32)]
        + [jax.ShapeDtypeStruct((out, width), BF)] * count,
        scratch_shapes=[
            pltpu.VMEM((BLK, BLK + MAX_DOC), F32),
            pltpu.VMEM((3, out, width), BF),
            pltpu.VMEM((2, own, width), BF),
        ]
        + [pltpu.VMEM((length, out), BF)] * 3
        + [pltpu.VMEM((length, width), BF), pltpu.VMEM((2, BLK, out), BF)]
        + gather_scratch(count, tp, piece, width)
        + [
            pltpu.VMEM((2, 2, piece, width), BF),
            pltpu.VMEM(biases.shape, F32),
            pltpu.SemaphoreType.DMA((tp,)),
            pltpu.SemaphoreType.DMA((tp,)),
            pltpu.SemaphoreType.DMA((count,)),
            pltpu.SemaphoreType.DMA((count * tp,)),
            pltpu.SemaphoreType.DMA((2, 2)),
            pltpu.SemaphoreType.DMA((5, n)),
            pltpu.SemaphoreType.DMA((2,)),
        ],
        compiler_params=hosting(1, 0),
        cost_estimate=pl.CostEstimate(
            flops=int(6 * tokens * width * out + pairs * 8 * WIN),
            bytes_accessed=12 * tokens * width + 4 * count * out * width,
            transcendentals=int(pairs),
        ),
        name="front",
    )(x, g1, c1, seg, biases, *shards_)


def attend_back_kernel(
    steps, bits, q_ref, do_ref, o_ref, lse_ref, k_ref, v_ref, seg_ref, part_ref, dq_ref, dk_ref, dv_ref, go_ref, g1_ref, g2_ref,
    bias, dq_acc, lse_t, delta_t, *reduce_refs,
):
    s, j = pl.program_id(0), pl.program_id(1)
    n = pl.num_programs(1)
    length, width = q_ref.shape
    groups = width // GROUP
    ahead = MAX_DOC // BLK

    step = s * n + j

    def publish(m, total):
        (go_ref, g1_ref, g2_ref)[m][...] = total

    if bits is not None:
        work = Reduce(Place(bits), part_ref, reduce_refs, BACK_PLAN, publish)

        @pl.when(step == 0)
        def _():
            greet(work.greet())
            work.point(0)

    @pl.when(j == 0)
    def _():
        dq_acc[...] = jnp.zeros_like(dq_acc)
        head = lax.broadcasted_iota(jnp.int32, (16, width), 0)
        lane = lax.broadcasted_iota(jnp.int32, (16, width), 1)
        pick = jnp.where((lane >= head * HEAD_DIM) & (lane < (head + 1) * HEAD_DIM), 1.0, 0.0).astype(BF)
        for b in range(length // BLK):
            at = slice(b * BLK, (b + 1) * BLK)
            lse_t[:, at] = lse_ref[at, :].T[:16, :]
            prod = do_ref[at, :].astype(F32) * o_ref[at, :].astype(F32)
            high = prod.astype(BF)
            rest = (prod - high.astype(F32)).astype(BF)
            delta_t[:, at] = nt(pick, high) + nt(pick, rest)

    count = jnp.minimum(n - j, ahead + 1)
    start = pl.multiple_of(j * BLK, BLK)
    seg_col = column_of(seg_ref[pl.ds(s, 1), pl.ds(start, BLK)])

    def mask_of(blocks):
        queries = blocks * BLK
        row = lax.broadcasted_iota(jnp.int32, (BLK, queries), 0)
        col = lax.broadcasted_iota(jnp.int32, (BLK, queries), 1)
        allowed = (row <= col) & (seg_col == seg_ref[pl.ds(s, 1), pl.ds(start, queries)])
        bias[:, :queries] = jnp.where(allowed, 0.0, NEG)

    def heads(gi, blocks):
        queries = blocks * BLK
        span = pl.ds(start, queries)
        dks, dvs = [], []
        for h in range(HEADS_IN_GROUP):
            at, off = window_of(h)
            lanes = pl.ds(pl.multiple_of(gi * GROUP + at, LANES), WIN)
            mask = lane_mask(off)
            head = pl.ds(gi * HEADS_IN_GROUP + h, 1)
            k = k_ref[:, lanes]
            k = jnp.where(mask, k, jnp.zeros_like(k))
            v = v_ref[:, lanes]
            v = jnp.where(mask, v, jnp.zeros_like(v))
            q = q_ref[span, lanes]
            do = do_ref[span, lanes]
            t = nt(k, q) * (SCALE * LOG2E) + bias[:, :queries]
            p = jnp.exp2(t - lse_t[head, span])
            dvs.append(jnp.where(mask, nn(p.astype(BF), do), 0.0))
            ds = (p * (nt(v, do) - delta_t[head, span])).astype(BF)
            dks.append(jnp.where(mask, nn(ds, q), 0.0))
            dq_acc[span, lanes] += tn(ds, k)
        out = pl.ds(pl.multiple_of(gi * GROUP, LANES), GROUP)
        dk_ref[:, out] = (spread(dks) * SCALE).astype(BF)
        dv_ref[:, out] = spread(dvs).astype(BF)

    kinds = range(1, ahead + 2)
    for blocks in kinds:
        pl.when(count == blocks)(functools.partial(mask_of, blocks))

    def group(gi, carry):
        for blocks in kinds:
            pl.when(count == blocks)(functools.partial(heads, gi, blocks))
        if bits is not None:
            for p in range(1, work.points):
                pl.when(step * groups + gi + 1 == p)(functools.partial(work.point, p))
        return carry

    lax.fori_loop(0, groups, group, 0)

    if bits is not None:
        pl.when(step == steps - 1)(work.end)
    else:
        for m in range(3):
            publish(m, part_ref[m])

    @pl.when(j == n - 1)
    def _():
        dq_ref[...] = (dq_acc[...] * SCALE).astype(BF)


def attend_back(q, k, v, seg, mixed, d_mixed, lse, parts, bits):
    tokens, width = q.shape
    seqs, length = seg.shape
    own, model = parts.shape[1:]
    n = length // BLK
    spec_k = pl.BlockSpec((BLK, width), lambda s, j: (s * n + j, 0))
    spec_q = pl.BlockSpec((length, width), lambda s, j: (s, 0))
    pairs = seqs * n * 2.5 * BLK * BLK * (width // HEAD_DIM)
    hosted = bits is not None
    return pl.pallas_call(
        functools.partial(attend_back_kernel, seqs * n, bits),
        grid=(seqs, n),
        in_specs=[
            spec_q,
            spec_q,
            spec_q,
            pl.BlockSpec((length, LANES), lambda s, j: (s, 0)),
            spec_k,
            spec_k,
            whole(seg.shape),
            whole(parts.shape),
        ],
        out_specs=[spec_q, spec_k, spec_k] + [held((own, model))] * 3,
        scratch_shapes=[
            pltpu.VMEM((BLK, BLK + MAX_DOC), F32),
            pltpu.VMEM((length, width), F32),
            pltpu.VMEM((16, length), F32),
            pltpu.VMEM((16, length), F32),
        ]
        + (reduce_scratch(*parts.shape) if hosted else []),
        out_shape=[jax.ShapeDtypeStruct((tokens, width), BF)] * 3 + [jax.ShapeDtypeStruct((own, model), F32)] * 3,
        compiler_params=hosting(2, 3) if hosted else params(2),
        cost_estimate=pl.CostEstimate(
            flops=int(pairs * 20 * WIN), bytes_accessed=16 * tokens * width, transcendentals=int(pairs)
        ),
        name="attend_back",
    )(q, d_mixed, mixed, lse, k, v, seg, parts)


BACK_PLAN = (
    (1, 2, 4, 8, 10, 13, 16),
    (0, 1, 3, 4, 6, 12, 16),
    (3, 4, 9, 10, 11, 13, 16),
    (0, 2, 8, 9, 12, 14, 16),
    (0, 1, 3, 5, 12, 15, 16),
    (2, 3, 7, 9, 11, 13, 16),
)
FINISH_PLAN = (
    (0, 1, 6, 10, 13, 19, 26),
    (0, 1, 5, 9, 13, 18, 21),
    (5, 6, 12, 16, 19, 24, 26),
    (1, 3, 10, 17, 21, 25, 26),
    (2, 3, 9, 17, 20, 25, 26),
    (4, 5, 12, 16, 19, 23, 25),
)

OWN_ROW = 6


def middle_kernel(
    own, m_ref, x_ref, g_ref, w_ref, wo_ref, w1_ref, w2_ref, bo_ref, g2_ref, c2_ref, b2_ref, b1_ref,
    y_ref, dr_ref, dm_ref, part_ref, small_ref, rms_ref, vec, sums,
):
    i = pl.program_id(0)

    @pl.when(i == 0)
    def _():
        part_ref[...] = jnp.zeros_like(part_ref)
        vec[...] = jnp.zeros_like(vec)
        sums[...] = jnp.zeros_like(sums)

    mixed = m_ref[...]
    cot = g_ref[...]
    attended = nn(mixed, wo_ref[...]) + line(bo_ref)
    resid = x_ref[...].astype(F32) + attended
    hat, inv = normalize(resid)
    normed = (hat * line(g2_ref) + line(c2_ref)).astype(BF)
    pre = nt(normed, w1_ref[...]) + b1_ref[2:3]
    cdf = 0.5 + 0.5 * lax.erf(pre * math.sqrt(0.5))
    act = (pre * cdf).astype(BF)
    slope = cdf + pre * jnp.exp(-0.5 * pre * pre) * (1.0 / math.sqrt(2.0 * math.pi))
    branch = nn(act, w2_ref[...]) + line(b2_ref)
    output = resid + branch
    y_ref[...] = output.astype(BF)
    per = w_ref.shape[1] // BLK
    seq, at_ = i // per, i % per
    valid = w_ref[pl.ds(seq, 1), pl.ds(pl.multiple_of(at_ * BLK, BLK), BLK)].astype(F32)
    weight = column_of(valid)
    lane = lax.broadcasted_iota(jnp.int32, (1, LANES), 1)
    found = jnp.where(lane == 3, jnp.sum(valid, axis=1, keepdims=True), 0.0)
    for at, v in enumerate((attended, branch, output)):
        one = jnp.sum(weight * jnp.sum(v * v, axis=1, keepdims=True), axis=0, keepdims=True)
        found = jnp.where(lane == at, one, found)
    at_row = lax.broadcasted_iota(jnp.int32, sums.shape, 0) == seq
    sums[...] += jnp.where(at_row, found, 0.0)

    d_pre = (nt(cot, w2_ref[...]) * slope).astype(BF)
    part_ref[2] += tn(act[:, :own], cot)
    part_ref[1] += tn(d_pre[:, :own], normed)
    d_normed = nn(d_pre, w1_ref[...])
    d_hat = d_normed * line(g2_ref)
    grad = cot.astype(F32)
    d_resid = grad + inv * (
        d_hat - jnp.mean(d_hat, axis=1, keepdims=True) - hat * jnp.mean(d_hat * hat, axis=1, keepdims=True)
    )
    dr_ref[...] = d_resid
    low = d_resid.astype(BF)
    part_ref[0] += tn(mixed[:, :own], low)
    dm_ref[...] = nt(low, wo_ref[...]).astype(BF)
    for at, v in enumerate((grad, d_normed * hat, d_normed, low.astype(F32), d_pre.astype(F32))):
        vec[at] += fold8(v)

    @pl.when(i == pl.num_programs(0) - 1)
    def _():
        total = sums[...]
        counted = jnp.sum(jnp.where(lane == 3, total, 0.0), axis=1, keepdims=True)
        each = jnp.sqrt(total / (jnp.maximum(counted, 1.0) * attended.shape[1]))
        rms_ref[...] = each[: rms_ref.shape[0], : rms_ref.shape[1]]
        small_ref[...] = jnp.zeros_like(small_ref)
        for at, row in enumerate((0, 1, 2, 3, OWN_ROW)):
            small_ref[row : row + 1] = jnp.sum(vec[at], axis=0, keepdims=True)


def middle(own, mixed, x, cot, valid, wo, w1, w2, bo, g2, c2, b2, b1):
    tokens, width = x.shape
    inner, hidden = wo.shape[0], w1.shape[0]
    n = tokens // BLK
    return pl.pallas_call(
        functools.partial(middle_kernel, own),
        grid=(n,),
        in_specs=[rows(inner), rows(width), rows(width), whole(valid.shape)]
        + [whole((inner, width)), whole((hidden, width)), whole((hidden, width))]
        + [whole((width,))] * 4
        + [whole(b1.shape)],
        out_specs=[
            rows(width),
            rows(width),
            rows(inner),
            held((3, own, width)),
            held((8, width)),
            held((valid.shape[0], 3)),
        ],
        out_shape=[
            jax.ShapeDtypeStruct((tokens, width), BF),
            jax.ShapeDtypeStruct((tokens, width), F32),
            jax.ShapeDtypeStruct((tokens, inner), BF),
            jax.ShapeDtypeStruct((3, own, width), F32),
            jax.ShapeDtypeStruct((8, width), F32),
            jax.ShapeDtypeStruct((valid.shape[0], 3), F32),
        ],
        scratch_shapes=[pltpu.VMEM((5, 8, width), F32), pltpu.VMEM((-(-valid.shape[0] // 8) * 8, LANES), F32)],
        compiler_params=params(1),
        cost_estimate=pl.CostEstimate(
            flops=2 * tokens * width * (6 * width + 3 * own),
            bytes_accessed=14 * tokens * width + 6 * width * width,
            transcendentals=2 * tokens * hidden,
        ),
        name="middle",
    )(mixed, x, cot, valid, wo, w1, w2, bo, g2, c2, b2, b1)


def finish_kernel(
    bits, own, steps, dq_ref, dk_ref, dv_ref, x_ref, dr_ref, g_ref, wq_ref, wk_ref, wv_ref, mq_ref, mk_ref, mv_ref, n_ref, in_ref,
    dx_ref, gq_ref, gk_ref, gv_ref, small_ref, vec, part, acc, *refs,
):
    step = pl.program_id(0)
    grads = (mq_ref, mk_ref, mv_ref)
    count = len(grads)
    half = part.shape[2] // 2

    def publish(m, total):
        (gq_ref, gk_ref, gv_ref)[m][...] = total

    if bits is not None:
        place = Place(bits)
        work = Reduce(place, part, refs[:-3], FINISH_PLAN, publish)
        box, *sems = refs[-3:]

    @pl.when(step == 0)
    def _():
        vec[...] = jnp.zeros_like(vec)
        small_ref[...] = in_ref[...]
        if bits is not None:
            greet(place.plane())

    def weight_grad(m):
        mine = grads[m][:, :own]
        part[m] = tn(mine, n_ref[...])
        if m != 1:
            at = 0 if m == 0 else half
            small_ref[OWN_ROW + 1 : OWN_ROW + 2, at : at + own] = jnp.sum(mine.astype(F32), axis=0, keepdims=True)

    def points(first, at, every):
        if bits is not None:
            for p in range(first, work.points, every):
                if work.plan[p]:
                    pl.when(step == at + (p - first) // every)(functools.partial(work.point, p))

    for m in range(count):
        pl.when(step == m)(functools.partial(weight_grad, m))
        if bits is not None:
            pl.when(step == m)(functools.partial(work.point, m))

    @pl.when(step >= count)
    def _():
        acc[...] = nn(dq_ref[...], wq_ref[...])
        points(count, count, 3)
        acc[...] += nn(dk_ref[...], wk_ref[...])
        points(count + 1, count, 3)
        d_normed = acc[...] + nn(dv_ref[...], wv_ref[...])
        hat, inv = normalize(x_ref[...].astype(F32))
        d_hat = d_normed * line(g_ref)
        dx_ref[...] = dr_ref[...] + inv * (
            d_hat - jnp.mean(d_hat, axis=1, keepdims=True) - hat * jnp.mean(d_hat * hat, axis=1, keepdims=True)
        )
        vec[0] += fold8(d_normed * hat)
        vec[1] += fold8(d_normed)
        points(count + 2, count, 3)

    @pl.when(step == steps - 1)
    def _():
        for at in range(2):
            small_ref[4 + at : 5 + at] = jnp.sum(vec[at], axis=0, keepdims=True)
        if bits is None:
            for m in range(count):
                publish(m, part[m])
        else:
            copies = [send(small_ref, box.at[place.d], sems, i, peer) for i, peer in enumerate(place.plane())]
            for one in copies:
                one.start()
            box[place.d] = small_ref[...]
            for one in copies:
                one.wait_recv()
            for one in copies:
                one.wait_send()
            total = box[0]
            for i in range(1, 8):
                total = total + box[i]
            small_ref[...] = total
            work.end()


def finish(dq, dk, dv, x, d_resid, g1, wq, wk, wv, normed1, small, own, bits):
    tokens, width = x.shape
    inner = wq.shape[0]
    hosted = bits is not None
    count = 3
    pad = -(-own // LANES) * LANES
    mine = pl.BlockSpec((tokens, pad), lambda i: (0, 0), pipeline_mode=pl.Buffered(1))

    def late(size):
        return pl.BlockSpec((BLK, size), lambda i: (jnp.maximum(i - count, 0), 0))

    return pl.pallas_call(
        functools.partial(finish_kernel, bits, own, count + tokens // BLK),
        grid=(count + tokens // BLK,),
        in_specs=[late(inner)] * 3
        + [late(width), late(width), whole((width,))]
        + [whole((inner, width))] * 3
        + [mine] * 3
        + [whole((tokens, width)), whole((8, width))],
        out_specs=[late(width)] + [held((own, width))] * 3 + [held((8, width))],
        out_shape=[jax.ShapeDtypeStruct((tokens, width), F32)]
        + [jax.ShapeDtypeStruct((own, width), F32)] * 3
        + [jax.ShapeDtypeStruct((8, width), F32)],
        scratch_shapes=[
            pltpu.VMEM((2, 8, width), F32),
            pltpu.VMEM((count, own, width), F32),
            pltpu.VMEM((BLK, width), F32),
        ]
        + (
            reduce_scratch(count, own, width)
            + [pltpu.VMEM((8, 8, width), F32), pltpu.SemaphoreType.DMA((7,)), pltpu.SemaphoreType.DMA((7,))]
            if hosted
            else []
        ),
        compiler_params=hosting(1, 4) if hosted else params(1),
        cost_estimate=pl.CostEstimate(
            flops=6 * tokens * width * inner, bytes_accessed=16 * tokens * width + 6 * width * inner, transcendentals=0
        ),
        name="finish",
    )(dq, dk, dv, x, d_resid, g1, wq, wk, wv, dq, dk, dv, normed1, small)


def shards(dp, tp, x, g1, c1, wq, bq, wk, wv, bv, wo, bo, g2, c2, w1, b1, w2, b2, seg, valid, cot):
    tokens, width = x.shape
    seqs, length = seg.shape
    own = wq.shape[1]
    bits = bits_of(dp) if dp == 8 else None

    own_biases = jnp.stack([bq, bv, b1])
    own_biases = jnp.concatenate([jnp.tile(own_biases, (1, tp)), jnp.zeros((5, tp * own), F32)], axis=0)
    place = lax.broadcasted_iota(jnp.int32, (tp, 8, tp * own), 2) // own
    biases = jnp.where(place == lax.broadcasted_iota(jnp.int32, place.shape, 0), own_biases[None], 0.0)
    normed1, q, k, v, mixed, lse, vectors, fq, fk, fv, fo, f1, f2 = front(
        x, g1, c1, seg, biases, [wq.T, wk.T, wv.T, wo, w1.T, w2], dp, tp
    )

    y, d_resid, d_mixed, parts, small, rms = middle(
        own, mixed, x, cot, valid, fo, f1, f2, bo, g2, c2, b2, vectors
    )
    dq, dk, dv, gwo, gw1, gw2 = attend_back(q, k, v, seg, mixed, d_mixed, lse, parts, bits)
    grad_input, gq, gk, gv, small = finish(dq, dk, dv, x, d_resid, g1, fq, fk, fv, normed1, small, own, bits)
    if bits is None:
        gwo, gw1, gw2, gq, gk, gv, small = lax.psum((gwo, gw1, gw2, gq, gk, gv, small), "dp")

    gb2, gg2, gc2, gbo, gg1, gc1 = (small[r] for r in range(6))
    gb1 = small[OWN_ROW, :own]
    gbq = small[OWN_ROW + 1, :own]
    gbv = small[OWN_ROW + 1, width // 2 : width // 2 + own]
    return (y, grad_input, gg1, gc1, gq.T, gbq, gk.T, gv.T, gbv, gwo, gbo, gg2, gc2, gw1.T, gb1, gw2, gb2, rms)


def solution(mesh):
    dp, tp = mesh.shape["dp"], mesh.shape["tensor"]
    tok, col, row, vec, rep = P("dp", None), P(None, "tensor"), P("tensor", None), P("tensor"), P()
    return jax.shard_map(
        functools.partial(shards, dp, tp),
        mesh=mesh,
        in_specs=(tok, rep, rep, col, vec, col, col, vec, row, rep, rep, rep, col, vec, row, rep, tok, tok, tok),
        out_specs=(tok, tok, rep, rep, col, vec, col, col, vec, row, rep, rep, rep, col, vec, row, rep, tok),
        check_vma=False,
    )
```

```python
import functools
import math

import jax
import jax.numpy as jnp
from jax import lax
from jax.experimental import pallas as pl
from jax.experimental.pallas import tpu as pltpu
from jax.sharding import PartitionSpec as P

HEAD_DIM = 160
MAX_DOC = 512
EPS = 1e-05
NEG = -1e30
BLK = 256
WIN = 256
LANES = 128
SCALE = 1.0 / math.sqrt(HEAD_DIM)
LOG2E = 1.0 / math.log(2.0)
BF = jnp.bfloat16
F32 = jnp.float32
VMEM_MAX = 60 << 20


def nn(a, b):
    return lax.dot_general(a, b, (((1,), (0,)), ((), ())), preferred_element_type=F32)


def nt(a, b):
    return lax.dot_general(a, b, (((1,), (1,)), ((), ())), preferred_element_type=F32)


def tn(a, b):
    return lax.dot_general(a, b, (((0,), (0,)), ((), ())), preferred_element_type=F32)


def whole(shape):
    return pl.BlockSpec(shape, lambda *_: (0,) * len(shape), pipeline_mode=pl.Buffered(1))


def held(shape):
    return pl.BlockSpec(shape, lambda *_: (0,) * len(shape))


def rows(width):
    return pl.BlockSpec((BLK, width), lambda i: (i, 0))


def column_of(row):
    n = row.shape[1]
    eye = lax.broadcasted_iota(jnp.int32, (n, n), 0) == lax.broadcasted_iota(jnp.int32, (n, n), 1)
    return jnp.sum(jnp.where(eye, row, jnp.zeros_like(row)), axis=1, keepdims=True)


def line(ref):
    return ref[...].reshape(1, ref.shape[0])


def fold8(t):
    return jnp.sum(t.reshape(t.shape[0] // 8, 8, t.shape[1]), axis=0)


def params(grid, vmem=VMEM_MAX):
    return pltpu.CompilerParams(dimension_semantics=("arbitrary",) * grid, vmem_limit_bytes=vmem)


def hosting(grid, ident):
    return pltpu.CompilerParams(
        dimension_semantics=("arbitrary",) * grid,
        vmem_limit_bytes=VMEM_MAX,
        collective_id=ident,
        has_side_effects=True,
    )


def sibling(index, bit):
    return index + bit - 2 * bit * (index // bit % 2)


class Place:
    def __init__(self, bits):
        self.d, self.z = lax.axis_index("dp"), lax.axis_index("tensor")
        self.core = self.d % 2
        self.a, self.b = (self.d // bit % 2 for bit in bits)
        self.spot = self.a + 2 * self.b
        self.on_core = {"dp": sibling(self.d, 1), "tensor": self.z}
        self.on_a, self.on_b = ({"dp": sibling(self.d, bit), "tensor": self.z} for bit in bits)
        peers = (None, sibling(self.z, 1), sibling(self.z, 2), sibling(sibling(self.z, 1), 2))
        self.on_z = [None] + [{"dp": self.d, "tensor": peer} for peer in peers[1:]]

    def plane(self):
        return [{"dp": (self.d + step) % 8, "tensor": self.z} for step in range(1, 8)]


def greet(targets):
    barrier = pltpu.get_barrier_semaphore()
    for target in targets:
        pl.semaphore_signal(barrier, inc=1, device_id=target, device_id_type=pl.DeviceIdType.MESH)
    pl.semaphore_wait(barrier, len(targets))


def send(src, dst, sems, at, target):
    return pltpu.make_async_remote_copy(
        src_ref=src,
        dst_ref=dst,
        send_sem=sems[0].at[at],
        recv_sem=sems[1].at[at],
        device_id=target,
        device_id_type=pl.DeviceIdType.MESH,
    )


def bits_of(dp):
    return (2, 4) if dp == 8 else (2, 8)


def chunks_of(count, tp, piece):
    cut = (piece * 5 // 8) // 8 * 8
    orders = [[1 + (j + m % 2) % (tp - 1) for j in range(tp - 1)] for m in range(count)]
    return [(m, j, *span) for m in range(count) for span in ((0, cut), (cut, piece)) for j in orders[m]]


AHEAD = 6
LAG = 2
ATTEND_COST = 0.9


class Gather:
    def __init__(self, place, chunks, mine, land, sems, publish):
        self.place, self.chunks, self.mine, self.land, self.sems, self.publish = place, chunks, mine, land, sems, publish
        self.ticks = len(chunks) + 3 * LAG
        self.got = {}

    def slot(self, k, where, low=None, high=None):
        m, j, r0, r1 = self.chunks[k]
        low, high = (r0 if low is None else low), (r1 if high is None else high)
        return self.land.at[m, j - 1, self.place.core, where, pl.ds(low, high - low)]

    def middle(self, k):
        _, _, r0, r1 = self.chunks[k]
        half = (r1 - r0) // 2
        return r0 + (half + 7 if k % 2 else half) // 8 * 8

    def over_z(self, k):
        m, j, r0, r1 = self.chunks[k]
        spots = [self.place.spot] + ([3 - self.place.spot] if j == 1 else [])
        return [
            send(self.mine.at[m, i, pl.ds(r0, r1 - r0)], self.slot(k, spot), self.sems, (k, i), self.place.on_z[j])
            for i, spot in enumerate(spots)
        ]

    def over_a(self, k):
        here = self.slot(k, self.place.spot)
        return send(here, here, self.sems, (k, 2), self.place.on_a)

    def over_b(self, k):
        here = self.slot(k, self.place.spot)
        return send(here, here, self.sems, (k, 3), self.place.on_b)

    def on_a(self, k):
        part = self.slot(k, sibling(self.place.spot, 2), None, self.middle(k))
        return send(part, part, self.sems, (k, 4), self.place.on_a)

    def on_b(self, k):
        part = self.slot(k, sibling(self.place.spot, 1), self.middle(k), None)
        return send(part, part, self.sems, (k, 5), self.place.on_b)

    def relays(self, k):
        return [] if self.chunks[k][1] == 1 else [self.on_a(k), self.on_b(k)]

    def swap(self, k):
        m, j, r0, r1 = self.chunks[k]
        part = self.land.at[m, j - 1, self.place.core, :, pl.ds(r0, r1 - r0)]
        return send(part, part, self.sems, (k, 6), self.place.on_core)

    def start_z(self, k):
        for one in self.over_z(k):
            one.start()

    def tick(self, t):
        total = len(self.chunks)
        if 0 <= t < total:
            for one in self.over_z(t):
                one.wait_recv()
            self.over_a(t).start()
            self.over_b(t).start()
            if t + AHEAD < total:
                self.start_z(t + AHEAD)
        k = t - LAG
        if 0 <= k < total:
            self.over_b(k).wait_recv()
            for one in self.relays(k)[:1]:
                one.start()
            self.over_a(k).wait_recv()
            for one in self.relays(k)[1:]:
                one.start()
        k = t - 2 * LAG
        if 0 <= k < total:
            for one in self.relays(k):
                one.wait_recv()
            self.swap(k).start()
        k = t - 3 * LAG
        if 0 <= k < total:
            self.swap(k).wait_recv()
            m, j, r0, r1 = self.chunks[k]
            piece = self.land.shape[4]
            self.got[m, j] = self.got.get((m, j), 0) + r1 - r0
            if self.got[m, j] == piece:
                self.publish(m, j, self.land[m, j - 1].reshape(8 * piece, -1).astype(BF))

    def end(self):
        for k in range(len(self.chunks)):
            for one in self.over_z(k) + self.relays(k) + [self.over_a(k), self.over_b(k), self.swap(k)]:
                one.wait_send()


def gather_scratch(count, tp, piece, width):
    total = len(chunks_of(count, tp, piece))
    return [
        pltpu.VMEM((count, tp - 1, 2, 4, piece, width), F32),
        pltpu.SemaphoreType.DMA((total, 7)),
        pltpu.SemaphoreType.DMA((total, 7)),
        pltpu.VMEM((count, 2, piece, width), F32),
    ]


class Reduce:
    def __init__(self, place, part, scratch, plan, publish):
        self.place, self.part, self.publish = place, part, publish
        self.count, self.own, self.width = part.shape
        self.out, self.half, self.first, self.second, *self.sems = scratch
        self.points = 1 + max(row[-1] for row in plan)
        self.plan = {p: [] for p in range(self.points)}
        for k, row in enumerate(plan):
            for stage, p in enumerate(row):
                self.plan[p].append((k, stage))
        for p, found in self.plan.items():
            found.sort(key=lambda one: (one[1] if p == self.points - 1 else -one[1], one[0]))
        ends = [k for p in range(self.points) for k, stage in self.plan[p] if stage == 6]
        self.closing = [max(2 * m, 2 * m + 1, key=ends.index) for m in range(self.count)]

    def greet(self):
        return [self.place.on_a, self.place.on_b, self.place.on_core]

    def rows_of(self, size, index, count):
        return pl.ds(pl.multiple_of(size * index, 8), count)

    def way(self, k):
        p = self.place
        return (p.a, p.on_a, p.b, p.on_b) if k % 2 == 0 else (p.b, p.on_b, p.a, p.on_a)

    def columns(self, bit):
        lanes = self.width // 2
        return pl.ds(pl.multiple_of(lanes * bit, LANES), lanes)

    def out_rows(self, k, bit):
        piece = self.own // 8
        return self.rows_of(piece, 4 * self.place.core + 2 * (k % 2) + bit, piece)

    def quarter(self, k, core):
        size = self.own // 4
        return self.rows_of(size, 2 * core + k % 2, size)

    def copy(self, k, stage):
        place, m, piece = self.place, k // 2, self.own // 8
        bit, peer, bit2, peer2 = self.way(k)
        if stage == 0:
            src, dst, to = self.part.at[m, self.quarter(k, 1 - place.core)], self.half.at[k], place.on_core
        elif stage == 1:
            src, dst, to = self.half.at[k, self.rows_of(piece, 1 - bit, piece)], self.first.at[k], peer
        elif stage == 2:
            src, dst, to = self.half.at[k, self.rows_of(piece, bit, piece), self.columns(1 - bit2)], self.second.at[k], peer2
        elif stage == 3:
            src = dst = self.out.at[m, self.out_rows(k, bit), self.columns(bit2)]
            to = peer2
        elif stage == 4:
            src = dst = self.out.at[m, self.out_rows(k, bit)]
            to = peer
        else:
            src = dst = self.out.at[m, self.quarter(k, place.core)]
            to = place.on_core
        return send(src, dst, self.sems, (k, stage), to)

    def step(self, k, stage):
        m, piece = k // 2, self.own // 8
        bit, _, bit2, _ = self.way(k)
        mine = self.rows_of(piece, bit, piece)
        if stage >= 1:
            self.copy(k, stage - 1).wait_recv()
        if stage == 1:
            self.half[k] = self.part[m, self.quarter(k, self.place.core)] + self.half[k]
        if stage == 2:
            self.half[k, mine] = self.half[k, mine] + self.first[k]
        if stage == 3:
            columns = self.columns(bit2)
            self.out[m, self.out_rows(k, bit), columns] = self.half[k, mine, columns] + self.second[k]
        if stage < 6:
            self.copy(k, stage).start()
            return
        if k == self.closing[m]:
            self.publish(m, self.out[m])

    def point(self, p):
        for k, stage in self.plan[p]:
            self.step(k, stage)

    def end(self):
        for k in range(2 * self.count):
            for stage in range(6):
                self.copy(k, stage).wait_send()


def reduce_scratch(count, own, width):
    chunks = 2 * count
    return [
        pltpu.VMEM((count, own, width), F32),
        pltpu.VMEM((chunks, own // 4, width), F32),
        pltpu.VMEM((chunks, own // 8, width), F32),
        pltpu.VMEM((chunks, own // 8, width // 2), F32),
        pltpu.SemaphoreType.DMA((chunks, 6)),
        pltpu.SemaphoreType.DMA((chunks, 6)),
    ]


def normalize(v):
    center = v - jnp.mean(v, axis=-1, keepdims=True)
    inv = lax.rsqrt(jnp.mean(center * center, axis=-1, keepdims=True) + EPS)
    return center * inv, inv


HEADS_IN_GROUP = 4
GROUP = HEADS_IN_GROUP * HEAD_DIM


def window_of(head):
    low = head * HEAD_DIM
    start = low // LANES * LANES
    return start, low - start


def lane_mask(offset):
    lane = lax.broadcasted_iota(jnp.int32, (1, WIN), 1)
    return (lane >= offset) & (lane < offset + HEAD_DIM)


def spread(parts):
    tiles = [None] * (GROUP // LANES)
    for head, part in enumerate(parts):
        first = window_of(head)[0] // LANES
        for half in range(WIN // LANES):
            piece = part[:, half * LANES : (half + 1) * LANES]
            at = first + half
            tiles[at] = piece if tiles[at] is None else tiles[at] + piece
    return jnp.concatenate(tiles, axis=1)


def attend_block(seq, i, q_ref, k_ref, v_ref, seg_ref, o_ref, lse_ref, bias):
    groups = q_ref.shape[1] // GROUP
    back = MAX_DOC // BLK
    here = pl.ds(pl.multiple_of(i * BLK, BLK), BLK)
    row = pl.ds(seq, 1)
    seg_col = column_of(seg_ref[row, here])

    def body(blocks):
        keys = blocks * BLK
        start = pl.multiple_of((i + 1 - blocks) * BLK, BLK)
        query = i * BLK + lax.broadcasted_iota(jnp.int32, (BLK, keys), 0)
        key = start + lax.broadcasted_iota(jnp.int32, (BLK, keys), 1)
        allowed = (query >= key) & (seg_col == seg_ref[row, pl.ds(start, keys)])
        bias[:, :keys] = jnp.where(allowed, 0.0, NEG)

        def group(gi, _):
            parts = []
            lse = lse_ref[...]
            head_lane = lax.broadcasted_iota(jnp.int32, (1, LANES), 1)
            for h in range(HEADS_IN_GROUP):
                at, off = window_of(h)
                lanes = pl.ds(pl.multiple_of(gi * GROUP + at, LANES), WIN)
                mask = lane_mask(off)
                q = q_ref[here, lanes]
                q = jnp.where(mask, q, jnp.zeros_like(q))
                t = nt(q, k_ref[pl.ds(start, keys), lanes]) * (SCALE * LOG2E) + bias[:, :keys]
                top = jnp.max(t, axis=1, keepdims=True)
                p = jnp.exp2(t - top)
                total = jnp.sum(p, axis=1, keepdims=True)
                o = nn(p.astype(BF), v_ref[pl.ds(start, keys), lanes])
                parts.append(jnp.where(mask, o * (1.0 / total), 0.0))
                lse = jnp.where(head_lane == gi * HEADS_IN_GROUP + h, top + jnp.log2(total), lse)
            lse_ref[...] = lse
            o_ref[:, pl.ds(pl.multiple_of(gi * GROUP, LANES), GROUP)] = spread(parts).astype(BF)
            return 0

        lax.fori_loop(0, groups, group, 0)

    lse_ref[...] = jnp.zeros_like(lse_ref)
    count = jnp.minimum(i, back) + 1
    for blocks in range(1, back + 2):
        pl.when(count == blocks)(functools.partial(body, blocks))


def front_kernel(
    bits, n, seqs, steps, chunks, count, x_ref, g_ref, c_ref, seg_ref, bias_ref, *refs
):
    local, refs = refs[:count], refs[count:]
    n_ref, q_ref, k_ref, v_ref, o_ref, lse_ref, vec_ref, *refs = refs
    full, refs = refs[:count], refs[count:]
    bias, weights, stage, qs, ks, vs, ns, passing, fresh, land, gather_s, gather_r, mine, raw, bias_in, bias_s, bias_r, local_sem, out_sem, raw_sem, copy_sem, back_sem = refs
    own = local[0].shape[0]
    held_here = weights.shape[0]
    step = pl.program_id(0)
    place = Place(bits)
    shards_ = len(place.on_z)
    ahead = 2 * n + (seqs - 1) * n
    order = {}

    def rows_of(j):
        return pl.ds(j * own, own)

    def stage_copy(number):
        m, j = order[number]
        return pltpu.make_async_copy(stage.at[number % 2], full[m].at[rows_of(j)], out_sem.at[number])

    def publish(m, j, shard):
        if m < held_here:
            weights[m, rows_of(j)] = shard
            return
        number = len(order)
        order[number] = m, j
        if number >= 2:
            stage_copy(number - 2).wait()
        stage[number % 2] = shard
        stage_copy(number).start()

    work = Gather(place, chunks, mine, land, (gather_s, gather_r), publish)
    ready = [max(k for k, chunk in enumerate(chunks) if chunk[0] == m) + 3 * LAG + 1 for m in range(held_here)]

    def own_copies():
        held_ = [pltpu.make_async_copy(local[m], weights.at[m, rows_of(0)], local_sem.at[m]) for m in range(held_here)]
        rest = [
            pltpu.make_async_copy(local[m], full[m].at[rows_of(0)], local_sem.at[m]) for m in range(held_here, count)
        ]
        return held_, rest

    def held_out():
        return [pltpu.make_async_copy(weights.at[m], full[m], local_sem.at[m]) for m in range(held_here)]

    @pl.when(step == 0)
    def _():
        held_, rest = own_copies()
        piece = own // 8
        raws = [
            [
                pltpu.make_async_copy(
                    local[m].at[pl.ds(pl.multiple_of(piece * (4 * place.core + spot), 8), piece)],
                    raw.at[m % 2, i],
                    raw_sem.at[m % 2, i],
                )
                for i, spot in enumerate((place.spot, 3 - place.spot))
            ]
            for m in range(count)
        ]
        for one in sum(raws[:2], []) + held_ + rest:
            one.start()
        greet(place.on_z[1:] + [place.on_a, place.on_b, place.on_core])
        for m in range(count):
            for i, one in enumerate(raws[m]):
                one.wait()
                mine[m, i] = raw[m % 2, i].astype(F32)
            for one in raws[m + 2] if m + 2 < count else []:
                one.start()
            if m == 0:
                for k in range(AHEAD):
                    work.start_z(k)
        vectors = [
            send(bias_ref.at[j], bias_in.at[j], (bias_s, bias_r), j, place.on_z[j]) for j in range(1, shards_)
        ]
        for one in vectors:
            one.start()
        for t in range(ready[0]):
            work.tick(t)
        for one in vectors:
            one.wait()
        vec_ref[...] = sum((bias_in[j] for j in range(1, shards_)), bias_ref[0])
        for one in held_:
            one.wait()

    @pl.when(step == 1 + ahead)
    def _():
        for one in held_out():
            one.start()

    unit = jnp.maximum(step - 1 - ahead, 0)
    seq, part = unit // (2 * n), unit % (2 * n)
    early = jnp.maximum(step - 1 - 2 * n, 0)
    block = jnp.where(step <= 2 * n, (step - 1 + n) % n, jnp.where(step <= ahead, early % n, part % n))
    here = pl.ds(pl.multiple_of(block * BLK, BLK), BLK)

    def leave(i, src, dst, sequence):
        there = pl.ds(pl.multiple_of((sequence * n + block) * BLK, BLK), BLK)
        return pltpu.make_async_copy(src, dst.at[there], copy_sem.at[i, block])

    def enter(sequence):
        there = pl.ds(pl.multiple_of(sequence * n * BLK, BLK), n * BLK)
        return [
            pltpu.make_async_copy(src.at[there], dst, back_sem.at[i]) for i, (src, dst) in enumerate(((q_ref, qs), (k_ref, ks)))
        ]

    first = (step > 0) & (step <= n)
    second = (step > n) & (step <= 2 * n)
    passing_by = (step > 2 * n) & (step <= ahead)
    third = (step > ahead) & (part < n)
    again = third & (seq > 0)

    @pl.when(again)
    def _():
        @pl.when(part == 0)
        def _():
            for one in enter(seq):
                one.start()

        leave(2, ns.at[here], n_ref, seq - 1).wait()
        leave(3, vs.at[here], v_ref, seq - 1).wait()

    @pl.when(first | passing_by | again)
    def _():
        hat, _ = normalize(x_ref[...].astype(F32))
        fresh[...] = (hat * line(g_ref) + line(c_ref)).astype(BF)

    @pl.when(first | again)
    def _():
        ns[here] = fresh[...]

    @pl.when(second | (third & (seq == 0)))
    def _():
        fresh[...] = ns[here]

    @pl.when(first | second | passing_by | third)
    def _():
        low = jnp.where(third, 2, jnp.where(second, 1, 0))

        def make(m, carry):
            row = jnp.where(m == 0, 0, jnp.where(m == 1, 3, 1))
            passing[m % 2] = (nt(fresh[...], weights[m]) + vec_ref[pl.ds(row, 1)]).astype(BF)
            return carry

        lax.fori_loop(low, low + jnp.where(passing_by, 2, 1), make, 0)

    @pl.when(first)
    def _():
        qs[here] = passing[0]
        leave(0, qs.at[here], q_ref, 0).start()
        leave(2, ns.at[here], n_ref, 0).start()

    @pl.when(second)
    def _():
        ks[here] = passing[1]
        leave(1, ks.at[here], k_ref, 0).start()

    @pl.when(passing_by)
    def _():
        copies = [leave(3 + i, passing.at[i], dst, 1 + early // n) for i, dst in enumerate((q_ref, k_ref))]
        for one in copies:
            one.start()
        for one in copies:
            one.wait()

    @pl.when(third)
    def _():
        vs[here] = passing[0]
        leave(3, vs.at[here], v_ref, seq).start()

    @pl.when(again)
    def _():
        leave(2, ns.at[here], n_ref, seq).start()

        @pl.when(part == n - 1)
        def _():
            for one in enter(seq):
                one.wait()

    @pl.when((step > ahead) & (part == n) & (seq == 0))
    def _():
        for b in range(n):
            there = pl.ds(b * BLK, BLK)
            pltpu.make_async_copy(qs.at[there], q_ref.at[there], copy_sem.at[0, b]).wait()
            pltpu.make_async_copy(ks.at[there], k_ref.at[there], copy_sem.at[1, b]).wait()

    @pl.when((step > ahead) & (part >= n))
    def _():
        attend_block(seq, part - n, qs, ks, vs, seg_ref, o_ref, lse_ref, bias)

    reach = MAX_DOC // BLK + 1
    attention = [min(i + 1, reach) * ATTEND_COST for i in range(n)]
    lengths = [1.0] * (ahead + 1) + [1.0] * n + attention + ([1.6] * n + attention) * (seqs - 1)
    starts = (1, 1 + n, 1 + ahead, steps)
    for t in range(ready[0], work.ticks):
        m = sum(t >= one for one in ready)
        first, upto = ready[m - 1], (ready + [work.ticks])[m]
        span = lengths[starts[m - 1] : starts[m]]
        goal, at, passed = (t - first + 1) / (upto - first) * sum(span), starts[m - 1], span[0]
        while passed < goal - 1e-6 and at < starts[m] - 1:
            at += 1
            passed += lengths[at]
        pl.when(step == at)(functools.partial(work.tick, t))

    @pl.when(step == steps - 1)
    def _():
        work.end()
        for number in range(max(0, len(order) - 2), len(order)):
            stage_copy(number).wait()
        for one in held_out() + own_copies()[1]:
            one.wait()
        for b in range(n):
            for i, (src, dst) in ((2, (ns, n_ref)), (3, (vs, v_ref))):
                there = pl.ds(((seqs - 1) * n + b) * BLK, BLK)
                pltpu.make_async_copy(src.at[pl.ds(b * BLK, BLK)], dst.at[there], copy_sem.at[i, b]).wait()


def front(x, g1, c1, seg, biases, shards_, dp, tp):
    tokens, width = x.shape
    seqs, length = seg.shape
    n = length // BLK
    count, own = len(shards_), shards_[0].shape[0]
    bits, piece, steps, out = bits_of(dp), own // 8, 1 + 2 * n + (seqs - 1) * n + 2 * seqs * n, tp * own
    chunks = chunks_of(count, tp, piece)

    ahead = 2 * n + (seqs - 1) * n

    def unit(i):
        return jnp.maximum(i - 1 - ahead, 0)

    def early(i):
        opening = jnp.minimum(jnp.maximum(i - 1, 0), n - 1)
        later = n + jnp.maximum(i - 1 - 2 * n, 0)
        again = unit(i) // (2 * n) * n + jnp.minimum(unit(i) % (2 * n), n - 1)
        return (jnp.where(i <= 2 * n, opening, jnp.where(i <= ahead, later, jnp.where(unit(i) < 2 * n, ahead - n - 1, again))), 0)

    def late(size):
        return pl.BlockSpec((BLK, size), lambda i: (unit(i) // (2 * n) * n + jnp.maximum(unit(i) % (2 * n) - n, 0), 0))

    anywhere = pl.BlockSpec(memory_space=pl.ANY)
    pairs = seqs * n * 2.5 * BLK * BLK * (out // HEAD_DIM)
    return pl.pallas_call(
        functools.partial(front_kernel, bits, n, seqs, steps, chunks, count),
        grid=(steps,),
        in_specs=[
            pl.BlockSpec((BLK, width), early),
            whole(g1.shape),
            whole(c1.shape),
            whole(seg.shape),
            whole(biases.shape),
        ]
        + [anywhere] * count,
        out_specs=[anywhere] * 4 + [late(out), late(LANES), held(biases.shape[1:])] + [anywhere] * count,
        out_shape=[jax.ShapeDtypeStruct((tokens, width), BF)]
        + [jax.ShapeDtypeStruct((tokens, out), BF)] * 4
        + [jax.ShapeDtypeStruct((tokens, LANES), F32), jax.ShapeDtypeStruct(biases.shape[1:], F32)]
        + [jax.ShapeDtypeStruct((out, width), BF)] * count,
        scratch_shapes=[
            pltpu.VMEM((BLK, BLK + MAX_DOC), F32),
            pltpu.VMEM((3, out, width), BF),
            pltpu.VMEM((2, own, width), BF),
        ]
        + [pltpu.VMEM((length, out), BF)] * 3
        + [pltpu.VMEM((length, width), BF), pltpu.VMEM((2, BLK, out), BF), pltpu.VMEM((BLK, width), BF)]
        + gather_scratch(count, tp, piece, width)
        + [
            pltpu.VMEM((2, 2, piece, width), BF),
            pltpu.VMEM(biases.shape, F32),
            pltpu.SemaphoreType.DMA((tp,)),
            pltpu.SemaphoreType.DMA((tp,)),
            pltpu.SemaphoreType.DMA((count,)),
            pltpu.SemaphoreType.DMA((count * tp,)),
            pltpu.SemaphoreType.DMA((2, 2)),
            pltpu.SemaphoreType.DMA((5, n)),
            pltpu.SemaphoreType.DMA((2,)),
        ],
        compiler_params=hosting(1, 0),
        cost_estimate=pl.CostEstimate(
            flops=int(6 * tokens * width * out + pairs * 8 * WIN),
            bytes_accessed=12 * tokens * width + 4 * count * out * width,
            transcendentals=int(pairs),
        ),
        name="front",
    )(x, g1, c1, seg, biases, *shards_)


def attend_back_kernel(
    steps, bits, q_ref, do_ref, o_ref, lse_ref, k_ref, v_ref, seg_ref, part_ref, dq_ref, dk_ref, dv_ref, go_ref, g1_ref, g2_ref,
    bias, dq_acc, lse_t, delta_t, *reduce_refs,
):
    s, j = pl.program_id(0), pl.program_id(1)
    n = pl.num_programs(1)
    length, width = q_ref.shape
    groups = width // GROUP
    ahead = MAX_DOC // BLK

    step = s * n + j

    def publish(m, total):
        (go_ref, g1_ref, g2_ref)[m][...] = total

    if bits is not None:
        work = Reduce(Place(bits), part_ref, reduce_refs, BACK_PLAN, publish)

        @pl.when(step == 0)
        def _():
            greet(work.greet())
            work.point(0)

    @pl.when(j == 0)
    def _():
        dq_acc[...] = jnp.zeros_like(dq_acc)
        head = lax.broadcasted_iota(jnp.int32, (16, width), 0)
        lane = lax.broadcasted_iota(jnp.int32, (16, width), 1)
        pick = jnp.where((lane >= head * HEAD_DIM) & (lane < (head + 1) * HEAD_DIM), 1.0, 0.0).astype(BF)
        for b in range(length // BLK):
            at = slice(b * BLK, (b + 1) * BLK)
            lse_t[:, at] = lse_ref[at, :].T[:16, :]
            prod = do_ref[at, :].astype(F32) * o_ref[at, :].astype(F32)
            high = prod.astype(BF)
            rest = (prod - high.astype(F32)).astype(BF)
            delta_t[:, at] = nt(pick, high) + nt(pick, rest)

    count = jnp.minimum(n - j, ahead + 1)
    start = pl.multiple_of(j * BLK, BLK)
    seg_col = column_of(seg_ref[pl.ds(s, 1), pl.ds(start, BLK)])

    def mask_of(blocks):
        queries = blocks * BLK
        row = lax.broadcasted_iota(jnp.int32, (BLK, queries), 0)
        col = lax.broadcasted_iota(jnp.int32, (BLK, queries), 1)
        allowed = (row <= col) & (seg_col == seg_ref[pl.ds(s, 1), pl.ds(start, queries)])
        bias[:, :queries] = jnp.where(allowed, 0.0, NEG)

    def heads(gi, blocks):
        queries = blocks * BLK
        span = pl.ds(start, queries)
        dks, dvs = [], []
        for h in range(HEADS_IN_GROUP):
            at, off = window_of(h)
            lanes = pl.ds(pl.multiple_of(gi * GROUP + at, LANES), WIN)
            mask = lane_mask(off)
            head = pl.ds(gi * HEADS_IN_GROUP + h, 1)
            k = k_ref[:, lanes]
            k = jnp.where(mask, k, jnp.zeros_like(k))
            v = v_ref[:, lanes]
            v = jnp.where(mask, v, jnp.zeros_like(v))
            q = q_ref[span, lanes]
            do = do_ref[span, lanes]
            t = nt(k, q) * (SCALE * LOG2E) + bias[:, :queries]
            p = jnp.exp2(t - lse_t[head, span])
            dvs.append(jnp.where(mask, nn(p.astype(BF), do), 0.0))
            ds = (p * (nt(v, do) - delta_t[head, span])).astype(BF)
            dks.append(jnp.where(mask, nn(ds, q), 0.0))
            dq_acc[span, lanes] += tn(ds, k)
        out = pl.ds(pl.multiple_of(gi * GROUP, LANES), GROUP)
        dk_ref[:, out] = (spread(dks) * SCALE).astype(BF)
        dv_ref[:, out] = spread(dvs).astype(BF)

    kinds = range(1, ahead + 2)
    for blocks in kinds:
        pl.when(count == blocks)(functools.partial(mask_of, blocks))

    def group(gi, carry):
        for blocks in kinds:
            pl.when(count == blocks)(functools.partial(heads, gi, blocks))
        if bits is not None:
            for p in range(1, work.points):
                pl.when(step * groups + gi + 1 == p)(functools.partial(work.point, p))
        return carry

    lax.fori_loop(0, groups, group, 0)

    if bits is not None:
        pl.when(step == steps - 1)(work.end)
    else:
        for m in range(3):
            publish(m, part_ref[m])

    @pl.when(j == n - 1)
    def _():
        dq_ref[...] = (dq_acc[...] * SCALE).astype(BF)


def attend_back(q, k, v, seg, mixed, d_mixed, lse, parts, bits):
    tokens, width = q.shape
    seqs, length = seg.shape
    own, model = parts.shape[1:]
    n = length // BLK
    spec_k = pl.BlockSpec((BLK, width), lambda s, j: (s * n + j, 0))
    spec_q = pl.BlockSpec((length, width), lambda s, j: (s, 0))
    pairs = seqs * n * 2.5 * BLK * BLK * (width // HEAD_DIM)
    hosted = bits is not None
    return pl.pallas_call(
        functools.partial(attend_back_kernel, seqs * n, bits),
        grid=(seqs, n),
        in_specs=[
            spec_q,
            spec_q,
            spec_q,
            pl.BlockSpec((length, LANES), lambda s, j: (s, 0)),
            spec_k,
            spec_k,
            whole(seg.shape),
            whole(parts.shape),
        ],
        out_specs=[spec_q, spec_k, spec_k] + [held((own, model))] * 3,
        scratch_shapes=[
            pltpu.VMEM((BLK, BLK + MAX_DOC), F32),
            pltpu.VMEM((length, width), F32),
            pltpu.VMEM((16, length), F32),
            pltpu.VMEM((16, length), F32),
        ]
        + (reduce_scratch(*parts.shape) if hosted else []),
        out_shape=[jax.ShapeDtypeStruct((tokens, width), BF)] * 3 + [jax.ShapeDtypeStruct((own, model), F32)] * 3,
        compiler_params=hosting(2, 3) if hosted else params(2),
        cost_estimate=pl.CostEstimate(
            flops=int(pairs * 20 * WIN), bytes_accessed=16 * tokens * width, transcendentals=int(pairs)
        ),
        name="attend_back",
    )(q, d_mixed, mixed, lse, k, v, seg, parts)


BACK_PLAN = (
    (0, 1, 4, 7, 9, 11, 14),
    (0, 2, 4, 6, 10, 13, 14),
    (1, 2, 5, 8, 10, 13, 14),
    (0, 1, 3, 8, 11, 14, 16),
    (0, 5, 9, 10, 13, 15, 16),
    (0, 3, 6, 11, 13, 15, 16),
)
FINISH_PLAN = (
    (0, 1, 6, 10, 13, 19, 26),
    (0, 1, 5, 9, 13, 18, 21),
    (5, 6, 12, 16, 19, 24, 26),
    (1, 3, 10, 17, 21, 25, 26),
    (2, 3, 9, 17, 20, 25, 26),
    (4, 5, 12, 16, 19, 23, 25),
)

OWN_ROW = 6


def middle_kernel(
    own, m_ref, x_ref, g_ref, w_ref, wo_ref, w1_ref, w2_ref, bo_ref, g2_ref, c2_ref, b2_ref, b1_ref,
    y_ref, dr_ref, dm_ref, part_ref, small_ref, rms_ref, vec, sums,
):
    i = pl.program_id(0)

    @pl.when(i == 0)
    def _():
        part_ref[...] = jnp.zeros_like(part_ref)
        vec[...] = jnp.zeros_like(vec)
        sums[...] = jnp.zeros_like(sums)

    mixed = m_ref[...]
    cot = g_ref[...]
    attended = nn(mixed, wo_ref[...]) + line(bo_ref)
    resid = x_ref[...].astype(F32) + attended
    hat, inv = normalize(resid)
    normed = (hat * line(g2_ref) + line(c2_ref)).astype(BF)
    pre = nt(normed, w1_ref[...]) + b1_ref[2:3]
    cdf = 0.5 + 0.5 * lax.erf(pre * math.sqrt(0.5))
    act = (pre * cdf).astype(BF)
    slope = cdf + pre * jnp.exp(-0.5 * pre * pre) * (1.0 / math.sqrt(2.0 * math.pi))
    branch = nn(act, w2_ref[...]) + line(b2_ref)
    output = resid + branch
    y_ref[...] = output.astype(BF)
    per = w_ref.shape[1] // BLK
    seq, at_ = i // per, i % per
    valid = w_ref[pl.ds(seq, 1), pl.ds(pl.multiple_of(at_ * BLK, BLK), BLK)].astype(F32)
    weight = column_of(valid)
    lane = lax.broadcasted_iota(jnp.int32, (1, LANES), 1)
    found = jnp.where(lane == 3, jnp.sum(valid, axis=1, keepdims=True), 0.0)
    for at, v in enumerate((attended, branch, output)):
        one = jnp.sum(weight * jnp.sum(v * v, axis=1, keepdims=True), axis=0, keepdims=True)
        found = jnp.where(lane == at, one, found)
    at_row = lax.broadcasted_iota(jnp.int32, sums.shape, 0) == seq
    sums[...] += jnp.where(at_row, found, 0.0)

    d_pre = (nt(cot, w2_ref[...]) * slope).astype(BF)
    part_ref[2] += tn(act[:, :own], cot)
    part_ref[1] += tn(d_pre[:, :own], normed)
    d_normed = nn(d_pre, w1_ref[...])
    d_hat = d_normed * line(g2_ref)
    grad = cot.astype(F32)
    d_resid = grad + inv * (
        d_hat - jnp.mean(d_hat, axis=1, keepdims=True) - hat * jnp.mean(d_hat * hat, axis=1, keepdims=True)
    )
    dr_ref[...] = d_resid
    low = d_resid.astype(BF)
    part_ref[0] += tn(mixed[:, :own], low)
    dm_ref[...] = nt(low, wo_ref[...]).astype(BF)
    for at, v in enumerate((grad, d_normed * hat, d_normed, low.astype(F32), d_pre.astype(F32))):
        vec[at] += fold8(v)

    @pl.when(i == pl.num_programs(0) - 1)
    def _():
        total = sums[...]
        counted = jnp.sum(jnp.where(lane == 3, total, 0.0), axis=1, keepdims=True)
        each = jnp.sqrt(total / (jnp.maximum(counted, 1.0) * attended.shape[1]))
        rms_ref[...] = each[: rms_ref.shape[0], : rms_ref.shape[1]]
        small_ref[...] = jnp.zeros_like(small_ref)
        for at, row in enumerate((0, 1, 2, 3, OWN_ROW)):
            small_ref[row : row + 1] = jnp.sum(vec[at], axis=0, keepdims=True)


def middle(own, mixed, x, cot, valid, wo, w1, w2, bo, g2, c2, b2, b1):
    tokens, width = x.shape
    inner, hidden = wo.shape[0], w1.shape[0]
    n = tokens // BLK
    return pl.pallas_call(
        functools.partial(middle_kernel, own),
        grid=(n,),
        in_specs=[rows(inner), rows(width), rows(width), whole(valid.shape)]
        + [whole((inner, width)), whole((hidden, width)), whole((hidden, width))]
        + [whole((width,))] * 4
        + [whole(b1.shape)],
        out_specs=[
            rows(width),
            rows(width),
            rows(inner),
            held((3, own, width)),
            held((8, width)),
            held((valid.shape[0], 3)),
        ],
        out_shape=[
            jax.ShapeDtypeStruct((tokens, width), BF),
            jax.ShapeDtypeStruct((tokens, width), F32),
            jax.ShapeDtypeStruct((tokens, inner), BF),
            jax.ShapeDtypeStruct((3, own, width), F32),
            jax.ShapeDtypeStruct((8, width), F32),
            jax.ShapeDtypeStruct((valid.shape[0], 3), F32),
        ],
        scratch_shapes=[pltpu.VMEM((5, 8, width), F32), pltpu.VMEM((-(-valid.shape[0] // 8) * 8, LANES), F32)],
        compiler_params=params(1),
        cost_estimate=pl.CostEstimate(
            flops=2 * tokens * width * (6 * width + 3 * own),
            bytes_accessed=14 * tokens * width + 6 * width * width,
            transcendentals=2 * tokens * hidden,
        ),
        name="middle",
    )(mixed, x, cot, valid, wo, w1, w2, bo, g2, c2, b2, b1)


def finish_kernel(
    bits, own, steps, dq_ref, dk_ref, dv_ref, x_ref, dr_ref, g_ref, wq_ref, wk_ref, wv_ref, mq_ref, mk_ref, mv_ref, n_ref, in_ref,
    dx_ref, gq_ref, gk_ref, gv_ref, small_ref, vec, part, acc, taken, *refs,
):
    step = pl.program_id(0)
    grads = (mq_ref, mk_ref, mv_ref)
    count = len(grads)
    half = part.shape[2] // 2

    def publish(m, total):
        (gq_ref, gk_ref, gv_ref)[m][...] = total

    if bits is not None:
        place = Place(bits)
        work = Reduce(place, part, refs[:-3], FINISH_PLAN, publish)
        box, *sems = refs[-3:]

    @pl.when(step == 0)
    def _():
        vec[...] = jnp.zeros_like(vec)
        small_ref[...] = in_ref[...]
        if bits is not None:
            greet(place.plane())

    def take(m):
        taken[...] = grads[m][...]

    for m in range(count):
        pl.when(step == m)(functools.partial(take, m))

    @pl.when(step < count)
    def _():
        mine = taken[:, :own]
        part[step] = tn(mine, n_ref[...])
        total = jnp.sum(mine.astype(F32), axis=0, keepdims=True)
        for m in (0, 2):

            @pl.when(step == m)
            def _(at=m // 2 * half):
                small_ref[OWN_ROW + 1 : OWN_ROW + 2, at : at + own] = total

    def points(first, at, every):
        if bits is not None:
            for p in range(first, work.points, every):
                if work.plan[p]:
                    pl.when(step == at + (p - first) // every)(functools.partial(work.point, p))

    if bits is not None:
        for m in range(count):
            pl.when(step == m)(functools.partial(work.point, m))

    @pl.when(step >= count)
    def _():
        acc[...] = nn(dq_ref[...], wq_ref[...])
        points(count, count, 3)
        acc[...] += nn(dk_ref[...], wk_ref[...])
        points(count + 1, count, 3)
        d_normed = acc[...] + nn(dv_ref[...], wv_ref[...])
        hat, inv = normalize(x_ref[...].astype(F32))
        d_hat = d_normed * line(g_ref)
        dx_ref[...] = dr_ref[...] + inv * (
            d_hat - jnp.mean(d_hat, axis=1, keepdims=True) - hat * jnp.mean(d_hat * hat, axis=1, keepdims=True)
        )
        vec[0] += fold8(d_normed * hat)
        vec[1] += fold8(d_normed)
        points(count + 2, count, 3)

    @pl.when(step == steps - 1)
    def _():
        for at in range(2):
            small_ref[4 + at : 5 + at] = jnp.sum(vec[at], axis=0, keepdims=True)
        if bits is None:
            for m in range(count):
                publish(m, part[m])
        else:
            copies = [send(small_ref, box.at[place.d], sems, i, peer) for i, peer in enumerate(place.plane())]
            for one in copies:
                one.start()
            box[place.d] = small_ref[...]
            for one in copies:
                one.wait_recv()
            for one in copies:
                one.wait_send()
            total = box[0]
            for i in range(1, 8):
                total = total + box[i]
            small_ref[...] = total
            work.end()


def finish(dq, dk, dv, x, d_resid, g1, wq, wk, wv, normed1, small, own, bits):
    tokens, width = x.shape
    inner = wq.shape[0]
    hosted = bits is not None
    count = 3
    pad = -(-own // LANES) * LANES
    mine = pl.BlockSpec((tokens, pad), lambda i: (0, 0), pipeline_mode=pl.Buffered(1))

    def late(size):
        return pl.BlockSpec((BLK, size), lambda i: (jnp.maximum(i - count, 0), 0))

    return pl.pallas_call(
        functools.partial(finish_kernel, bits, own, count + tokens // BLK),
        grid=(count + tokens // BLK,),
        in_specs=[late(inner)] * 3
        + [late(width), late(width), whole((width,))]
        + [whole((inner, width))] * 3
        + [mine] * 3
        + [whole((tokens, width)), whole((8, width))],
        out_specs=[late(width)] + [held((own, width))] * 3 + [held((8, width))],
        out_shape=[jax.ShapeDtypeStruct((tokens, width), F32)]
        + [jax.ShapeDtypeStruct((own, width), F32)] * 3
        + [jax.ShapeDtypeStruct((8, width), F32)],
        scratch_shapes=[
            pltpu.VMEM((2, 8, width), F32),
            pltpu.VMEM((count, own, width), F32),
            pltpu.VMEM((BLK, width), F32),
            pltpu.VMEM((tokens, pad), BF),
        ]
        + (
            reduce_scratch(count, own, width)
            + [pltpu.VMEM((8, 8, width), F32), pltpu.SemaphoreType.DMA((7,)), pltpu.SemaphoreType.DMA((7,))]
            if hosted
            else []
        ),
        compiler_params=hosting(1, 4) if hosted else params(1),
        cost_estimate=pl.CostEstimate(
            flops=6 * tokens * width * inner, bytes_accessed=16 * tokens * width + 6 * width * inner, transcendentals=0
        ),
        name="finish",
    )(dq, dk, dv, x, d_resid, g1, wq, wk, wv, dq, dk, dv, normed1, small)


def shards(dp, tp, x, g1, c1, wq, bq, wk, wv, bv, wo, bo, g2, c2, w1, b1, w2, b2, seg, valid, cot):
    tokens, width = x.shape
    seqs, length = seg.shape
    own = wq.shape[1]
    bits = bits_of(dp) if dp == 8 else None

    own_biases = jnp.stack([bq, bv, b1])
    own_biases = jnp.concatenate([jnp.tile(own_biases, (1, tp)), jnp.zeros((5, tp * own), F32)], axis=0)
    place = lax.broadcasted_iota(jnp.int32, (tp, 8, tp * own), 2) // own
    biases = jnp.where(place == lax.broadcasted_iota(jnp.int32, place.shape, 0), own_biases[None], 0.0)
    normed1, q, k, v, mixed, lse, vectors, fq, fk, fv, fo, f1, f2 = front(
        x, g1, c1, seg, biases, [wq.T, wk.T, wv.T, wo, w1.T, w2], dp, tp
    )

    y, d_resid, d_mixed, parts, small, rms = middle(
        own, mixed, x, cot, valid, fo, f1, f2, bo, g2, c2, b2, vectors
    )
    dq, dk, dv, gwo, gw1, gw2 = attend_back(q, k, v, seg, mixed, d_mixed, lse, parts, bits)
    grad_input, gq, gk, gv, small = finish(dq, dk, dv, x, d_resid, g1, fq, fk, fv, normed1, small, own, bits)
    if bits is None:
        gwo, gw1, gw2, gq, gk, gv, small = lax.psum((gwo, gw1, gw2, gq, gk, gv, small), "dp")

    gb2, gg2, gc2, gbo, gg1, gc1 = (small[r] for r in range(6))
    gb1 = small[OWN_ROW, :own]
    gbq = small[OWN_ROW + 1, :own]
    gbv = small[OWN_ROW + 1, width // 2 : width // 2 + own]
    return (y, grad_input, gg1, gc1, gq.T, gbq, gk.T, gv.T, gbv, gwo, gbo, gg2, gc2, gw1.T, gb1, gw2, gb2, rms)


def solution(mesh):
    dp, tp = mesh.shape["dp"], mesh.shape["tensor"]
    tok, col, row, vec, rep = P("dp", None), P(None, "tensor"), P("tensor", None), P("tensor"), P()
    return jax.shard_map(
        functools.partial(shards, dp, tp),
        mesh=mesh,
        in_specs=(tok, rep, rep, col, vec, col, col, vec, row, rep, rep, rep, col, vec, row, rep, tok, tok, tok),
        out_specs=(tok, tok, rep, rep, col, vec, col, col, vec, row, rep, rep, rep, col, vec, row, rep, tok),
        check_vma=False,
    )
```

```python
import functools
import math

import jax
import jax.numpy as jnp
from jax import lax
from jax.experimental import pallas as pl
from jax.experimental.pallas import tpu as pltpu
from jax.sharding import PartitionSpec as P

HEAD_DIM = 160
MAX_DOC = 512
EPS = 1e-05
NEG = -1e30
BLK = 256
WIN = 256
LANES = 128
SCALE = 1.0 / math.sqrt(HEAD_DIM)
LOG2E = 1.0 / math.log(2.0)
BF = jnp.bfloat16
F32 = jnp.float32
VMEM_MAX = 60 << 20


def nn(a, b):
    return lax.dot_general(a, b, (((1,), (0,)), ((), ())), preferred_element_type=F32)


def nt(a, b):
    return lax.dot_general(a, b, (((1,), (1,)), ((), ())), preferred_element_type=F32)


def tn(a, b):
    return lax.dot_general(a, b, (((0,), (0,)), ((), ())), preferred_element_type=F32)


def whole(shape):
    return pl.BlockSpec(shape, lambda *_: (0,) * len(shape), pipeline_mode=pl.Buffered(1))


def held(shape):
    return pl.BlockSpec(shape, lambda *_: (0,) * len(shape))


def rows(width):
    return pl.BlockSpec((BLK, width), lambda i: (i, 0))


def column_of(row):
    n = row.shape[1]
    eye = lax.broadcasted_iota(jnp.int32, (n, n), 0) == lax.broadcasted_iota(jnp.int32, (n, n), 1)
    return jnp.sum(jnp.where(eye, row, jnp.zeros_like(row)), axis=1, keepdims=True)


def line(ref):
    return ref[...].reshape(1, ref.shape[0])


def fold8(t):
    return jnp.sum(t.reshape(t.shape[0] // 8, 8, t.shape[1]), axis=0)


def params(grid, vmem=VMEM_MAX):
    return pltpu.CompilerParams(dimension_semantics=("arbitrary",) * grid, vmem_limit_bytes=vmem)


def hosting(grid, ident):
    return pltpu.CompilerParams(
        dimension_semantics=("arbitrary",) * grid,
        vmem_limit_bytes=VMEM_MAX,
        collective_id=ident,
        has_side_effects=True,
    )


def sibling(index, bit):
    return index + bit - 2 * bit * (index // bit % 2)


class Place:
    def __init__(self, bits):
        self.d, self.z = lax.axis_index("dp"), lax.axis_index("tensor")
        self.core = self.d % 2
        self.a, self.b = (self.d // bit % 2 for bit in bits)
        self.spot = self.a + 2 * self.b
        self.on_core = {"dp": sibling(self.d, 1), "tensor": self.z}
        self.on_a, self.on_b = ({"dp": sibling(self.d, bit), "tensor": self.z} for bit in bits)
        peers = (None, sibling(self.z, 1), sibling(self.z, 2), sibling(sibling(self.z, 1), 2))
        self.on_z = [None] + [{"dp": self.d, "tensor": peer} for peer in peers[1:]]

    def plane(self):
        return [{"dp": (self.d + step) % 8, "tensor": self.z} for step in range(1, 8)]


def greet(targets):
    barrier = pltpu.get_barrier_semaphore()
    for target in targets:
        pl.semaphore_signal(barrier, inc=1, device_id=target, device_id_type=pl.DeviceIdType.MESH)
    pl.semaphore_wait(barrier, len(targets))


def send(src, dst, sems, at, target):
    return pltpu.make_async_remote_copy(
        src_ref=src,
        dst_ref=dst,
        send_sem=sems[0].at[at],
        recv_sem=sems[1].at[at],
        device_id=target,
        device_id_type=pl.DeviceIdType.MESH,
    )


def bits_of(dp):
    return (2, 4) if dp == 8 else (2, 8)


def chunks_of(count, tp, piece):
    cut = (piece * 5 // 8) // 8 * 8
    orders = [[1 + (j + m % 2) % (tp - 1) for j in range(tp - 1)] for m in range(count)]
    return [(m, j, *span) for m in range(count) for span in ((0, cut), (cut, piece)) for j in orders[m]]


AHEAD = 6
LAG = 2
ATTEND_COST = 0.9


class Gather:
    def __init__(self, place, chunks, mine, land, sems, publish):
        self.place, self.chunks, self.mine, self.land, self.sems, self.publish = place, chunks, mine, land, sems, publish
        self.ticks = len(chunks) + 3 * LAG
        self.closing = {(m, j): k for k, (m, j, _, _) in enumerate(chunks)}

    def slot(self, k, where, low=None, high=None):
        m, j, r0, r1 = self.chunks[k]
        low, high = (r0 if low is None else low), (r1 if high is None else high)
        return self.land.at[m, j - 1, self.place.core, where, pl.ds(low, high - low)]

    def middle(self, k):
        _, _, r0, r1 = self.chunks[k]
        half = (r1 - r0) // 2
        return r0 + (half + 7 if k % 2 else half) // 8 * 8

    def over_z(self, k):
        m, j, r0, r1 = self.chunks[k]
        spots = [self.place.spot] + ([3 - self.place.spot] if j == 1 else [])
        return [
            send(self.mine.at[m, i, pl.ds(r0, r1 - r0)], self.slot(k, spot), self.sems, (k, i), self.place.on_z[j])
            for i, spot in enumerate(spots)
        ]

    def over_a(self, k):
        here = self.slot(k, self.place.spot)
        return send(here, here, self.sems, (k, 2), self.place.on_a)

    def over_b(self, k):
        here = self.slot(k, self.place.spot)
        return send(here, here, self.sems, (k, 3), self.place.on_b)

    def on_a(self, k):
        part = self.slot(k, sibling(self.place.spot, 2), None, self.middle(k))
        return send(part, part, self.sems, (k, 4), self.place.on_a)

    def on_b(self, k):
        part = self.slot(k, sibling(self.place.spot, 1), self.middle(k), None)
        return send(part, part, self.sems, (k, 5), self.place.on_b)

    def relays(self, k):
        return [] if self.chunks[k][1] == 1 else [self.on_a(k), self.on_b(k)]

    def swap(self, k):
        m, j, r0, r1 = self.chunks[k]
        part = self.land.at[m, j - 1, self.place.core, :, pl.ds(r0, r1 - r0)]
        return send(part, part, self.sems, (k, 6), self.place.on_core)

    def start_z(self, k):
        for one in self.over_z(k):
            one.start()

    def tick(self, t):
        total = len(self.chunks)
        if 0 <= t < total:
            for one in self.over_z(t):
                one.wait_recv()
            self.over_a(t).start()
            self.over_b(t).start()
            if t + AHEAD < total:
                self.start_z(t + AHEAD)
        k = t - LAG
        if 0 <= k < total:
            self.over_b(k).wait_recv()
            for one in self.relays(k)[:1]:
                one.start()
            self.over_a(k).wait_recv()
            for one in self.relays(k)[1:]:
                one.start()
        k = t - 2 * LAG
        if 0 <= k < total:
            for one in self.relays(k):
                one.wait_recv()
            self.swap(k).start()
        k = t - 3 * LAG
        if 0 <= k < total:
            self.swap(k).wait_recv()
            m, j, _, _ = self.chunks[k]
            if self.closing[m, j] == k:
                piece = self.land.shape[4]
                self.publish(m, j, self.land[m, j - 1].reshape(8 * piece, -1).astype(BF))

    def end(self):
        for k in range(len(self.chunks)):
            for one in self.over_z(k) + self.relays(k) + [self.over_a(k), self.over_b(k), self.swap(k)]:
                one.wait_send()


def gather_scratch(count, tp, piece, width):
    total = len(chunks_of(count, tp, piece))
    return [
        pltpu.VMEM((count, tp - 1, 2, 4, piece, width), F32),
        pltpu.SemaphoreType.DMA((total, 7)),
        pltpu.SemaphoreType.DMA((total, 7)),
        pltpu.VMEM((count, 2, piece, width), F32),
    ]


class Reduce:
    def __init__(self, place, part, scratch, plan, publish):
        self.place, self.part, self.publish = place, part, publish
        self.count, self.own, self.width = part.shape
        self.out, self.half, self.first, self.second, *self.sems = scratch
        self.points = 1 + max(row[-1] for row in plan)
        self.plan = {p: [] for p in range(self.points)}
        for k, row in enumerate(plan):
            for stage, p in enumerate(row):
                self.plan[p].append((k, stage))
        for p, found in self.plan.items():
            found.sort(key=lambda one: (one[1] if p == self.points - 1 else -one[1], one[0]))
        ends = [k for p in range(self.points) for k, stage in self.plan[p] if stage == 6]
        self.closing = [max(2 * m, 2 * m + 1, key=ends.index) for m in range(self.count)]

    def greet(self):
        return [self.place.on_a, self.place.on_b, self.place.on_core]

    def rows_of(self, size, index, count):
        return pl.ds(pl.multiple_of(size * index, 8), count)

    def way(self, k):
        p = self.place
        return (p.a, p.on_a, p.b, p.on_b) if k % 2 == 0 else (p.b, p.on_b, p.a, p.on_a)

    def columns(self, bit):
        lanes = self.width // 2
        return pl.ds(pl.multiple_of(lanes * bit, LANES), lanes)

    def out_rows(self, k, bit):
        piece = self.own // 8
        return self.rows_of(piece, 4 * self.place.core + 2 * (k % 2) + bit, piece)

    def quarter(self, k, core):
        size = self.own // 4
        return self.rows_of(size, 2 * core + k % 2, size)

    def copy(self, k, stage):
        place, m, piece = self.place, k // 2, self.own // 8
        bit, peer, bit2, peer2 = self.way(k)
        if stage == 0:
            src, dst, to = self.part.at[m, self.quarter(k, 1 - place.core)], self.half.at[k], place.on_core
        elif stage == 1:
            src, dst, to = self.half.at[k, self.rows_of(piece, 1 - bit, piece)], self.first.at[k], peer
        elif stage == 2:
            src, dst, to = self.half.at[k, self.rows_of(piece, bit, piece), self.columns(1 - bit2)], self.second.at[k], peer2
        elif stage == 3:
            src = dst = self.out.at[m, self.out_rows(k, bit), self.columns(bit2)]
            to = peer2
        elif stage == 4:
            src = dst = self.out.at[m, self.out_rows(k, bit)]
            to = peer
        else:
            src = dst = self.out.at[m, self.quarter(k, place.core)]
            to = place.on_core
        return send(src, dst, self.sems, (k, stage), to)

    def step(self, k, stage):
        m, piece = k // 2, self.own // 8
        bit, _, bit2, _ = self.way(k)
        mine = self.rows_of(piece, bit, piece)
        if stage >= 1:
            self.copy(k, stage - 1).wait_recv()
        if stage == 1:
            self.half[k] = self.part[m, self.quarter(k, self.place.core)] + self.half[k]
        if stage == 2:
            self.half[k, mine] = self.half[k, mine] + self.first[k]
        if stage == 3:
            columns = self.columns(bit2)
            self.out[m, self.out_rows(k, bit), columns] = self.half[k, mine, columns] + self.second[k]
        if stage < 6:
            self.copy(k, stage).start()
            return
        if k == self.closing[m]:
            self.publish(m, self.out[m])

    def point(self, p):
        for k, stage in self.plan[p]:
            self.step(k, stage)

    def end(self):
        for k in range(2 * self.count):
            for stage in range(6):
                self.copy(k, stage).wait_send()


def reduce_scratch(count, own, width):
    chunks = 2 * count
    return [
        pltpu.VMEM((count, own, width), F32),
        pltpu.VMEM((chunks, own // 4, width), F32),
        pltpu.VMEM((chunks, own // 8, width), F32),
        pltpu.VMEM((chunks, own // 8, width // 2), F32),
        pltpu.SemaphoreType.DMA((chunks, 6)),
        pltpu.SemaphoreType.DMA((chunks, 6)),
    ]


def normalize(v):
    center = v - jnp.mean(v, axis=-1, keepdims=True)
    inv = lax.rsqrt(jnp.mean(center * center, axis=-1, keepdims=True) + EPS)
    return center * inv, inv


HEADS_IN_GROUP = 4
GROUP = HEADS_IN_GROUP * HEAD_DIM


def window_of(head):
    low = head * HEAD_DIM
    start = low // LANES * LANES
    return start, low - start


def lane_mask(offset):
    lane = lax.broadcasted_iota(jnp.int32, (1, WIN), 1)
    return (lane >= offset) & (lane < offset + HEAD_DIM)


def spread(parts):
    tiles = [None] * (GROUP // LANES)
    for head, part in enumerate(parts):
        first = window_of(head)[0] // LANES
        for half in range(WIN // LANES):
            piece = part[:, half * LANES : (half + 1) * LANES]
            at = first + half
            tiles[at] = piece if tiles[at] is None else tiles[at] + piece
    return jnp.concatenate(tiles, axis=1)


def attend_block(seq, i, q_ref, k_ref, v_ref, seg_ref, o_ref, lse_ref, bias, between):
    groups = q_ref.shape[1] // GROUP
    back = MAX_DOC // BLK
    here = pl.ds(pl.multiple_of(i * BLK, BLK), BLK)
    row = pl.ds(seq, 1)
    seg_col = column_of(seg_ref[row, here])
    count = jnp.minimum(i, back) + 1
    kinds = range(1, back + 2)

    def first(blocks):
        return pl.multiple_of((i + 1 - blocks) * BLK, BLK)

    def mask_of(blocks):
        keys, start = blocks * BLK, first(blocks)
        query = i * BLK + lax.broadcasted_iota(jnp.int32, (BLK, keys), 0)
        key = start + lax.broadcasted_iota(jnp.int32, (BLK, keys), 1)
        allowed = (query >= key) & (seg_col == seg_ref[row, pl.ds(start, keys)])
        bias[:, :keys] = jnp.where(allowed, 0.0, NEG)

    def heads(gi, blocks):
        keys, start = blocks * BLK, first(blocks)
        parts = []
        lse = lse_ref[...]
        head_lane = lax.broadcasted_iota(jnp.int32, (1, LANES), 1)
        for h in range(HEADS_IN_GROUP):
            at, off = window_of(h)
            lanes = pl.ds(pl.multiple_of(gi * GROUP + at, LANES), WIN)
            mask = lane_mask(off)
            q = q_ref[here, lanes]
            q = jnp.where(mask, q, jnp.zeros_like(q))
            t = nt(q, k_ref[pl.ds(start, keys), lanes]) * (SCALE * LOG2E) + bias[:, :keys]
            top = jnp.max(t, axis=1, keepdims=True)
            p = jnp.exp2(t - top)
            total = jnp.sum(p, axis=1, keepdims=True)
            o = nn(p.astype(BF), v_ref[pl.ds(start, keys), lanes])
            parts.append(jnp.where(mask, o * (1.0 / total), 0.0))
            lse = jnp.where(head_lane == gi * HEADS_IN_GROUP + h, top + jnp.log2(total), lse)
        lse_ref[...] = lse
        o_ref[:, pl.ds(pl.multiple_of(gi * GROUP, LANES), GROUP)] = spread(parts).astype(BF)

    lse_ref[...] = jnp.zeros_like(lse_ref)
    for blocks in kinds:
        pl.when(count == blocks)(functools.partial(mask_of, blocks))

    def group(gi, carry):
        for blocks in kinds:
            pl.when(count == blocks)(functools.partial(heads, gi, blocks))
        between(gi)
        return carry

    lax.fori_loop(0, groups, group, 0)


def front_kernel(
    bits, n, seqs, steps, chunks, count, x_ref, g_ref, c_ref, seg_ref, bq_ref, bv_ref, bh_ref, *refs
):
    local, refs = refs[:count], refs[count:]
    n_ref, q_ref, k_ref, v_ref, o_ref, lse_ref, vec_ref, *refs = refs
    full, refs = refs[:count], refs[count:]
    bias, weights, stage, qs, ks, vs, ns, passing, fresh, land, gather_s, gather_r, mine, raw, bias_in, bias_s, bias_r, local_sem, out_sem, raw_sem, copy_sem, back_sem, bias_ref = refs
    own = local[0].shape[0]
    held_here = weights.shape[0]
    step = pl.program_id(0)
    place = Place(bits)
    shards_ = len(place.on_z)
    ahead = 2 * n + (seqs - 1) * n
    order = sorted({chunk[:2] for chunk in chunks if chunk[0] >= held_here}, key=lambda one: max(k for k, chunk in enumerate(chunks) if chunk[:2] == one))

    def rows_of(j):
        return pl.ds(j * own, own)

    def stage_copy(number):
        m, j = order[number]
        return pltpu.make_async_copy(stage.at[number % 2], full[m].at[rows_of(j)], out_sem.at[number])

    def publish(m, j, shard):
        if m < held_here:
            weights[m, rows_of(j)] = shard
            return
        number = order.index((m, j))
        if number >= 2:
            stage_copy(number - 2).wait()
        stage[number % 2] = shard
        stage_copy(number).start()

    work = Gather(place, chunks, mine, land, (gather_s, gather_r), publish)
    ready = [max(k for k, chunk in enumerate(chunks) if chunk[0] == m) + 3 * LAG + 1 for m in range(held_here)]

    def own_copies():
        held_ = [pltpu.make_async_copy(local[m], weights.at[m, rows_of(0)], local_sem.at[m]) for m in range(held_here)]
        rest = [
            pltpu.make_async_copy(local[m], full[m].at[rows_of(0)], local_sem.at[m]) for m in range(held_here, count)
        ]
        return held_, rest

    def held_out():
        return [pltpu.make_async_copy(weights.at[m], full[m], local_sem.at[m]) for m in range(held_here)]

    @pl.when(step == 0)
    def _():
        held_, rest = own_copies()
        piece = own // 8
        raws = [
            [
                pltpu.make_async_copy(
                    local[m].at[pl.ds(pl.multiple_of(piece * (4 * place.core + spot), 8), piece)],
                    raw.at[m % 2, i],
                    raw_sem.at[m % 2, i],
                )
                for i, spot in enumerate((place.spot, 3 - place.spot))
            ]
            for m in range(count)
        ]
        for one in sum(raws[:2], []) + held_ + rest:
            one.start()
        greet(place.on_z[1:] + [place.on_a, place.on_b, place.on_core])
        for m in range(count):
            for i, one in enumerate(raws[m]):
                one.wait()
                mine[m, i] = raw[m % 2, i].astype(F32)
            for one in raws[m + 2] if m + 2 < count else []:
                one.start()
            if m == 0:
                for k in range(AHEAD):
                    work.start_z(k)
        bias_ref[...] = jnp.zeros_like(bias_ref)
        for r, ref in enumerate((bq_ref, bv_ref, bh_ref)):
            row = line(ref)
            for j in range(shards_):
                pieces = [jnp.zeros((1, j * own), F32), row, jnp.zeros((1, (shards_ - 1 - j) * own), F32)]
                bias_ref[j, r : r + 1] = jnp.concatenate([t for t in pieces if t.shape[1]], axis=1)
        vectors = [
            send(bias_ref.at[j], bias_in.at[j], (bias_s, bias_r), j, place.on_z[j]) for j in range(1, shards_)
        ]
        for one in vectors:
            one.start()
        for t in range(ready[0]):
            work.tick(t)
        for one in vectors:
            one.wait()
        vec_ref[...] = sum((bias_in[j] for j in range(1, shards_)), bias_ref[0])
        for one in held_:
            one.wait()

    @pl.when(step == 1 + ahead)
    def _():
        for one in held_out():
            one.start()

    unit = jnp.maximum(step - 1 - ahead, 0)
    seq, part = unit // (2 * n), unit % (2 * n)
    early = jnp.maximum(step - 1 - 2 * n, 0)
    block = jnp.where(step <= 2 * n, (step - 1 + n) % n, jnp.where(step <= ahead, early % n, part % n))
    here = pl.ds(pl.multiple_of(block * BLK, BLK), BLK)

    def leave(i, src, dst, sequence):
        there = pl.ds(pl.multiple_of((sequence * n + block) * BLK, BLK), BLK)
        return pltpu.make_async_copy(src, dst.at[there], copy_sem.at[i, block])

    def enter(sequence):
        there = pl.ds(pl.multiple_of(sequence * n * BLK, BLK), n * BLK)
        return [
            pltpu.make_async_copy(src.at[there], dst, back_sem.at[i]) for i, (src, dst) in enumerate(((q_ref, qs), (k_ref, ks)))
        ]

    first = (step > 0) & (step <= n)
    second = (step > n) & (step <= 2 * n)
    passing_by = (step > 2 * n) & (step <= ahead)
    third = (step > ahead) & (part < n)
    again = third & (seq > 0)

    @pl.when(again)
    def _():
        @pl.when(part == 0)
        def _():
            for one in enter(seq):
                one.start()

        leave(2, ns.at[here], n_ref, seq - 1).wait()
        leave(3, vs.at[here], v_ref, seq - 1).wait()

    @pl.when(first | passing_by | again)
    def _():
        hat, _ = normalize(x_ref[...].astype(F32))
        fresh[...] = (hat * line(g_ref) + line(c_ref)).astype(BF)

    @pl.when(first | again)
    def _():
        ns[here] = fresh[...]

    @pl.when(second | (third & (seq == 0)))
    def _():
        fresh[...] = ns[here]

    @pl.when(first | second | passing_by | third)
    def _():
        low = jnp.where(third, 2, jnp.where(second, 1, 0))

        def make(m, carry):
            row = jnp.where(m == 0, 0, jnp.where(m == 1, 3, 1))
            passing[m % 2] = (nt(fresh[...], weights[m]) + vec_ref[pl.ds(row, 1)]).astype(BF)
            return carry

        lax.fori_loop(low, low + jnp.where(passing_by, 2, 1), make, 0)

    @pl.when(first)
    def _():
        qs[here] = passing[0]
        leave(0, qs.at[here], q_ref, 0).start()
        leave(2, ns.at[here], n_ref, 0).start()

    @pl.when(second)
    def _():
        ks[here] = passing[1]
        leave(1, ks.at[here], k_ref, 0).start()

    @pl.when(passing_by)
    def _():
        copies = [leave(3 + i, passing.at[i], dst, 1 + early // n) for i, dst in enumerate((q_ref, k_ref))]
        for one in copies:
            one.start()
        for one in copies:
            one.wait()

    @pl.when(third)
    def _():
        vs[here] = passing[0]
        leave(3, vs.at[here], v_ref, seq).start()

    @pl.when(again)
    def _():
        leave(2, ns.at[here], n_ref, seq).start()

        @pl.when(part == n - 1)
        def _():
            for one in enter(seq):
                one.wait()

    @pl.when((step > ahead) & (part == n) & (seq == 0))
    def _():
        for b in range(n):
            there = pl.ds(b * BLK, BLK)
            pltpu.make_async_copy(qs.at[there], q_ref.at[there], copy_sem.at[0, b]).wait()
            pltpu.make_async_copy(ks.at[there], k_ref.at[there], copy_sem.at[1, b]).wait()

    reach = MAX_DOC // BLK + 1
    groups = qs.shape[1] // GROUP
    spots = [(at, None, 1.0) for at in range(1, ahead + 1)]
    for number in range(seqs):
        at = 1 + ahead + 2 * n * number
        spots += [(at + i, None, 1.6 if number else 1.0) for i in range(n)]
        for i in range(n):
            each = min(i + 1, reach) * ATTEND_COST / groups
            spots += [(at + n + i, gi, each) for gi in range(groups)]
    starts = (1, 1 + n, 1 + ahead, steps)
    where = {}
    for t in range(ready[0], work.ticks):
        m = sum(t >= one for one in ready)
        begin, upto = ready[m - 1], (ready + [work.ticks])[m]
        span = [one for one in spots if starts[m - 1] <= one[0] < starts[m]]
        goal, passed, i = (t - begin + 1) / (upto - begin) * sum(one[2] for one in span), span[0][2], 0
        while passed < goal - 1e-6 and i < len(span) - 1:
            i += 1
            passed += span[i][2]
        where[t] = span[i][:2]

    def between(gi):
        for t, (at, spot) in where.items():
            if spot is not None:
                pl.when((step == at) & (gi == spot))(functools.partial(work.tick, t))

    for t, (at, spot) in where.items():
        if spot is None and at <= ahead + n:
            pl.when(step == at)(functools.partial(work.tick, t))

    @pl.when((step > ahead) & (part >= n))
    def _():
        attend_block(seq, part - n, qs, ks, vs, seg_ref, o_ref, lse_ref, bias, between)

    for t, (at, spot) in where.items():
        if spot is None and at > ahead + n:
            pl.when(step == at)(functools.partial(work.tick, t))

    @pl.when(step == steps - 1)
    def _():
        work.end()
        for number in range(max(0, len(order) - 2), len(order)):
            stage_copy(number).wait()
        for one in held_out() + own_copies()[1]:
            one.wait()
        for b in range(n):
            for i, (src, dst) in ((2, (ns, n_ref)), (3, (vs, v_ref))):
                there = pl.ds(((seqs - 1) * n + b) * BLK, BLK)
                pltpu.make_async_copy(src.at[pl.ds(b * BLK, BLK)], dst.at[there], copy_sem.at[i, b]).wait()


def front(x, g1, c1, seg, biases, shards_, dp, tp):
    tokens, width = x.shape
    seqs, length = seg.shape
    n = length // BLK
    count, own = len(shards_), shards_[0].shape[0]
    bits, piece, steps, out = bits_of(dp), own // 8, 1 + 2 * n + (seqs - 1) * n + 2 * seqs * n, tp * own
    chunks = chunks_of(count, tp, piece)

    ahead = 2 * n + (seqs - 1) * n

    def unit(i):
        return jnp.maximum(i - 1 - ahead, 0)

    def early(i):
        opening = jnp.minimum(jnp.maximum(i - 1, 0), n - 1)
        later = n + jnp.maximum(i - 1 - 2 * n, 0)
        again = unit(i) // (2 * n) * n + jnp.minimum(unit(i) % (2 * n), n - 1)
        return (jnp.where(i <= 2 * n, opening, jnp.where(i <= ahead, later, jnp.where(unit(i) < 2 * n, ahead - n - 1, again))), 0)

    def late(size):
        return pl.BlockSpec((BLK, size), lambda i: (unit(i) // (2 * n) * n + jnp.maximum(unit(i) % (2 * n) - n, 0), 0))

    anywhere = pl.BlockSpec(memory_space=pl.ANY)
    pairs = seqs * n * 2.5 * BLK * BLK * (out // HEAD_DIM)
    return pl.pallas_call(
        functools.partial(front_kernel, bits, n, seqs, steps, chunks, count),
        grid=(steps,),
        in_specs=[
            pl.BlockSpec((BLK, width), early),
            whole(g1.shape),
            whole(c1.shape),
            whole(seg.shape),
        ]
        + [whole((own,))] * 3
        + [anywhere] * count,
        out_specs=[anywhere] * 4 + [late(out), late(LANES), held((8, out))] + [anywhere] * count,
        out_shape=[jax.ShapeDtypeStruct((tokens, width), BF)]
        + [jax.ShapeDtypeStruct((tokens, out), BF)] * 4
        + [jax.ShapeDtypeStruct((tokens, LANES), F32), jax.ShapeDtypeStruct((8, out), F32)]
        + [jax.ShapeDtypeStruct((out, width), BF)] * count,
        scratch_shapes=[
            pltpu.VMEM((BLK, BLK + MAX_DOC), F32),
            pltpu.VMEM((3, out, width), BF),
            pltpu.VMEM((2, own, width), BF),
        ]
        + [pltpu.VMEM((length, out), BF)] * 3
        + [pltpu.VMEM((length, width), BF), pltpu.VMEM((2, BLK, out), BF), pltpu.VMEM((BLK, width), BF)]
        + gather_scratch(count, tp, piece, width)
        + [
            pltpu.VMEM((2, 2, piece, width), BF),
            pltpu.VMEM((tp, 8, out), F32),
            pltpu.SemaphoreType.DMA((tp,)),
            pltpu.SemaphoreType.DMA((tp,)),
            pltpu.SemaphoreType.DMA((count,)),
            pltpu.SemaphoreType.DMA((count * tp,)),
            pltpu.SemaphoreType.DMA((2, 2)),
            pltpu.SemaphoreType.DMA((5, n)),
            pltpu.SemaphoreType.DMA((2,)),
            pltpu.VMEM((tp, 8, out), F32),
        ],
        compiler_params=hosting(1, 0),
        cost_estimate=pl.CostEstimate(
            flops=int(6 * tokens * width * out + pairs * 8 * WIN),
            bytes_accessed=12 * tokens * width + 4 * count * out * width,
            transcendentals=int(pairs),
        ),
        name="front",
    )(x, g1, c1, seg, *biases, *shards_)


def attend_back_kernel(
    steps, bits, q_ref, do_ref, o_ref, lse_ref, k_ref, v_ref, seg_ref, part_ref, dq_ref, dk_ref, dv_ref, go_ref, g1_ref, g2_ref,
    bias, dq_acc, lse_t, delta_t, *reduce_refs,
):
    s, j = pl.program_id(0), pl.program_id(1)
    n = pl.num_programs(1)
    length, width = q_ref.shape
    groups = width // GROUP
    ahead = MAX_DOC // BLK

    step = s * n + j

    def publish(m, total):
        (go_ref, g1_ref, g2_ref)[m][...] = total

    if bits is not None:
        work = Reduce(Place(bits), part_ref, reduce_refs, BACK_PLAN, publish)

        @pl.when(step == 0)
        def _():
            greet(work.greet())
            work.point(0)

    @pl.when(j == 0)
    def _():
        dq_acc[...] = jnp.zeros_like(dq_acc)
        head = lax.broadcasted_iota(jnp.int32, (16, width), 0)
        lane = lax.broadcasted_iota(jnp.int32, (16, width), 1)
        pick = jnp.where((lane >= head * HEAD_DIM) & (lane < (head + 1) * HEAD_DIM), 1.0, 0.0).astype(BF)
        for b in range(length // BLK):
            at = slice(b * BLK, (b + 1) * BLK)
            lse_t[:, at] = lse_ref[at, :].T[:16, :]
            prod = do_ref[at, :].astype(F32) * o_ref[at, :].astype(F32)
            high = prod.astype(BF)
            rest = (prod - high.astype(F32)).astype(BF)
            delta_t[:, at] = nt(pick, high) + nt(pick, rest)

    count = jnp.minimum(n - j, ahead + 1)
    start = pl.multiple_of(j * BLK, BLK)
    seg_col = column_of(seg_ref[pl.ds(s, 1), pl.ds(start, BLK)])

    def mask_of(blocks):
        queries = blocks * BLK
        row = lax.broadcasted_iota(jnp.int32, (BLK, queries), 0)
        col = lax.broadcasted_iota(jnp.int32, (BLK, queries), 1)
        allowed = (row <= col) & (seg_col == seg_ref[pl.ds(s, 1), pl.ds(start, queries)])
        bias[:, :queries] = jnp.where(allowed, 0.0, NEG)

    def heads(gi, blocks):
        queries = blocks * BLK
        span = pl.ds(start, queries)
        dks, dvs = [], []
        for h in range(HEADS_IN_GROUP):
            at, off = window_of(h)
            lanes = pl.ds(pl.multiple_of(gi * GROUP + at, LANES), WIN)
            mask = lane_mask(off)
            head = pl.ds(gi * HEADS_IN_GROUP + h, 1)
            k = k_ref[:, lanes]
            k = jnp.where(mask, k, jnp.zeros_like(k))
            v = v_ref[:, lanes]
            v = jnp.where(mask, v, jnp.zeros_like(v))
            q = q_ref[span, lanes]
            do = do_ref[span, lanes]
            t = nt(k, q) * (SCALE * LOG2E) + bias[:, :queries]
            p = jnp.exp2(t - lse_t[head, span])
            dvs.append(jnp.where(mask, nn(p.astype(BF), do), 0.0))
            ds = (p * (nt(v, do) - delta_t[head, span])).astype(BF)
            dks.append(jnp.where(mask, nn(ds, q), 0.0))
            dq_acc[span, lanes] += tn(ds, k)
        out = pl.ds(pl.multiple_of(gi * GROUP, LANES), GROUP)
        dk_ref[:, out] = (spread(dks) * SCALE).astype(BF)
        dv_ref[:, out] = spread(dvs).astype(BF)

    kinds = range(1, ahead + 2)
    for blocks in kinds:
        pl.when(count == blocks)(functools.partial(mask_of, blocks))

    def group(gi, carry):
        for blocks in kinds:
            pl.when(count == blocks)(functools.partial(heads, gi, blocks))
        if bits is not None:
            for p in range(1, work.points):
                pl.when(step * groups + gi + 1 == p)(functools.partial(work.point, p))
        return carry

    lax.fori_loop(0, groups, group, 0)

    if bits is not None:
        pl.when(step == steps - 1)(work.end)
    else:
        for m in range(3):
            publish(m, part_ref[m])

    @pl.when(j == n - 1)
    def _():
        dq_ref[...] = (dq_acc[...] * SCALE).astype(BF)


def attend_back(q, k, v, seg, mixed, d_mixed, lse, parts, bits):
    tokens, width = q.shape
    seqs, length = seg.shape
    own, model = parts.shape[1:]
    n = length // BLK
    spec_k = pl.BlockSpec((BLK, width), lambda s, j: (s * n + j, 0))
    spec_q = pl.BlockSpec((length, width), lambda s, j: (s, 0))
    pairs = seqs * n * 2.5 * BLK * BLK * (width // HEAD_DIM)
    hosted = bits is not None
    return pl.pallas_call(
        functools.partial(attend_back_kernel, seqs * n, bits),
        grid=(seqs, n),
        in_specs=[
            spec_q,
            spec_q,
            spec_q,
            pl.BlockSpec((length, LANES), lambda s, j: (s, 0)),
            spec_k,
            spec_k,
            whole(seg.shape),
            whole(parts.shape),
        ],
        out_specs=[spec_q, spec_k, spec_k] + [held((own, model))] * 3,
        scratch_shapes=[
            pltpu.VMEM((BLK, BLK + MAX_DOC), F32),
            pltpu.VMEM((length, width), F32),
            pltpu.VMEM((16, length), F32),
            pltpu.VMEM((16, length), F32),
        ]
        + (reduce_scratch(*parts.shape) if hosted else []),
        out_shape=[jax.ShapeDtypeStruct((tokens, width), BF)] * 3 + [jax.ShapeDtypeStruct((own, model), F32)] * 3,
        compiler_params=hosting(2, 3) if hosted else params(2),
        cost_estimate=pl.CostEstimate(
            flops=int(pairs * 20 * WIN), bytes_accessed=16 * tokens * width, transcendentals=int(pairs)
        ),
        name="attend_back",
    )(q, d_mixed, mixed, lse, k, v, seg, parts)


BACK_PLAN = (
    (0, 1, 4, 7, 9, 11, 14),
    (0, 2, 4, 6, 10, 13, 14),
    (1, 2, 5, 8, 10, 13, 14),
    (0, 1, 3, 8, 11, 14, 16),
    (0, 5, 9, 10, 13, 15, 16),
    (0, 3, 6, 11, 13, 15, 16),
)
FINISH_PLAN = (
    (0, 1, 6, 10, 13, 19, 26),
    (0, 1, 5, 9, 13, 18, 21),
    (5, 6, 12, 16, 19, 24, 26),
    (1, 3, 10, 17, 21, 25, 26),
    (2, 3, 9, 17, 20, 25, 26),
    (4, 5, 12, 16, 19, 23, 25),
)

OWN_ROW = 6


def middle_kernel(
    own, m_ref, x_ref, g_ref, w_ref, wo_ref, w1_ref, w2_ref, bo_ref, g2_ref, c2_ref, b2_ref, b1_ref,
    y_ref, dr_ref, dm_ref, part_ref, small_ref, rms_ref, vec, sums,
):
    i = pl.program_id(0)

    @pl.when(i == 0)
    def _():
        part_ref[...] = jnp.zeros_like(part_ref)
        vec[...] = jnp.zeros_like(vec)
        sums[...] = jnp.zeros_like(sums)

    mixed = m_ref[...]
    cot = g_ref[...]
    attended = nn(mixed, wo_ref[...]) + line(bo_ref)
    resid = x_ref[...].astype(F32) + attended
    hat, inv = normalize(resid)
    normed = (hat * line(g2_ref) + line(c2_ref)).astype(BF)
    pre = nt(normed, w1_ref[...]) + b1_ref[2:3]
    cdf = 0.5 + 0.5 * lax.erf(pre * math.sqrt(0.5))
    act = (pre * cdf).astype(BF)
    slope = cdf + pre * jnp.exp(-0.5 * pre * pre) * (1.0 / math.sqrt(2.0 * math.pi))
    branch = nn(act, w2_ref[...]) + line(b2_ref)
    output = resid + branch
    y_ref[...] = output.astype(BF)
    per = w_ref.shape[1] // BLK
    seq, at_ = i // per, i % per
    valid = w_ref[pl.ds(seq, 1), pl.ds(pl.multiple_of(at_ * BLK, BLK), BLK)].astype(F32)
    weight = column_of(valid)
    lane = lax.broadcasted_iota(jnp.int32, (1, LANES), 1)
    found = jnp.where(lane == 3, jnp.sum(valid, axis=1, keepdims=True), 0.0)
    for at, v in enumerate((attended, branch, output)):
        one = jnp.sum(weight * jnp.sum(v * v, axis=1, keepdims=True), axis=0, keepdims=True)
        found = jnp.where(lane == at, one, found)
    at_row = lax.broadcasted_iota(jnp.int32, sums.shape, 0) == seq
    sums[...] += jnp.where(at_row, found, 0.0)

    d_pre = (nt(cot, w2_ref[...]) * slope).astype(BF)
    part_ref[2] += tn(act[:, :own], cot)
    part_ref[1] += tn(d_pre[:, :own], normed)
    d_normed = nn(d_pre, w1_ref[...])
    d_hat = d_normed * line(g2_ref)
    grad = cot.astype(F32)
    d_resid = grad + inv * (
        d_hat - jnp.mean(d_hat, axis=1, keepdims=True) - hat * jnp.mean(d_hat * hat, axis=1, keepdims=True)
    )
    dr_ref[...] = d_resid
    low = d_resid.astype(BF)
    part_ref[0] += tn(mixed[:, :own], low)
    dm_ref[...] = nt(low, wo_ref[...]).astype(BF)
    for at, v in enumerate((grad, d_normed * hat, d_normed, low.astype(F32), d_pre.astype(F32))):
        vec[at] += fold8(v)

    @pl.when(i == pl.num_programs(0) - 1)
    def _():
        total = sums[...]
        counted = jnp.sum(jnp.where(lane == 3, total, 0.0), axis=1, keepdims=True)
        each = jnp.sqrt(total / (jnp.maximum(counted, 1.0) * attended.shape[1]))
        rms_ref[...] = each[: rms_ref.shape[0], : rms_ref.shape[1]]
        small_ref[...] = jnp.zeros_like(small_ref)
        for at, row in enumerate((0, 1, 2, 3, OWN_ROW)):
            small_ref[row : row + 1] = jnp.sum(vec[at], axis=0, keepdims=True)


def middle(own, mixed, x, cot, valid, wo, w1, w2, bo, g2, c2, b2, b1):
    tokens, width = x.shape
    inner, hidden = wo.shape[0], w1.shape[0]
    n = tokens // BLK
    return pl.pallas_call(
        functools.partial(middle_kernel, own),
        grid=(n,),
        in_specs=[rows(inner), rows(width), rows(width), whole(valid.shape)]
        + [whole((inner, width)), whole((hidden, width)), whole((hidden, width))]
        + [whole((width,))] * 4
        + [whole(b1.shape)],
        out_specs=[
            rows(width),
            rows(width),
            rows(inner),
            held((3, own, width)),
            held((8, width)),
            held((valid.shape[0], 3)),
        ],
        out_shape=[
            jax.ShapeDtypeStruct((tokens, width), BF),
            jax.ShapeDtypeStruct((tokens, width), F32),
            jax.ShapeDtypeStruct((tokens, inner), BF),
            jax.ShapeDtypeStruct((3, own, width), F32),
            jax.ShapeDtypeStruct((8, width), F32),
            jax.ShapeDtypeStruct((valid.shape[0], 3), F32),
        ],
        scratch_shapes=[pltpu.VMEM((5, 8, width), F32), pltpu.VMEM((-(-valid.shape[0] // 8) * 8, LANES), F32)],
        compiler_params=params(1),
        cost_estimate=pl.CostEstimate(
            flops=2 * tokens * width * (6 * width + 3 * own),
            bytes_accessed=14 * tokens * width + 6 * width * width,
            transcendentals=2 * tokens * hidden,
        ),
        name="middle",
    )(mixed, x, cot, valid, wo, w1, w2, bo, g2, c2, b2, b1)


def finish_kernel(
    bits, own, steps, dq_ref, dk_ref, dv_ref, x_ref, dr_ref, g_ref, wq_ref, wk_ref, wv_ref, mq_ref, mk_ref, mv_ref, n_ref, in_ref,
    dx_ref, gq_ref, gk_ref, gv_ref, small_ref, vec, part, acc, taken, weights, weight_sem, *refs,
):
    step = pl.program_id(0)
    grads = (mq_ref, mk_ref, mv_ref)
    count = len(grads)
    half = part.shape[2] // 2

    def publish(m, total):
        (gq_ref, gk_ref, gv_ref)[m][...] = total

    if bits is not None:
        place = Place(bits)
        work = Reduce(place, part, refs[:-3], FINISH_PLAN, publish)
        box, *sems = refs[-3:]

    loads = [
        pltpu.make_async_copy(src, weights.at[m], weight_sem.at[m]) for m, src in enumerate((wq_ref, wk_ref, wv_ref))
    ]

    @pl.when(step == 0)
    def _():
        for one in loads:
            one.start()
        vec[...] = jnp.zeros_like(vec)
        small_ref[...] = in_ref[...]
        if bits is not None:
            greet(place.plane())

    def take(m):
        taken[...] = grads[m][...]

    for m in range(count):
        pl.when(step == m)(functools.partial(take, m))

    @pl.when(step < count)
    def _():
        mine = taken[:, :own]
        part[step] = tn(mine, n_ref[...])
        total = jnp.sum(mine.astype(F32), axis=0, keepdims=True)
        for m in (0, 2):

            @pl.when(step == m)
            def _(at=m // 2 * half):
                small_ref[OWN_ROW + 1 : OWN_ROW + 2, at : at + own] = total

    def points(first, at, every):
        if bits is not None:
            for p in range(first, work.points, every):
                if work.plan[p]:
                    pl.when(step == at + (p - first) // every)(functools.partial(work.point, p))

    if bits is not None:
        for m in range(count):
            pl.when(step == m)(functools.partial(work.point, m))

    @pl.when(step == count)
    def _():
        for one in loads:
            one.wait()

    @pl.when(step >= count)
    def _():
        acc[...] = nn(dq_ref[...], weights[0])
        points(count, count, 3)
        acc[...] += nn(dk_ref[...], weights[1])
        points(count + 1, count, 3)
        d_normed = acc[...] + nn(dv_ref[...], weights[2])
        hat, inv = normalize(x_ref[...].astype(F32))
        d_hat = d_normed * line(g_ref)
        dx_ref[...] = dr_ref[...] + inv * (
            d_hat - jnp.mean(d_hat, axis=1, keepdims=True) - hat * jnp.mean(d_hat * hat, axis=1, keepdims=True)
        )
        vec[0] += fold8(d_normed * hat)
        vec[1] += fold8(d_normed)
        points(count + 2, count, 3)

    @pl.when(step == steps - 1)
    def _():
        for at in range(2):
            small_ref[4 + at : 5 + at] = jnp.sum(vec[at], axis=0, keepdims=True)
        if bits is None:
            for m in range(count):
                publish(m, part[m])
        else:
            copies = [send(small_ref, box.at[place.d], sems, i, peer) for i, peer in enumerate(place.plane())]
            for one in copies:
                one.start()
            box[place.d] = small_ref[...]
            for one in copies:
                one.wait_recv()
            for one in copies:
                one.wait_send()
            total = box[0]
            for i in range(1, 8):
                total = total + box[i]
            small_ref[...] = total
            work.end()


def finish(dq, dk, dv, x, d_resid, g1, wq, wk, wv, normed1, small, own, bits):
    tokens, width = x.shape
    inner = wq.shape[0]
    hosted = bits is not None
    count = 3
    pad = -(-own // LANES) * LANES
    mine = pl.BlockSpec((tokens, pad), lambda i: (0, 0), pipeline_mode=pl.Buffered(1))

    def late(size):
        return pl.BlockSpec((BLK, size), lambda i: (jnp.maximum(i - count, 0), 0))

    return pl.pallas_call(
        functools.partial(finish_kernel, bits, own, count + tokens // BLK),
        grid=(count + tokens // BLK,),
        in_specs=[late(inner)] * 3
        + [late(width), late(width), whole((width,))]
        + [pl.BlockSpec(memory_space=pl.ANY)] * 3
        + [mine] * 3
        + [whole((tokens, width)), whole((8, width))],
        out_specs=[late(width)] + [held((own, width))] * 3 + [held((8, width))],
        out_shape=[jax.ShapeDtypeStruct((tokens, width), F32)]
        + [jax.ShapeDtypeStruct((own, width), F32)] * 3
        + [jax.ShapeDtypeStruct((8, width), F32)],
        scratch_shapes=[
            pltpu.VMEM((2, 8, width), F32),
            pltpu.VMEM((count, own, width), F32),
            pltpu.VMEM((BLK, width), F32),
            pltpu.VMEM((tokens, pad), BF),
            pltpu.VMEM((3, inner, width), BF),
            pltpu.SemaphoreType.DMA((3,)),
        ]
        + (
            reduce_scratch(count, own, width)
            + [pltpu.VMEM((8, 8, width), F32), pltpu.SemaphoreType.DMA((7,)), pltpu.SemaphoreType.DMA((7,))]
            if hosted
            else []
        ),
        compiler_params=hosting(1, 4) if hosted else params(1),
        cost_estimate=pl.CostEstimate(
            flops=6 * tokens * width * inner, bytes_accessed=16 * tokens * width + 6 * width * inner, transcendentals=0
        ),
        name="finish",
    )(dq, dk, dv, x, d_resid, g1, wq, wk, wv, dq, dk, dv, normed1, small)


def shards(dp, tp, x, g1, c1, wq, bq, wk, wv, bv, wo, bo, g2, c2, w1, b1, w2, b2, seg, valid, cot):
    tokens, width = x.shape
    seqs, length = seg.shape
    own = wq.shape[1]
    bits = bits_of(dp) if dp == 8 else None

    normed1, q, k, v, mixed, lse, vectors, fq, fk, fv, fo, f1, f2 = front(
        x, g1, c1, seg, (bq, bv, b1), [wq.T, wk.T, wv.T, wo, w1.T, w2], dp, tp
    )

    y, d_resid, d_mixed, parts, small, rms = middle(
        own, mixed, x, cot, valid, fo, f1, f2, bo, g2, c2, b2, vectors
    )
    dq, dk, dv, gwo, gw1, gw2 = attend_back(q, k, v, seg, mixed, d_mixed, lse, parts, bits)
    grad_input, gq, gk, gv, small = finish(dq, dk, dv, x, d_resid, g1, fq, fk, fv, normed1, small, own, bits)
    if bits is None:
        gwo, gw1, gw2, gq, gk, gv, small = lax.psum((gwo, gw1, gw2, gq, gk, gv, small), "dp")

    gb2, gg2, gc2, gbo, gg1, gc1 = (small[r] for r in range(6))
    gb1 = small[OWN_ROW, :own]
    gbq = small[OWN_ROW + 1, :own]
    gbv = small[OWN_ROW + 1, width // 2 : width // 2 + own]
    return (y, grad_input, gg1, gc1, gq.T, gbq, gk.T, gv.T, gbv, gwo, gbo, gg2, gc2, gw1.T, gb1, gw2, gb2, rms)


def solution(mesh):
    dp, tp = mesh.shape["dp"], mesh.shape["tensor"]
    tok, col, row, vec, rep = P("dp", None), P(None, "tensor"), P("tensor", None), P("tensor"), P()
    return jax.shard_map(
        functools.partial(shards, dp, tp),
        mesh=mesh,
        in_specs=(tok, rep, rep, col, vec, col, col, vec, row, rep, rep, rep, col, vec, row, rep, tok, tok, tok),
        out_specs=(tok, tok, rep, rep, col, vec, col, col, vec, row, rep, rep, rep, col, vec, row, rep, tok),
        check_vma=False,
    )
```

```python
import functools
import math

import jax
import jax.numpy as jnp
from jax import lax
from jax.experimental import pallas as pl
from jax.experimental.pallas import tpu as pltpu
from jax.sharding import PartitionSpec as P

HEAD_DIM = 160
MAX_DOC = 512
EPS = 1e-05
NEG = -1e30
BLK = 256
WIN = 256
LANES = 128
SCALE = 1.0 / math.sqrt(HEAD_DIM)
LOG2E = 1.0 / math.log(2.0)
BF = jnp.bfloat16
F32 = jnp.float32
VMEM_MAX = 60 << 20


def nn(a, b):
    return lax.dot_general(a, b, (((1,), (0,)), ((), ())), preferred_element_type=F32)


def nt(a, b):
    return lax.dot_general(a, b, (((1,), (1,)), ((), ())), preferred_element_type=F32)


def tn(a, b):
    return lax.dot_general(a, b, (((0,), (0,)), ((), ())), preferred_element_type=F32)


def whole(shape):
    return pl.BlockSpec(shape, lambda *_: (0,) * len(shape), pipeline_mode=pl.Buffered(1))


def held(shape):
    return pl.BlockSpec(shape, lambda *_: (0,) * len(shape))


def rows(width):
    return pl.BlockSpec((BLK, width), lambda i: (i, 0))


def column_of(row):
    n = row.shape[1]
    eye = lax.broadcasted_iota(jnp.int32, (n, n), 0) == lax.broadcasted_iota(jnp.int32, (n, n), 1)
    return jnp.sum(jnp.where(eye, row, jnp.zeros_like(row)), axis=1, keepdims=True)


def line(ref):
    return ref[...].reshape(1, ref.shape[0])


def fold8(t):
    return jnp.sum(t.reshape(t.shape[0] // 8, 8, t.shape[1]), axis=0)


def params(grid, vmem=VMEM_MAX):
    return pltpu.CompilerParams(dimension_semantics=("arbitrary",) * grid, vmem_limit_bytes=vmem)


def hosting(grid, ident):
    return pltpu.CompilerParams(
        dimension_semantics=("arbitrary",) * grid,
        vmem_limit_bytes=VMEM_MAX,
        collective_id=ident,
        has_side_effects=True,
    )


def sibling(index, bit):
    return index + bit - 2 * bit * (index // bit % 2)


class Place:
    def __init__(self, bits):
        self.d, self.z = lax.axis_index("dp"), lax.axis_index("tensor")
        self.core = self.d % 2
        self.a, self.b = (self.d // bit % 2 for bit in bits)
        self.spot = self.a + 2 * self.b
        self.on_core = {"dp": sibling(self.d, 1), "tensor": self.z}
        self.on_a, self.on_b = ({"dp": sibling(self.d, bit), "tensor": self.z} for bit in bits)
        peers = (None, sibling(self.z, 1), sibling(self.z, 2), sibling(sibling(self.z, 1), 2))
        self.on_z = [None] + [{"dp": self.d, "tensor": peer} for peer in peers[1:]]

    def plane(self):
        return [{"dp": (self.d + step) % 8, "tensor": self.z} for step in range(1, 8)]


def greet(targets):
    barrier = pltpu.get_barrier_semaphore()
    for target in targets:
        pl.semaphore_signal(barrier, inc=1, device_id=target, device_id_type=pl.DeviceIdType.MESH)
    pl.semaphore_wait(barrier, len(targets))


def send(src, dst, sems, at, target):
    return pltpu.make_async_remote_copy(
        src_ref=src,
        dst_ref=dst,
        send_sem=sems[0].at[at],
        recv_sem=sems[1].at[at],
        device_id=target,
        device_id_type=pl.DeviceIdType.MESH,
    )


def bits_of(dp):
    return (2, 4) if dp == 8 else (2, 8)


def chunks_of(count, tp, piece):
    cut = (piece * 5 // 8) // 8 * 8
    orders = [[1 + (j + m % 2) % (tp - 1) for j in range(tp - 1)] for m in range(count)]
    return [(m, j, *span) for m in range(count) for span in ((0, cut), (cut, piece)) for j in orders[m]]


AHEAD = 6
LAG = 2
ATTEND_COST = 0.9


class Gather:
    def __init__(self, place, chunks, mine, land, sems, publish):
        self.place, self.chunks, self.mine, self.land, self.sems, self.publish = place, chunks, mine, land, sems, publish
        self.ticks = len(chunks) + 3 * LAG
        self.closing = {(m, j): k for k, (m, j, _, _) in enumerate(chunks)}

    def slot(self, k, where, low=None, high=None):
        m, j, r0, r1 = self.chunks[k]
        low, high = (r0 if low is None else low), (r1 if high is None else high)
        return self.land.at[m, j - 1, self.place.core, where, pl.ds(low, high - low)]

    def middle(self, k):
        _, _, r0, r1 = self.chunks[k]
        half = (r1 - r0) // 2
        return r0 + (half + 7 if k % 2 else half) // 8 * 8

    def over_z(self, k):
        m, j, r0, r1 = self.chunks[k]
        spots = [self.place.spot] + ([3 - self.place.spot] if j == 1 else [])
        return [
            send(self.mine.at[m, i, pl.ds(r0, r1 - r0)], self.slot(k, spot), self.sems, (k, i), self.place.on_z[j])
            for i, spot in enumerate(spots)
        ]

    def over_a(self, k):
        here = self.slot(k, self.place.spot)
        return send(here, here, self.sems, (k, 2), self.place.on_a)

    def over_b(self, k):
        here = self.slot(k, self.place.spot)
        return send(here, here, self.sems, (k, 3), self.place.on_b)

    def on_a(self, k):
        part = self.slot(k, sibling(self.place.spot, 2), None, self.middle(k))
        return send(part, part, self.sems, (k, 4), self.place.on_a)

    def on_b(self, k):
        part = self.slot(k, sibling(self.place.spot, 1), self.middle(k), None)
        return send(part, part, self.sems, (k, 5), self.place.on_b)

    def relays(self, k):
        return [] if self.chunks[k][1] == 1 else [self.on_a(k), self.on_b(k)]

    def swap(self, k):
        m, j, r0, r1 = self.chunks[k]
        part = self.land.at[m, j - 1, self.place.core, :, pl.ds(r0, r1 - r0)]
        return send(part, part, self.sems, (k, 6), self.place.on_core)

    def start_z(self, k):
        for one in self.over_z(k):
            one.start()

    def tick(self, t):
        total = len(self.chunks)
        if 0 <= t < total:
            for one in self.over_z(t):
                one.wait_recv()
            self.over_a(t).start()
            self.over_b(t).start()
            if t + AHEAD < total:
                self.start_z(t + AHEAD)
        k = t - LAG
        if 0 <= k < total:
            self.over_b(k).wait_recv()
            for one in self.relays(k)[:1]:
                one.start()
            self.over_a(k).wait_recv()
            for one in self.relays(k)[1:]:
                one.start()
        k = t - 2 * LAG
        if 0 <= k < total:
            for one in self.relays(k):
                one.wait_recv()
            self.swap(k).start()
        k = t - 3 * LAG
        if 0 <= k < total:
            self.swap(k).wait_recv()
            m, j, _, _ = self.chunks[k]
            if self.closing[m, j] == k:
                piece = self.land.shape[4]
                self.publish(m, j, self.land[m, j - 1].reshape(8 * piece, -1).astype(BF))

    def end(self):
        for k in range(len(self.chunks)):
            for one in self.over_z(k) + self.relays(k) + [self.over_a(k), self.over_b(k), self.swap(k)]:
                one.wait_send()


def gather_scratch(count, tp, piece, width):
    total = len(chunks_of(count, tp, piece))
    return [
        pltpu.VMEM((count, tp - 1, 2, 4, piece, width), F32),
        pltpu.SemaphoreType.DMA((total, 7)),
        pltpu.SemaphoreType.DMA((total, 7)),
        pltpu.VMEM((count, 2, piece, width), F32),
    ]


class Reduce:
    def __init__(self, place, part, scratch, plan, publish):
        self.place, self.part, self.publish = place, part, publish
        self.count, self.own, self.width = part.shape
        self.out, self.half, self.first, self.second, *self.sems = scratch
        self.points = 1 + max(row[-1] for row in plan)
        self.plan = {p: [] for p in range(self.points)}
        for k, row in enumerate(plan):
            for stage, p in enumerate(row):
                self.plan[p].append((k, stage))
        for p, found in self.plan.items():
            found.sort(key=lambda one: (one[1] if p == self.points - 1 else -one[1], one[0]))
        ends = [k for p in range(self.points) for k, stage in self.plan[p] if stage == 6]
        self.closing = [max(2 * m, 2 * m + 1, key=ends.index) for m in range(self.count)]

    def greet(self):
        return [self.place.on_a, self.place.on_b, self.place.on_core]

    def rows_of(self, size, index, count):
        return pl.ds(pl.multiple_of(size * index, 8), count)

    def way(self, k):
        p = self.place
        return (p.a, p.on_a, p.b, p.on_b) if k % 2 == 0 else (p.b, p.on_b, p.a, p.on_a)

    def columns(self, bit):
        lanes = self.width // 2
        return pl.ds(pl.multiple_of(lanes * bit, LANES), lanes)

    def out_rows(self, k, bit):
        piece = self.own // 8
        return self.rows_of(piece, 4 * self.place.core + 2 * (k % 2) + bit, piece)

    def quarter(self, k, core):
        size = self.own // 4
        return self.rows_of(size, 2 * core + k % 2, size)

    def copy(self, k, stage):
        place, m, piece = self.place, k // 2, self.own // 8
        bit, peer, bit2, peer2 = self.way(k)
        if stage == 0:
            src, dst, to = self.part.at[m, self.quarter(k, 1 - place.core)], self.half.at[k], place.on_core
        elif stage == 1:
            src, dst, to = self.half.at[k, self.rows_of(piece, 1 - bit, piece)], self.first.at[k], peer
        elif stage == 2:
            src, dst, to = self.half.at[k, self.rows_of(piece, bit, piece), self.columns(1 - bit2)], self.second.at[k], peer2
        elif stage == 3:
            src = dst = self.out.at[m, self.out_rows(k, bit), self.columns(bit2)]
            to = peer2
        elif stage == 4:
            src = dst = self.out.at[m, self.out_rows(k, bit)]
            to = peer
        else:
            src = dst = self.out.at[m, self.quarter(k, place.core)]
            to = place.on_core
        return send(src, dst, self.sems, (k, stage), to)

    def step(self, k, stage):
        m, piece = k // 2, self.own // 8
        bit, _, bit2, _ = self.way(k)
        mine = self.rows_of(piece, bit, piece)
        if stage >= 1:
            self.copy(k, stage - 1).wait_recv()
        if stage == 1:
            self.half[k] = self.part[m, self.quarter(k, self.place.core)] + self.half[k]
        if stage == 2:
            self.half[k, mine] = self.half[k, mine] + self.first[k]
        if stage == 3:
            columns = self.columns(bit2)
            self.out[m, self.out_rows(k, bit), columns] = self.half[k, mine, columns] + self.second[k]
        if stage < 6:
            self.copy(k, stage).start()
            return
        if k == self.closing[m]:
            self.publish(m, self.out[m])

    def point(self, p):
        for k, stage in self.plan[p]:
            self.step(k, stage)

    def end(self):
        for k in range(2 * self.count):
            for stage in range(6):
                self.copy(k, stage).wait_send()


def reduce_scratch(count, own, width):
    chunks = 2 * count
    return [
        pltpu.VMEM((count, own, width), F32),
        pltpu.VMEM((chunks, own // 4, width), F32),
        pltpu.VMEM((chunks, own // 8, width), F32),
        pltpu.VMEM((chunks, own // 8, width // 2), F32),
        pltpu.SemaphoreType.DMA((chunks, 6)),
        pltpu.SemaphoreType.DMA((chunks, 6)),
    ]


def normalize(v):
    center = v - jnp.mean(v, axis=-1, keepdims=True)
    inv = lax.rsqrt(jnp.mean(center * center, axis=-1, keepdims=True) + EPS)
    return center * inv, inv


HEADS_IN_GROUP = 4
GROUP = HEADS_IN_GROUP * HEAD_DIM


def window_of(head):
    low = head * HEAD_DIM
    start = low // LANES * LANES
    return start, low - start


def lane_mask(offset):
    lane = lax.broadcasted_iota(jnp.int32, (1, WIN), 1)
    return (lane >= offset) & (lane < offset + HEAD_DIM)


def spread(parts):
    tiles = [None] * (GROUP // LANES)
    for head, part in enumerate(parts):
        first = window_of(head)[0] // LANES
        for half in range(WIN // LANES):
            piece = part[:, half * LANES : (half + 1) * LANES]
            at = first + half
            tiles[at] = piece if tiles[at] is None else tiles[at] + piece
    return jnp.concatenate(tiles, axis=1)


def attend_block(seq, i, q_ref, k_ref, v_ref, seg_ref, o_ref, lse_ref, bias, between):
    groups = q_ref.shape[1] // GROUP
    back = MAX_DOC // BLK
    here = pl.ds(pl.multiple_of(i * BLK, BLK), BLK)
    row = pl.ds(seq, 1)
    seg_col = column_of(seg_ref[row, here])
    count = jnp.minimum(i, back) + 1
    kinds = range(1, back + 2)

    def first(blocks):
        return pl.multiple_of((i + 1 - blocks) * BLK, BLK)

    def mask_of(blocks):
        keys, start = blocks * BLK, first(blocks)
        query = i * BLK + lax.broadcasted_iota(jnp.int32, (BLK, keys), 0)
        key = start + lax.broadcasted_iota(jnp.int32, (BLK, keys), 1)
        allowed = (query >= key) & (seg_col == seg_ref[row, pl.ds(start, keys)])
        bias[:, :keys] = jnp.where(allowed, 0.0, NEG)

    def heads(gi, blocks):
        keys, start = blocks * BLK, first(blocks)
        parts = []
        lse = lse_ref[...]
        head_lane = lax.broadcasted_iota(jnp.int32, (1, LANES), 1)
        for h in range(HEADS_IN_GROUP):
            at, off = window_of(h)
            lanes = pl.ds(pl.multiple_of(gi * GROUP + at, LANES), WIN)
            mask = lane_mask(off)
            q = q_ref[here, lanes]
            q = jnp.where(mask, q, jnp.zeros_like(q))
            t = nt(q, k_ref[pl.ds(start, keys), lanes]) * (SCALE * LOG2E) + bias[:, :keys]
            top = jnp.max(t, axis=1, keepdims=True)
            p = jnp.exp2(t - top)
            total = jnp.sum(p, axis=1, keepdims=True)
            o = nn(p.astype(BF), v_ref[pl.ds(start, keys), lanes])
            parts.append(jnp.where(mask, o * (1.0 / total), 0.0))
            lse = jnp.where(head_lane == gi * HEADS_IN_GROUP + h, top + jnp.log2(total), lse)
        lse_ref[...] = lse
        o_ref[:, pl.ds(pl.multiple_of(gi * GROUP, LANES), GROUP)] = spread(parts).astype(BF)

    lse_ref[...] = jnp.zeros_like(lse_ref)
    for blocks in kinds:
        pl.when(count == blocks)(functools.partial(mask_of, blocks))

    def group(gi, carry):
        for blocks in kinds:
            pl.when(count == blocks)(functools.partial(heads, gi, blocks))
        between(gi)
        return carry

    lax.fori_loop(0, groups, group, 0)


def front_kernel(
    bits, n, seqs, steps, chunks, count, x_ref, g_ref, c_ref, seg_ref, bq_ref, bv_ref, bh_ref, *refs
):
    local, refs = refs[:count], refs[count:]
    n_ref, q_ref, k_ref, v_ref, o_ref, lse_ref, vec_ref, *refs = refs
    full, refs = refs[:count], refs[count:]
    bias, weights, stage, qs, ks, vs, ns, passing, fresh, land, gather_s, gather_r, mine, raw, bias_in, bias_s, bias_r, local_sem, out_sem, raw_sem, copy_sem, back_sem, bias_ref = refs
    own = local[0].shape[0]
    held_here = weights.shape[0]
    step = pl.program_id(0)
    place = Place(bits)
    shards_ = len(place.on_z)
    ahead = 2 * n + (seqs - 1) * n
    order = sorted({chunk[:2] for chunk in chunks if chunk[0] >= held_here}, key=lambda one: max(k for k, chunk in enumerate(chunks) if chunk[:2] == one))

    def rows_of(j):
        return pl.ds(j * own, own)

    def stage_copy(number):
        m, j = order[number]
        return pltpu.make_async_copy(stage.at[number % 2], full[m].at[rows_of(j)], out_sem.at[number])

    def publish(m, j, shard):
        if m < held_here:
            weights[m, rows_of(j)] = shard
            return
        number = order.index((m, j))
        if number >= 2:
            stage_copy(number - 2).wait()
        stage[number % 2] = shard
        stage_copy(number).start()

    work = Gather(place, chunks, mine, land, (gather_s, gather_r), publish)
    ready = [max(k for k, chunk in enumerate(chunks) if chunk[0] == m) + 3 * LAG + 1 for m in range(held_here)]

    def own_copies():
        held_ = [pltpu.make_async_copy(local[m], weights.at[m, rows_of(0)], local_sem.at[m]) for m in range(held_here)]
        rest = [
            pltpu.make_async_copy(local[m], full[m].at[rows_of(0)], local_sem.at[m]) for m in range(held_here, count)
        ]
        return held_, rest

    def held_out():
        return [pltpu.make_async_copy(weights.at[m], full[m], local_sem.at[m]) for m in range(held_here)]

    @pl.when(step == 0)
    def _():
        held_, rest = own_copies()
        piece = own // 8
        raws = [
            [
                pltpu.make_async_copy(
                    local[m].at[pl.ds(pl.multiple_of(piece * (4 * place.core + spot), 8), piece)],
                    raw.at[m % 2, i],
                    raw_sem.at[m % 2, i],
                )
                for i, spot in enumerate((place.spot, 3 - place.spot))
            ]
            for m in range(count)
        ]
        for one in sum(raws[:2], []) + held_ + rest:
            one.start()
        greet(place.on_z[1:] + [place.on_a, place.on_b, place.on_core])
        for m in range(count):
            for i, one in enumerate(raws[m]):
                one.wait()
                mine[m, i] = raw[m % 2, i].astype(F32)
            for one in raws[m + 2] if m + 2 < count else []:
                one.start()
            if m == 0:
                for k in range(AHEAD):
                    work.start_z(k)
        bias_ref[...] = jnp.zeros_like(bias_ref)
        for r, ref in enumerate((bq_ref, bv_ref, bh_ref)):
            row = line(ref)
            for j in range(shards_):
                pieces = [jnp.zeros((1, j * own), F32), row, jnp.zeros((1, (shards_ - 1 - j) * own), F32)]
                bias_ref[j, r : r + 1] = jnp.concatenate([t for t in pieces if t.shape[1]], axis=1)
        vectors = [
            send(bias_ref.at[j], bias_in.at[j], (bias_s, bias_r), j, place.on_z[j]) for j in range(1, shards_)
        ]
        for one in vectors:
            one.start()
        for t in range(ready[0]):
            work.tick(t)
        for one in vectors:
            one.wait()
        vec_ref[...] = sum((bias_in[j] for j in range(1, shards_)), bias_ref[0])
        for one in held_:
            one.wait()

    @pl.when(step == 1 + ahead)
    def _():
        for one in held_out():
            one.start()

    unit = jnp.maximum(step - 1 - ahead, 0)
    seq, part = unit // (2 * n), unit % (2 * n)
    early = jnp.maximum(step - 1 - 2 * n, 0)
    block = jnp.where(step <= 2 * n, (step - 1 + n) % n, jnp.where(step <= ahead, early % n, part % n))
    here = pl.ds(pl.multiple_of(block * BLK, BLK), BLK)

    def leave(i, src, dst, sequence):
        there = pl.ds(pl.multiple_of((sequence * n + block) * BLK, BLK), BLK)
        return pltpu.make_async_copy(src, dst.at[there], copy_sem.at[i, block])

    def enter(sequence):
        there = pl.ds(pl.multiple_of(sequence * n * BLK, BLK), n * BLK)
        return [
            pltpu.make_async_copy(src.at[there], dst, back_sem.at[i]) for i, (src, dst) in enumerate(((q_ref, qs), (k_ref, ks)))
        ]

    first = (step > 0) & (step <= n)
    second = (step > n) & (step <= 2 * n)
    passing_by = (step > 2 * n) & (step <= ahead)
    third = (step > ahead) & (part < n)
    again = third & (seq > 0)

    @pl.when(again)
    def _():
        @pl.when(part == 0)
        def _():
            for one in enter(seq):
                one.start()

        leave(2, ns.at[here], n_ref, seq - 1).wait()
        leave(3, vs.at[here], v_ref, seq - 1).wait()

    @pl.when(first | passing_by | again)
    def _():
        hat, _ = normalize(x_ref[...].astype(F32))
        fresh[...] = (hat * line(g_ref) + line(c_ref)).astype(BF)

    @pl.when(first | again)
    def _():
        ns[here] = fresh[...]

    @pl.when(second | (third & (seq == 0)))
    def _():
        fresh[...] = ns[here]

    @pl.when(first | second | passing_by | third)
    def _():
        low = jnp.where(third, 2, jnp.where(second, 1, 0))

        def make(m, carry):
            row = jnp.where(m == 0, 0, jnp.where(m == 1, 3, 1))
            passing[m % 2] = (nt(fresh[...], weights[m]) + vec_ref[pl.ds(row, 1)]).astype(BF)
            return carry

        lax.fori_loop(low, low + jnp.where(passing_by, 2, 1), make, 0)

    @pl.when(first)
    def _():
        qs[here] = passing[0]
        leave(0, qs.at[here], q_ref, 0).start()
        leave(2, ns.at[here], n_ref, 0).start()

    @pl.when(second)
    def _():
        ks[here] = passing[1]
        leave(1, ks.at[here], k_ref, 0).start()

    @pl.when(passing_by)
    def _():
        copies = [leave(3 + i, passing.at[i], dst, 1 + early // n) for i, dst in enumerate((q_ref, k_ref))]
        for one in copies:
            one.start()
        for one in copies:
            one.wait()

    @pl.when(third)
    def _():
        vs[here] = passing[0]
        leave(3, vs.at[here], v_ref, seq).start()

    @pl.when(again)
    def _():
        leave(2, ns.at[here], n_ref, seq).start()

        @pl.when(part == n - 1)
        def _():
            for one in enter(seq):
                one.wait()

    @pl.when((step > ahead) & (part == n) & (seq == 0))
    def _():
        for b in range(n):
            there = pl.ds(b * BLK, BLK)
            pltpu.make_async_copy(qs.at[there], q_ref.at[there], copy_sem.at[0, b]).wait()
            pltpu.make_async_copy(ks.at[there], k_ref.at[there], copy_sem.at[1, b]).wait()

    reach = MAX_DOC // BLK + 1
    groups = qs.shape[1] // GROUP
    spots = [(at, None, 1.0) for at in range(1, ahead + 1)]
    for number in range(seqs):
        at = 1 + ahead + 2 * n * number
        spots += [(at + i, None, 1.6 if number else 1.0) for i in range(n)]
        for i in range(n):
            each = min(i + 1, reach) * ATTEND_COST / groups
            spots += [(at + n + i, gi, each) for gi in range(groups)]
    starts = (1, 1 + n, 1 + ahead, steps)
    where = {}
    for t in range(ready[0], work.ticks):
        m = sum(t >= one for one in ready)
        begin, upto = ready[m - 1], (ready + [work.ticks])[m]
        span = [one for one in spots if starts[m - 1] <= one[0] < starts[m]]
        goal, passed, i = (t - begin + 1) / (upto - begin) * sum(one[2] for one in span), span[0][2], 0
        while passed < goal - 1e-6 and i < len(span) - 1:
            i += 1
            passed += span[i][2]
        where[t] = span[i][:2]

    def between(gi):
        for t, (at, spot) in where.items():
            if spot is not None:
                pl.when((step == at) & (gi == spot))(functools.partial(work.tick, t))

    for t, (at, spot) in where.items():
        if spot is None and at <= ahead + n:
            pl.when(step == at)(functools.partial(work.tick, t))

    @pl.when((step > ahead) & (part >= n))
    def _():
        attend_block(seq, part - n, qs, ks, vs, seg_ref, o_ref, lse_ref, bias, between)

    for t, (at, spot) in where.items():
        if spot is None and at > ahead + n:
            pl.when(step == at)(functools.partial(work.tick, t))

    @pl.when(step == steps - 1)
    def _():
        work.end()
        for number in range(max(0, len(order) - 2), len(order)):
            stage_copy(number).wait()
        for one in held_out() + own_copies()[1]:
            one.wait()
        for b in range(n):
            for i, (src, dst) in ((2, (ns, n_ref)), (3, (vs, v_ref))):
                there = pl.ds(((seqs - 1) * n + b) * BLK, BLK)
                pltpu.make_async_copy(src.at[pl.ds(b * BLK, BLK)], dst.at[there], copy_sem.at[i, b]).wait()


def front(x, g1, c1, seg, biases, shards_, dp, tp):
    tokens, width = x.shape
    seqs, length = seg.shape
    n = length // BLK
    count, own = len(shards_), shards_[0].shape[0]
    bits, piece, steps, out = bits_of(dp), own // 8, 1 + 2 * n + (seqs - 1) * n + 2 * seqs * n, tp * own
    chunks = chunks_of(count, tp, piece)

    ahead = 2 * n + (seqs - 1) * n

    def unit(i):
        return jnp.maximum(i - 1 - ahead, 0)

    def early(i):
        opening = jnp.minimum(jnp.maximum(i - 1, 0), n - 1)
        later = n + jnp.maximum(i - 1 - 2 * n, 0)
        again = unit(i) // (2 * n) * n + jnp.minimum(unit(i) % (2 * n), n - 1)
        return (jnp.where(i <= 2 * n, opening, jnp.where(i <= ahead, later, jnp.where(unit(i) < 2 * n, ahead - n - 1, again))), 0)

    def late(size):
        return pl.BlockSpec((BLK, size), lambda i: (unit(i) // (2 * n) * n + jnp.maximum(unit(i) % (2 * n) - n, 0), 0))

    anywhere = pl.BlockSpec(memory_space=pl.ANY)
    pairs = seqs * n * 2.5 * BLK * BLK * (out // HEAD_DIM)
    return pl.pallas_call(
        functools.partial(front_kernel, bits, n, seqs, steps, chunks, count),
        grid=(steps,),
        in_specs=[
            pl.BlockSpec((BLK, width), early),
            whole(g1.shape),
            whole(c1.shape),
            whole(seg.shape),
        ]
        + [whole((own,))] * 3
        + [anywhere] * count,
        out_specs=[anywhere] * 4 + [late(out), late(LANES), held((8, out))] + [anywhere] * count,
        out_shape=[jax.ShapeDtypeStruct((tokens, width), BF)]
        + [jax.ShapeDtypeStruct((tokens, out), BF)] * 4
        + [jax.ShapeDtypeStruct((tokens, LANES), F32), jax.ShapeDtypeStruct((8, out), F32)]
        + [jax.ShapeDtypeStruct((out, width), BF)] * count,
        scratch_shapes=[
            pltpu.VMEM((BLK, BLK + MAX_DOC), F32),
            pltpu.VMEM((3, out, width), BF),
            pltpu.VMEM((2, own, width), BF),
        ]
        + [pltpu.VMEM((length, out), BF)] * 3
        + [pltpu.VMEM((length, width), BF), pltpu.VMEM((2, BLK, out), BF), pltpu.VMEM((BLK, width), BF)]
        + gather_scratch(count, tp, piece, width)
        + [
            pltpu.VMEM((2, 2, piece, width), BF),
            pltpu.VMEM((tp, 8, out), F32),
            pltpu.SemaphoreType.DMA((tp,)),
            pltpu.SemaphoreType.DMA((tp,)),
            pltpu.SemaphoreType.DMA((count,)),
            pltpu.SemaphoreType.DMA((count * tp,)),
            pltpu.SemaphoreType.DMA((2, 2)),
            pltpu.SemaphoreType.DMA((5, n)),
            pltpu.SemaphoreType.DMA((2,)),
            pltpu.VMEM((tp, 8, out), F32),
        ],
        compiler_params=hosting(1, 0),
        cost_estimate=pl.CostEstimate(
            flops=int(6 * tokens * width * out + pairs * 8 * WIN),
            bytes_accessed=12 * tokens * width + 4 * count * out * width,
            transcendentals=int(pairs),
        ),
        name="front",
    )(x, g1, c1, seg, *biases, *shards_)


def attend_back_kernel(
    steps, bits, q_ref, do_ref, o_ref, lse_ref, k_ref, v_ref, seg_ref, part_ref, dq_ref, dk_ref, dv_ref, go_ref, g1_ref, g2_ref,
    bias, dq_acc, lse_t, delta_t, *reduce_refs,
):
    s, j = pl.program_id(0), pl.program_id(1)
    n = pl.num_programs(1)
    length, width = q_ref.shape
    groups = width // GROUP
    ahead = MAX_DOC // BLK

    step = s * n + j

    def publish(m, total):
        (go_ref, g1_ref, g2_ref)[m][...] = total

    if bits is not None:
        work = Reduce(Place(bits), part_ref, reduce_refs, BACK_PLAN, publish)

        @pl.when(step == 0)
        def _():
            greet(work.greet())
            work.point(0)

    @pl.when(j == 0)
    def _():
        dq_acc[...] = jnp.zeros_like(dq_acc)
        head = lax.broadcasted_iota(jnp.int32, (16, width), 0)
        lane = lax.broadcasted_iota(jnp.int32, (16, width), 1)
        pick = jnp.where((lane >= head * HEAD_DIM) & (lane < (head + 1) * HEAD_DIM), 1.0, 0.0).astype(BF)
        for b in range(length // BLK):
            at = slice(b * BLK, (b + 1) * BLK)
            lse_t[:, at] = lse_ref[at, :].T[:16, :]
            prod = do_ref[at, :].astype(F32) * o_ref[at, :].astype(F32)
            high = prod.astype(BF)
            rest = (prod - high.astype(F32)).astype(BF)
            delta_t[:, at] = nt(pick, high) + nt(pick, rest)

    count = jnp.minimum(n - j, ahead + 1)
    start = pl.multiple_of(j * BLK, BLK)
    seg_col = column_of(seg_ref[pl.ds(s, 1), pl.ds(start, BLK)])

    def mask_of(blocks):
        queries = blocks * BLK
        row = lax.broadcasted_iota(jnp.int32, (BLK, queries), 0)
        col = lax.broadcasted_iota(jnp.int32, (BLK, queries), 1)
        allowed = (row <= col) & (seg_col == seg_ref[pl.ds(s, 1), pl.ds(start, queries)])
        bias[:, :queries] = jnp.where(allowed, 0.0, NEG)

    def heads(gi, blocks):
        queries = blocks * BLK
        span = pl.ds(start, queries)
        dks, dvs = [], []
        for h in range(HEADS_IN_GROUP):
            at, off = window_of(h)
            lanes = pl.ds(pl.multiple_of(gi * GROUP + at, LANES), WIN)
            mask = lane_mask(off)
            head = pl.ds(gi * HEADS_IN_GROUP + h, 1)
            k = k_ref[:, lanes]
            k = jnp.where(mask, k, jnp.zeros_like(k))
            v = v_ref[:, lanes]
            v = jnp.where(mask, v, jnp.zeros_like(v))
            q = q_ref[span, lanes]
            do = do_ref[span, lanes]
            t = nt(k, q) * (SCALE * LOG2E) + bias[:, :queries]
            p = jnp.exp2(t - lse_t[head, span])
            dvs.append(jnp.where(mask, nn(p.astype(BF), do), 0.0))
            ds = (p * (nt(v, do) - delta_t[head, span])).astype(BF)
            dks.append(jnp.where(mask, nn(ds, q), 0.0))
            dq_acc[span, lanes] += tn(ds, k)
        out = pl.ds(pl.multiple_of(gi * GROUP, LANES), GROUP)
        dk_ref[:, out] = (spread(dks) * SCALE).astype(BF)
        dv_ref[:, out] = spread(dvs).astype(BF)

    kinds = range(1, ahead + 2)
    for blocks in kinds:
        pl.when(count == blocks)(functools.partial(mask_of, blocks))

    def group(gi, carry):
        for blocks in kinds:
            pl.when(count == blocks)(functools.partial(heads, gi, blocks))
        if bits is not None:
            for p in range(1, work.points):
                pl.when(step * groups + gi + 1 == p)(functools.partial(work.point, p))
        return carry

    lax.fori_loop(0, groups, group, 0)

    if bits is not None:
        pl.when(step == steps - 1)(work.end)
    else:
        for m in range(3):
            publish(m, part_ref[m])

    @pl.when(j == n - 1)
    def _():
        dq_ref[...] = (dq_acc[...] * SCALE).astype(BF)


def attend_back(q, k, v, seg, mixed, d_mixed, lse, parts, bits):
    tokens, width = q.shape
    seqs, length = seg.shape
    own, model = parts.shape[1:]
    n = length // BLK
    spec_k = pl.BlockSpec((BLK, width), lambda s, j: (s * n + j, 0))
    spec_q = pl.BlockSpec((length, width), lambda s, j: (s, 0))
    pairs = seqs * n * 2.5 * BLK * BLK * (width // HEAD_DIM)
    hosted = bits is not None
    return pl.pallas_call(
        functools.partial(attend_back_kernel, seqs * n, bits),
        grid=(seqs, n),
        in_specs=[
            spec_q,
            spec_q,
            spec_q,
            pl.BlockSpec((length, LANES), lambda s, j: (s, 0)),
            spec_k,
            spec_k,
            whole(seg.shape),
            whole(parts.shape),
        ],
        out_specs=[spec_q, spec_k, spec_k] + [held((own, model))] * 3,
        scratch_shapes=[
            pltpu.VMEM((BLK, BLK + MAX_DOC), F32),
            pltpu.VMEM((length, width), F32),
            pltpu.VMEM((16, length), F32),
            pltpu.VMEM((16, length), F32),
        ]
        + (reduce_scratch(*parts.shape) if hosted else []),
        out_shape=[jax.ShapeDtypeStruct((tokens, width), BF)] * 3 + [jax.ShapeDtypeStruct((own, model), F32)] * 3,
        compiler_params=hosting(2, 3) if hosted else params(2),
        cost_estimate=pl.CostEstimate(
            flops=int(pairs * 20 * WIN), bytes_accessed=16 * tokens * width, transcendentals=int(pairs)
        ),
        name="attend_back",
    )(q, d_mixed, mixed, lse, k, v, seg, parts)


BACK_PLAN = (
    (0, 1, 4, 7, 9, 11, 14),
    (0, 2, 4, 6, 10, 13, 14),
    (1, 2, 5, 8, 10, 13, 14),
    (0, 1, 3, 8, 11, 14, 16),
    (0, 5, 9, 10, 13, 15, 16),
    (0, 3, 6, 11, 13, 15, 16),
)
FINISH_PLAN = (
    (0, 1, 6, 10, 13, 19, 26),
    (0, 1, 5, 9, 13, 18, 21),
    (5, 6, 12, 16, 19, 24, 26),
    (1, 3, 10, 17, 21, 25, 26),
    (2, 3, 9, 17, 20, 25, 26),
    (4, 5, 12, 16, 19, 23, 25),
)

OWN_ROW = 6


def middle_kernel(
    own, m_ref, x_ref, g_ref, w_ref, wo_ref, w1_ref, w2_ref, bo_ref, g2_ref, c2_ref, b2_ref, b1_ref,
    y_ref, dr_ref, dm_ref, part_ref, small_ref, rms_ref, vec, sums,
):
    i = pl.program_id(0)

    @pl.when(i == 0)
    def _():
        part_ref[...] = jnp.zeros_like(part_ref)
        vec[...] = jnp.zeros_like(vec)
        sums[...] = jnp.zeros_like(sums)

    mixed = m_ref[...]
    cot = g_ref[...]
    attended = nn(mixed, wo_ref[...]) + line(bo_ref)
    resid = x_ref[...].astype(F32) + attended
    hat, inv = normalize(resid)
    normed = (hat * line(g2_ref) + line(c2_ref)).astype(BF)
    pre = nt(normed, w1_ref[...]) + b1_ref[2:3]
    cdf = 0.5 + 0.5 * lax.erf(pre * math.sqrt(0.5))
    act = (pre * cdf).astype(BF)
    slope = cdf + pre * jnp.exp(-0.5 * pre * pre) * (1.0 / math.sqrt(2.0 * math.pi))
    branch = nn(act, w2_ref[...]) + line(b2_ref)
    output = resid + branch
    y_ref[...] = output.astype(BF)
    per = w_ref.shape[1] // BLK
    seq, at_ = i // per, i % per
    valid = w_ref[pl.ds(seq, 1), pl.ds(pl.multiple_of(at_ * BLK, BLK), BLK)].astype(F32)
    weight = column_of(valid)
    lane = lax.broadcasted_iota(jnp.int32, (1, LANES), 1)
    found = jnp.where(lane == 3, jnp.sum(valid, axis=1, keepdims=True), 0.0)
    for at, v in enumerate((attended, branch, output)):
        one = jnp.sum(weight * jnp.sum(v * v, axis=1, keepdims=True), axis=0, keepdims=True)
        found = jnp.where(lane == at, one, found)
    at_row = lax.broadcasted_iota(jnp.int32, sums.shape, 0) == seq
    sums[...] += jnp.where(at_row, found, 0.0)

    d_pre = (nt(cot, w2_ref[...]) * slope).astype(BF)
    part_ref[2] += tn(act[:, :own], cot)
    part_ref[1] += tn(d_pre[:, :own], normed)
    d_normed = nn(d_pre, w1_ref[...])
    d_hat = d_normed * line(g2_ref)
    grad = cot.astype(F32)
    d_resid = grad + inv * (
        d_hat - jnp.mean(d_hat, axis=1, keepdims=True) - hat * jnp.mean(d_hat * hat, axis=1, keepdims=True)
    )
    dr_ref[...] = d_resid
    low = d_resid.astype(BF)
    part_ref[0] += tn(mixed[:, :own], low)
    dm_ref[...] = nt(low, wo_ref[...]).astype(BF)
    for at, v in enumerate((grad, d_normed * hat, d_normed, low.astype(F32), d_pre.astype(F32))):
        vec[at] += fold8(v)

    @pl.when(i == pl.num_programs(0) - 1)
    def _():
        total = sums[...]
        counted = jnp.sum(jnp.where(lane == 3, total, 0.0), axis=1, keepdims=True)
        each = jnp.sqrt(total / (jnp.maximum(counted, 1.0) * attended.shape[1]))
        rms_ref[...] = each[: rms_ref.shape[0], : rms_ref.shape[1]]
        small_ref[...] = jnp.zeros_like(small_ref)
        for at, row in enumerate((0, 1, 2, 3, OWN_ROW)):
            small_ref[row : row + 1] = jnp.sum(vec[at], axis=0, keepdims=True)


def middle(own, mixed, x, cot, valid, wo, w1, w2, bo, g2, c2, b2, b1):
    tokens, width = x.shape
    inner, hidden = wo.shape[0], w1.shape[0]
    n = tokens // BLK
    return pl.pallas_call(
        functools.partial(middle_kernel, own),
        grid=(n,),
        in_specs=[rows(inner), rows(width), rows(width), whole(valid.shape)]
        + [whole((inner, width)), whole((hidden, width)), whole((hidden, width))]
        + [whole((width,))] * 4
        + [whole(b1.shape)],
        out_specs=[
            rows(width),
            rows(width),
            rows(inner),
            held((3, own, width)),
            held((8, width)),
            held((valid.shape[0], 3)),
        ],
        out_shape=[
            jax.ShapeDtypeStruct((tokens, width), BF),
            jax.ShapeDtypeStruct((tokens, width), F32),
            jax.ShapeDtypeStruct((tokens, inner), BF),
            jax.ShapeDtypeStruct((3, own, width), F32),
            jax.ShapeDtypeStruct((8, width), F32),
            jax.ShapeDtypeStruct((valid.shape[0], 3), F32),
        ],
        scratch_shapes=[pltpu.VMEM((5, 8, width), F32), pltpu.VMEM((-(-valid.shape[0] // 8) * 8, LANES), F32)],
        compiler_params=params(1),
        cost_estimate=pl.CostEstimate(
            flops=2 * tokens * width * (6 * width + 3 * own),
            bytes_accessed=14 * tokens * width + 6 * width * width,
            transcendentals=2 * tokens * hidden,
        ),
        name="middle",
    )(mixed, x, cot, valid, wo, w1, w2, bo, g2, c2, b2, b1)


def finish_kernel(
    bits, own, steps, dq_ref, dk_ref, dv_ref, x_ref, dr_ref, g_ref, wq_ref, wk_ref, wv_ref, mq_ref, mk_ref, mv_ref, n_ref, in_ref,
    dx_ref, gq_ref, gk_ref, gv_ref, small_ref, vec, part, acc, taken, taken_sem, weights, weight_sem, *refs,
):
    step = pl.program_id(0)
    grads = (mq_ref, mk_ref, mv_ref)
    count = len(grads)
    half = part.shape[2] // 2

    def publish(m, total):
        (gq_ref, gk_ref, gv_ref)[m][...] = total

    if bits is not None:
        place = Place(bits)
        work = Reduce(place, part, refs[:-3], FINISH_PLAN, publish)
        box, *sems = refs[-3:]

    loads = [
        pltpu.make_async_copy(src, weights.at[m], weight_sem.at[m]) for m, src in enumerate((wq_ref, wk_ref, wv_ref))
    ]

    @pl.when(step == 0)
    def _():
        vec[...] = jnp.zeros_like(vec)
        small_ref[...] = in_ref[...]
        if bits is not None:
            greet(place.plane())

    def exchange():
        return [send(small_ref, box.at[place.d], sems, i, peer) for i, peer in enumerate(place.plane())]

    strips = [
        pltpu.make_async_copy(src.at[:, pl.ds(0, taken.shape[2])], taken.at[m], taken_sem.at[m])
        for m, src in enumerate(grads)
    ]

    @pl.when(step == 0)
    def _():
        for one in strips + loads:
            one.start()

    for m in range(count):
        pl.when(step == m)(strips[m].wait)

    @pl.when(step < count)
    def _():
        mine = taken[step][:, :own]
        part[step] = tn(mine, n_ref[...])
        total = jnp.sum(mine.astype(F32), axis=0, keepdims=True)
        for m in (0, 2):

            @pl.when(step == m)
            def _(at=m // 2 * half):
                small_ref[OWN_ROW + 1 : OWN_ROW + 2, at : at + own] = total

    def points(first, at, every):
        if bits is not None:
            for p in range(first, work.points, every):
                if work.plan[p]:
                    pl.when(step == at + (p - first) // every)(functools.partial(work.point, p))

    if bits is not None:
        for m in range(count):
            pl.when(step == m)(functools.partial(work.point, m))

    @pl.when(step == count)
    def _():
        for one in loads:
            one.wait()

    @pl.when(step >= count)
    def _():
        acc[...] = nn(dq_ref[...], weights[0])
        points(count, count, 3)
        acc[...] += nn(dk_ref[...], weights[1])
        points(count + 1, count, 3)
        d_normed = acc[...] + nn(dv_ref[...], weights[2])
        hat, inv = normalize(x_ref[...].astype(F32))
        d_hat = d_normed * line(g_ref)
        dx_ref[...] = dr_ref[...] + inv * (
            d_hat - jnp.mean(d_hat, axis=1, keepdims=True) - hat * jnp.mean(d_hat * hat, axis=1, keepdims=True)
        )
        vec[0] += fold8(d_normed * hat)
        vec[1] += fold8(d_normed)

        @pl.when(step == steps - 1)
        def _():
            for at in range(2):
                small_ref[4 + at : 5 + at] = jnp.sum(vec[at], axis=0, keepdims=True)
            if bits is not None:
                box[place.d] = small_ref[...]
                for one in exchange():
                    one.start()

        points(count + 2, count, 3)

    @pl.when(step == steps - 1)
    def _():
        if bits is None:
            for m in range(count):
                publish(m, part[m])
        else:
            for one in exchange():
                one.wait_recv()
            for one in exchange():
                one.wait_send()
            total = box[0]
            for i in range(1, 8):
                total = total + box[i]
            small_ref[...] = total
            work.end()


def finish(dq, dk, dv, x, d_resid, g1, wq, wk, wv, normed1, small, own, bits):
    tokens, width = x.shape
    inner = wq.shape[0]
    hosted = bits is not None
    count = 3
    pad = -(-own // LANES) * LANES

    def late(size):
        return pl.BlockSpec((BLK, size), lambda i: (jnp.maximum(i - count, 0), 0))

    return pl.pallas_call(
        functools.partial(finish_kernel, bits, own, count + tokens // BLK),
        grid=(count + tokens // BLK,),
        in_specs=[late(inner)] * 3
        + [late(width), late(width), whole((width,))]
        + [pl.BlockSpec(memory_space=pl.ANY)] * 3
        + [pl.BlockSpec(memory_space=pl.ANY)] * 3
        + [whole((tokens, width)), whole((8, width))],
        out_specs=[late(width)] + [held((own, width))] * 3 + [held((8, width))],
        out_shape=[jax.ShapeDtypeStruct((tokens, width), F32)]
        + [jax.ShapeDtypeStruct((own, width), F32)] * 3
        + [jax.ShapeDtypeStruct((8, width), F32)],
        scratch_shapes=[
            pltpu.VMEM((2, 8, width), F32),
            pltpu.VMEM((count, own, width), F32),
            pltpu.VMEM((BLK, width), F32),
            pltpu.VMEM((count, tokens, pad), BF),
            pltpu.SemaphoreType.DMA((count,)),
            pltpu.VMEM((3, inner, width), BF),
            pltpu.SemaphoreType.DMA((3,)),
        ]
        + (
            reduce_scratch(count, own, width)
            + [pltpu.VMEM((8, 8, width), F32), pltpu.SemaphoreType.DMA((7,)), pltpu.SemaphoreType.DMA((7,))]
            if hosted
            else []
        ),
        compiler_params=hosting(1, 4) if hosted else params(1),
        cost_estimate=pl.CostEstimate(
            flops=6 * tokens * width * inner, bytes_accessed=16 * tokens * width + 6 * width * inner, transcendentals=0
        ),
        name="finish",
    )(dq, dk, dv, x, d_resid, g1, wq, wk, wv, dq, dk, dv, normed1, small)


def shards(dp, tp, x, g1, c1, wq, bq, wk, wv, bv, wo, bo, g2, c2, w1, b1, w2, b2, seg, valid, cot):
    tokens, width = x.shape
    seqs, length = seg.shape
    own = wq.shape[1]
    bits = bits_of(dp) if dp == 8 else None

    normed1, q, k, v, mixed, lse, vectors, fq, fk, fv, fo, f1, f2 = front(
        x, g1, c1, seg, (bq, bv, b1), [wq.T, wk.T, wv.T, wo, w1.T, w2], dp, tp
    )

    y, d_resid, d_mixed, parts, small, rms = middle(
        own, mixed, x, cot, valid, fo, f1, f2, bo, g2, c2, b2, vectors
    )
    dq, dk, dv, gwo, gw1, gw2 = attend_back(q, k, v, seg, mixed, d_mixed, lse, parts, bits)
    grad_input, gq, gk, gv, small = finish(dq, dk, dv, x, d_resid, g1, fq, fk, fv, normed1, small, own, bits)
    if bits is None:
        gwo, gw1, gw2, gq, gk, gv, small = lax.psum((gwo, gw1, gw2, gq, gk, gv, small), "dp")

    gb2, gg2, gc2, gbo, gg1, gc1 = (small[r] for r in range(6))
    gb1 = small[OWN_ROW, :own]
    gbq = small[OWN_ROW + 1, :own]
    gbv = small[OWN_ROW + 1, width // 2 : width // 2 + own]
    return (y, grad_input, gg1, gc1, gq.T, gbq, gk.T, gv.T, gbv, gwo, gbo, gg2, gc2, gw1.T, gb1, gw2, gb2, rms)


def solution(mesh):
    dp, tp = mesh.shape["dp"], mesh.shape["tensor"]
    tok, col, row, vec, rep = P("dp", None), P(None, "tensor"), P("tensor", None), P("tensor"), P()
    return jax.shard_map(
        functools.partial(shards, dp, tp),
        mesh=mesh,
        in_specs=(tok, rep, rep, col, vec, col, col, vec, row, rep, rep, rep, col, vec, row, rep, tok, tok, tok),
        out_specs=(tok, tok, rep, rep, col, vec, col, col, vec, row, rep, rep, rep, col, vec, row, rep, tok),
        check_vma=False,
    )
```
